128 devices in a mesh: teacher: 4 (over y), dp: 32 (over x, z, core).
Axes of the slice: x: 4, y: 4, z: 4, core: 2. Of those that a mesh axis runs over, the one named last changes fastest.
Arguments:
- hid_whisper: bfloat16 [16384, 1280], P(('teacher', 'dp')), may hold values from -6 to 6
- hid_beats: bfloat16 [16384, 768], P(('teacher', 'dp')), may hold values from -6 to 6
- hid_wavlm: bfloat16 [16384, 1024], P(('teacher', 'dp')), may hold values from -6 to 6
- up_whisper: bfloat16 [1280, 5120], P(None, 'teacher'), may hold values from -0.15625 to 0.15625
- down_whisper: bfloat16 [5120, 1280], P('teacher'), may hold values from -0.078125 to 0.078125
- up_beats: bfloat16 [768, 3072], P(None, 'teacher'), may hold values from -0.21875 to 0.21875
- down_beats: bfloat16 [3072, 768], P('teacher'), may hold values from -0.109375 to 0.109375
- up_wavlm: bfloat16 [1024, 4096], P(None, 'teacher'), may hold values from -0.1875 to 0.1875
- down_wavlm: bfloat16 [4096, 1024], P('teacher'), may hold values from -0.09375 to 0.09375
- clip_len: int32 [128], P(('teacher', 'dp')), may hold values from 16 to 128
- send_counts: int32 [4, 32, 32], P('teacher'), may hold values from 0 to 8, as said below
- student_in: bfloat16 [16384, 512], P(('teacher', 'dp')), may hold values from -24 to 24
- w_in: bfloat16 [512, 1536], P('dp'), may hold values from -0.25 to 0.25
- w_out: bfloat16 [1536, 512], P('dp'), may hold values from -0.15625 to 0.15625
- w_head: bfloat16 [512, 3072], P('dp'), may hold values from -0.25 to 0.25
Outputs:
- grad_in: float32 [512, 1536], P('dp')
- grad_out: float32 [1536, 512], P('dp')
- grad_head: float32 [512, 3072], P('dp')
The draws below stay inside these ranges and needn't reach their ends.
Inputs may be any that keep to these rules, and one draw needn't show every extreme that they name: In every group t, each source s hands 128 frames in all (the sum over o of send_counts[t,s,o]), each owner o receives 128 frames in all, and in every group some source hands exactly 8 frames to some owner.
All inputs are finite; a program needn't handle non-finite values.
Results may differ from the reference program's by a relative error of at most 0.0031.
Values may be sent and summed in bfloat16 or wider, within the bound.
A program may use at most 128 MiB of HBM per device.

```python
import jax
import jax.numpy as jnp
from jax import lax

WH = 1280
HW = 5120
WB = 768
HB = 3072
WL = 1024
HL = 4096
SD = 512
SFF = 1536
FR_DEV = 128
CLIP = 128
CLIPS_DEV = 1
WALL = 3072
FRAMES = 16384
N_TEACHER = 4
N_DP = 32


def draw_send_counts(key, part):
    base = FR_DEV // N_DP
    marked = N_DP // 4

    def one_group(group):
        group_key = jax.random.fold_in(key, group)
        pattern = jnp.concatenate([jnp.full((marked,), base, jnp.int32), jnp.full((marked,), -base, jnp.int32), jnp.zeros((N_DP - 2 * marked,), jnp.int32)])
        pattern = jax.random.permutation(jax.random.fold_in(group_key, 1), pattern)
        owners = jax.random.permutation(jax.random.fold_in(group_key, 2), N_DP).astype(jnp.int32)
        sources = jnp.arange(N_DP, dtype=jnp.int32)
        shifted = (owners[None, :] - sources[:, None]) % N_DP
        return base + pattern[shifted]
    return jax.vmap(one_group)(jnp.arange(N_TEACHER, dtype=jnp.int32))


def touch_ends(values, rng, smallest, largest):
    place = [jax.random.randint(jax.random.fold_in(rng, axis), (), 0, length) for axis, length in enumerate(values.shape)]
    widest = values.shape.index(max(values.shape))
    next_to = place[:widest] + [(place[widest] + 1) % values.shape[widest]] + place[widest + 1:]
    return values.at[tuple(place)].set(smallest).at[tuple(next_to)].set(largest)


def raised(entries, stream_key, source, target, shards_of, factor):
    def block_of(axis_at):
        return (jnp.arange(entries.shape[axis_at]) // (entries.shape[axis_at] // shards_of)).reshape((-1,) + (1,) * (entries.ndim - 1 - axis_at))

    near = jax.random.permutation(stream_key, shards_of)[block_of(target)]
    second = (block_of(target) + shards_of // 2) % shards_of
    return jnp.where((block_of(source) == near) | (block_of(source) == second), factor * entries, entries)


def levels(key, shape, cuts, low, high):
    factor_of, own = 1.0, jax.random.fold_in(key, 6)
    for axis_at, blocks in cuts:
        heights = jnp.exp(jax.random.uniform(jax.random.fold_in(own, axis_at), (blocks,), jnp.float32, low / len(cuts), high / len(cuts)))
        factor_of = factor_of * jnp.repeat(heights, shape[axis_at] // blocks).reshape([-1 if axis == axis_at else 1 for axis in range(len(shape))])
    return factor_of


def bell_draw(rng, extent, width, most, cuts=(), kind=jnp.bfloat16):
    factor_of = levels(rng, extent, cuts, -0.22, 0.18) if cuts else 1.0
    array = jax.random.normal(rng, extent, jnp.float32) * width * factor_of
    return jnp.minimum(jnp.maximum(array, -most), most).astype(kind)


def gaussian_with(own_key, extent, scale, reach, cuts, heavy, kind=jnp.bfloat16):
    result = scale * jax.random.normal(own_key, extent, jnp.float32)
    if cuts:
        result = result * levels(own_key, extent, cuts, -0.22, 0.18)
    return jnp.clip(raised(result, jax.random.fold_in(own_key, 3), *heavy), -reach, reach).astype(kind)


def setup_inputs(seed: int = 0) -> dict:
    keys = jax.random.split(jax.random.key(seed), 16)
    hid_whisper = bell_draw(keys[0], (FRAMES, WH), 1.0, 6.0, ((0, 128),))
    hid_beats = bell_draw(keys[1], (FRAMES, WB), 1.0, 6.0, ((0, 128),))
    hid_wavlm = bell_draw(keys[2], (FRAMES, WL), 1.0, 6.0, ((0, 128),))
    up_whisper = bell_draw(keys[3], (WH, HW), WH ** -0.5, 0.15625, ((1, 4),))
    down_whisper = bell_draw(keys[4], (HW, WH), HW ** -0.5, 0.078125, ((0, 4),))
    up_beats = bell_draw(keys[5], (WB, HB), WB ** -0.5, 0.21875, ((1, 4),))
    down_beats = bell_draw(keys[6], (HB, WB), HB ** -0.5, 0.109375, ((0, 4),))
    up_wavlm = bell_draw(keys[7], (WL, HL), WL ** -0.5, 0.1875, ((1, 4),))
    down_wavlm = bell_draw(keys[8], (HL, WL), HL ** -0.5, 0.09375, ((0, 4),))
    clip_len = touch_ends(jax.random.randint(keys[9], (N_TEACHER * N_DP * CLIPS_DEV,), CLIP // 8, CLIP + 1), jax.random.fold_in(keys[9], 1), CLIP // 8, CLIP).astype(jnp.int32)
    send_counts = draw_send_counts(jax.random.fold_in(keys[15], 71), 0)
    student_in = gaussian_with(keys[11], (FRAMES, SD), 1.0, 24.0, ((0, 128),), (0, 1, 128, 5.5))
    w_in = bell_draw(keys[12], (SD, SFF), SD ** -0.5, 0.25, ((0, 32),))
    w_out = bell_draw(keys[13], (SFF, SD), SFF ** -0.5, 0.15625, ((0, 32),))
    w_head = bell_draw(keys[14], (SD, WALL), SD ** -0.5, 0.25, ((0, 32),))
    return dict(hid_whisper=hid_whisper, hid_beats=hid_beats, hid_wavlm=hid_wavlm, up_whisper=up_whisper, down_whisper=down_whisper, up_beats=up_beats, down_beats=down_beats, up_wavlm=up_wavlm, down_wavlm=down_wavlm, clip_len=clip_len, send_counts=send_counts, student_in=student_in, w_in=w_in, w_out=w_out, w_head=w_head)


EPS = 1e-05

def layer_norm(values):
    wide = values.astype(jnp.float32)
    center = wide - lax.optimization_barrier(jnp.mean(wide, axis=-1, keepdims=True))
    spread = lax.optimization_barrier(jnp.mean(center * center, axis=-1, keepdims=True))
    return center * lax.rsqrt(spread + EPS)

def swoosh_low(pre_act):
    return jax.nn.softplus(pre_act - 4.0) - 0.08 * pre_act - 0.035

def swoosh_slope(pre_act):
    return jax.nn.sigmoid(pre_act - 4.0) - 0.08

def column_scale():
    return jnp.concatenate([jnp.full((WH,), 2.0 / WH, jnp.float32), jnp.full((WB,), 2.0 / WB, jnp.float32), jnp.full((WL,), 2.0 / WL, jnp.float32)])

def reference(hid_whisper, hid_beats, hid_wavlm, up_whisper, down_whisper, up_beats, down_beats, up_wavlm, down_wavlm, clip_len, send_counts, student_in, w_in, w_out, w_head):
    blocks = N_TEACHER * N_DP
    pairs = ((up_whisper, down_whisper), (up_beats, down_beats), (up_wavlm, down_wavlm))

    def teacher_block(inputs):
        pieces = []
        for hidden_in, (up_proj, down_proj) in zip(inputs, pairs):
            normed = layer_norm(hidden_in).astype(jnp.bfloat16)
            quarter = up_proj.shape[1] // N_TEACHER
            total = jnp.zeros(hidden_in.shape, jnp.float32)
            for group in range(N_TEACHER):
                hidden = jax.nn.gelu(jnp.dot(normed, up_proj[:, group * quarter:(group + 1) * quarter], preferred_element_type=jnp.float32), approximate=False).astype(jnp.bfloat16)
                partial_sum = jnp.dot(hidden, down_proj[group * quarter:(group + 1) * quarter, :], preferred_element_type=jnp.float32)
                total = total + partial_sum
            pieces.append(total + hidden_in.astype(jnp.float32))
        return jnp.concatenate(pieces, axis=1).astype(jnp.bfloat16)
    inputs = (hid_whisper.reshape(blocks, FR_DEV, WH), hid_beats.reshape(blocks, FR_DEV, WB), hid_wavlm.reshape(blocks, FR_DEV, WL))
    targets = lax.map(teacher_block, inputs).reshape(blocks * FR_DEV, WH + WB + WL)
    frame_ids = jnp.arange(blocks * FR_DEV, dtype=jnp.int32)
    valid = (frame_ids % CLIP < clip_len[frame_ids // CLIP]).astype(jnp.int32)
    row_start = jnp.cumsum(send_counts, axis=2, dtype=jnp.int32) - send_counts
    col_end = jnp.cumsum(send_counts, axis=1, dtype=jnp.int32)
    col_start = col_end - send_counts
    end_to = jnp.transpose(col_end, (0, 2, 1))
    start_to = jnp.transpose(col_start, (0, 2, 1))
    offset_at = jnp.transpose(row_start, (0, 2, 1))
    positions = jnp.arange(FR_DEV, dtype=jnp.int32)
    source_of = lax.optimization_barrier(jnp.sum((end_to[:, :, None, :] <= positions[None, None, :, None]).astype(jnp.int32), axis=3, dtype=jnp.int32))
    select = jnp.arange(N_DP, dtype=jnp.int32)[None, None, None, :] == source_of[..., None]
    within = positions[None, None, :] - lax.optimization_barrier(jnp.sum(jnp.where(select, start_to[:, :, None, :], 0), axis=3, dtype=jnp.int32))
    offset = lax.optimization_barrier(jnp.sum(jnp.where(select, offset_at[:, :, None, :], 0), axis=3, dtype=jnp.int32))
    group_ids = jnp.arange(N_TEACHER, dtype=jnp.int32)[:, None, None]
    source_row = ((group_ids * N_DP + source_of) * FR_DEV + offset + within).reshape(-1).astype(jnp.int32)
    owner_target = targets[source_row]
    owner_mask = valid[source_row].astype(jnp.float32)
    pre_act = jnp.dot(student_in, w_in, preferred_element_type=jnp.float32)
    activated = swoosh_low(pre_act).astype(jnp.bfloat16)
    features = (student_in.astype(jnp.float32) + jnp.dot(activated, w_out, preferred_element_type=jnp.float32)).astype(jnp.bfloat16)
    predicted = jnp.dot(features, w_head, preferred_element_type=jnp.float32)
    err_grad = ((predicted - owner_target.astype(jnp.float32)) * column_scale()[None, :] * owner_mask[:, None]).astype(jnp.bfloat16)
    grad_head = jnp.dot(features.T, err_grad, preferred_element_type=jnp.float32)
    feat_grad = jnp.dot(err_grad, w_head.T, preferred_element_type=jnp.float32).astype(jnp.bfloat16)
    grad_out = jnp.dot(activated.T, feat_grad, preferred_element_type=jnp.float32)
    act_grad = jnp.dot(feat_grad, w_out.T, preferred_element_type=jnp.float32)
    pre_grad = (act_grad * swoosh_slope(pre_act)).astype(jnp.bfloat16)
    grad_in = jnp.dot(student_in.T, pre_grad, preferred_element_type=jnp.float32)
    return (grad_in, grad_out, grad_head)
```

```python
import jax
import jax.numpy as jnp
from jax import lax
from jax.experimental import pallas as pl
from jax.experimental.pallas import tpu as pltpu
from jax.sharding import PartitionSpec as P

WH = 1280
WB = 768
WL = 1024


EPS = 1e-05


def layer_norm(values):
    wide = values.astype(jnp.float32)
    center = wide - jnp.mean(wide, axis=-1, keepdims=True)
    spread = jnp.mean(center * center, axis=-1, keepdims=True)
    return center * lax.rsqrt(spread + EPS)


def swoosh_low(pre_act):
    return jax.nn.softplus(pre_act - 4.0) - 0.08 * pre_act - 0.035


def swoosh_slope(pre_act):
    return jax.nn.sigmoid(pre_act - 4.0) - 0.08


def column_scale():
    return jnp.concatenate(
        [
            jnp.full((WH,), 2.0 / WH, jnp.float32),
            jnp.full((WB,), 2.0 / WB, jnp.float32),
            jnp.full((WL,), 2.0 / WL, jnp.float32),
        ]
    )


GRAD_ROWS = 192
MESH_ID = pl.DeviceIdType.MESH


def grad_kernel(
    in_t, act_t, feat_t, pre, fgrad, err, out,
    lin, lact, lfeat, rpre, rfg, rerr,
    own1, send1, recv1, send2, recv2, send3, recv3, mine3,
    xs, xr, s1s, s1r, s2s, s2r, s3s, s3r, s4s, s4r,
):
    y = lax.axis_index("teacher")
    dp = lax.axis_index("dp")
    c = dp % 2
    z = (dp // 2) % 4
    x = dp // 8
    swap = c == 1
    first = jnp.where(swap, z, x)
    second = jnp.where(swap, x, z)

    def at_first(a):
        return {"dp": jnp.where(swap, (x * 4 + a) * 2 + 1, (a * 4 + z) * 2)}

    def at_second(b):
        return {"dp": jnp.where(swap, (b * 4 + z) * 2 + 1, (x * 4 + b) * 2)}

    def at_y(t):
        return {"teacher": t}

    pair = {"dp": (x * 4 + z) * 2 + (1 - c)}
    barrier = pltpu.get_barrier_semaphore()
    pl.semaphore_signal(barrier, inc=1, device_id=pair, device_id_type=MESH_ID)
    for d in range(1, 4):
        for dev in (at_first((first + d) % 4), at_second((second + d) % 4), at_y((y + d) % 4)):
            pl.semaphore_signal(barrier, inc=1, device_id=dev, device_id_type=MESH_ID)
    pl.semaphore_wait(barrier, 10)

    swaps = []
    for i, (src, dst) in enumerate((
        (fgrad, rfg.at[pl.ds(128, 128)]),
        (act_t.at[1 - c], lact.at[:, :, :, pl.ds(128, 128)]),
        (in_t.at[1 - c], lin.at[:, :, :, pl.ds(128, 128)]),
        (feat_t.at[1 - c], lfeat.at[:, :, :, pl.ds(128, 128)]),
        (pre, rpre.at[pl.ds(128, 128)]),
        (err, rerr.at[pl.ds(128, 128)]),
    )):
        cp = pltpu.make_async_remote_copy(
            src_ref=src, dst_ref=dst, send_sem=xs.at[i], recv_sem=xr.at[i],
            device_id=pair, device_id_type=MESH_ID)
        cp.start()
        swaps.append(cp)
    lin[:, :, :, 0:128] = in_t[c]
    lact[:, :, :, 0:128] = act_t[c]
    lfeat[:, :, :, 0:128] = feat_t[c]
    rpre[0:128] = pre[...]
    rfg[0:128] = fgrad[...]
    rerr[0:128] = err[...]
    for cp in swaps:
        cp.wait()

    def block(a, store):
        li = lin[a].reshape(64, 256)
        lo = lact[a].reshape(192, 256)
        lh = lfeat[a].reshape(64, 256)
        for n in range(3):
            v = jnp.dot(li, rpre[:, 512 * n:512 * n + 512], preferred_element_type=jnp.float32)
            store(16 * n, 16, v.reshape(4, 16, 512))
        v = jnp.dot(lo, rfg[...], preferred_element_type=jnp.float32)
        store(48, 48, v.reshape(4, 48, 512))
        for n in range(6):
            v = jnp.dot(lh, rerr[:, 512 * n:512 * n + 512], preferred_element_type=jnp.float32)
            store(96 + 16 * n, 16, v.reshape(4, 16, 512))

    def send(src, dst, ssem, rsem, dev):
        cp = pltpu.make_async_remote_copy(
            src_ref=src, dst_ref=dst, send_sem=ssem, recv_sem=rsem,
            device_id=dev, device_id_type=MESH_ID)
        cp.start()
        return cp

    copies = {}
    for d in (2, 1, 3):
        a = (first + d) % 4

        def put(r, h, v, d=d):
            send1[d - 1, :, r:r + h, :] = v.astype(send1.dtype)
        block(a, put)
        copies[d] = send(send1.at[d - 1], recv1.at[d - 1], s1s.at[d - 1], s1r.at[d - 1], at_first(a))

    def put_own(r, h, v):
        own1[:, r:r + h, :] = v
    block(first, put_own)
    for d in (1, 3, 2):
        copies[d].wait()

    def total1(b):
        return (own1[b] + recv1[0, b].astype(jnp.float32)
                + recv1[1, b].astype(jnp.float32) + recv1[2, b].astype(jnp.float32))

    for d in (2, 1, 3):
        b = (second + d) % 4
        send2[d - 1] = total1(b).astype(send2.dtype)
        copies[d] = send(send2.at[d - 1], recv2.at[d - 1], s2s.at[d - 1], s2r.at[d - 1], at_second(b))
    own2 = total1(second)
    for d in (1, 3, 2):
        copies[d].wait()
    total = (own2 + recv2[0].astype(jnp.float32) + recv2[1].astype(jnp.float32)
             + recv2[2].astype(jnp.float32))
    send3[...] = total.reshape(4, 48, 512)
    for d in (2, 1, 3):
        t = (y + d) % 4
        copies[d] = send(send3.at[t], recv3.at[d - 1], s3s.at[d - 1], s3r.at[d - 1], at_y(t))
    for d in (1, 3, 2):
        copies[d].wait()
    final = send3[y] + recv3[0] + recv3[1] + recv3[2]
    mine3[...] = final
    out[y] = final
    for d in (2, 1, 3):
        t = (y + d) % 4
        copies[d] = send(mine3, out.at[y], s4s.at[d - 1], s4r.at[d - 1], at_y(t))
    for d in (1, 3, 2):
        copies[d].wait()


def reduce_grads(student_in, activated, features, pre_grad, feat_grad, err_grad):
    def rows_of(values, h):
        t = values.T.reshape(4, 4, 2, h, values.shape[0])
        return jnp.stack([t[:, :, 0], t[:, :, 1].transpose(1, 0, 2, 3)])

    bf, f32 = jnp.bfloat16, jnp.float32
    vm = pl.BlockSpec(memory_space=pltpu.VMEM)
    dma = pltpu.SemaphoreType.DMA
    g = GRAD_ROWS
    out = pl.pallas_call(
        grad_kernel,
        out_shape=jax.ShapeDtypeStruct((4, 48, 512), f32),
        in_specs=[vm] * 6,
        out_specs=vm,
        scratch_shapes=[
            pltpu.VMEM((4, 4, 16, 256), bf), pltpu.VMEM((4, 4, 48, 256), bf), pltpu.VMEM((4, 4, 16, 256), bf),
            pltpu.VMEM((256, 1536), bf), pltpu.VMEM((256, 512), bf), pltpu.VMEM((256, 3072), bf),
            pltpu.VMEM((4, g, 512), f32), pltpu.VMEM((3, 4, g, 512), bf), pltpu.VMEM((3, 4, g, 512), bf),
            pltpu.VMEM((3, g, 512), bf), pltpu.VMEM((3, g, 512), bf),
            pltpu.VMEM((4, 48, 512), f32), pltpu.VMEM((3, 48, 512), f32), pltpu.VMEM((48, 512), f32),
            dma((6,)), dma((6,)), dma((3,)), dma((3,)), dma((3,)), dma((3,)), dma((3,)), dma((3,)), dma((3,)), dma((3,)),
        ],
        compiler_params=pltpu.CompilerParams(
            collective_id=0, has_side_effects=True, vmem_limit_bytes=40 * 1024 * 1024),
    )(rows_of(student_in, 16), rows_of(activated, 48), rows_of(features, 16), pre_grad, feat_grad, err_grad)
    flat = out.reshape(g, 512)
    wide = lambda v, n: v.reshape(n, 16, 512).transpose(1, 0, 2).reshape(16, n * 512)
    return wide(flat[0:48], 3), flat[48:96], wide(flat[96:192], 6)


def body(
    hid_whisper,
    hid_beats,
    hid_wavlm,
    up_whisper,
    down_whisper,
    up_beats,
    down_beats,
    up_wavlm,
    down_wavlm,
    clip_len,
    send_counts,
    student_in,
    w_in,
    w_out,
    w_head,
):
    owner_count = lax.axis_size("dp")
    owner_index = lax.axis_index("dp")
    frames = hid_whisper.shape[0]
    capacity = 2 * frames // owner_count
    normed_whisper = layer_norm(hid_whisper).astype(jnp.bfloat16)
    normed_beats = layer_norm(hid_beats).astype(jnp.bfloat16)
    normed_wavlm = layer_norm(hid_wavlm).astype(jnp.bfloat16)
    gathered = (
        lax.all_gather(normed_whisper, "teacher", axis=0, tiled=True),
        lax.all_gather(normed_beats, "teacher", axis=0, tiled=True),
        lax.all_gather(normed_wavlm, "teacher", axis=0, tiled=True),
    )
    pairs = ((up_whisper, down_whisper), (up_beats, down_beats), (up_wavlm, down_wavlm))
    pieces = []
    for rows_all, (up_proj, down_proj) in zip(gathered, pairs):
        hidden = jax.nn.gelu(
            jnp.dot(rows_all, up_proj, preferred_element_type=jnp.float32), approximate=False
        ).astype(jnp.bfloat16)
        pieces.append(jnp.dot(hidden, down_proj, preferred_element_type=jnp.float32))
    summed = lax.psum_scatter(
        jnp.concatenate(pieces, axis=1), "teacher", scatter_dimension=0, tiled=True
    )
    residual = jnp.concatenate([hid_whisper, hid_beats, hid_wavlm], axis=1).astype(jnp.float32)
    targets = (summed + residual).astype(jnp.bfloat16)
    positions = jnp.arange(frames, dtype=jnp.int32)
    clip_slots = frames // clip_len.shape[0]
    lengths = jnp.repeat(clip_len, clip_slots, total_repeat_length=frames)
    valid = positions % clip_slots < lengths
    table = send_counts[0]
    send_row = lax.dynamic_index_in_dim(table, owner_index, 0, keepdims=False)
    recv_col = lax.dynamic_index_in_dim(table, owner_index, 1, keepdims=False)
    slots = jnp.arange(capacity, dtype=jnp.int32)
    send_start = jnp.cumsum(send_row, dtype=jnp.int32) - send_row
    slot_rows = jnp.minimum(send_start[:, None] + slots[None, :], frames - 1)
    slot_used = slots[None, :] < send_row[:, None]
    outgoing = targets[slot_rows]
    out_mask = jnp.where(slot_used, valid[slot_rows], False).astype(jnp.bfloat16)
    incoming, in_mask = (
        lax.all_to_all(outgoing, "dp", split_axis=0, concat_axis=0, tiled=True),
        lax.all_to_all(out_mask, "dp", split_axis=0, concat_axis=0, tiled=True),
    )
    recv_end = jnp.cumsum(recv_col, dtype=jnp.int32)
    recv_start = recv_end - recv_col
    source_of = jnp.sum(
        (recv_end[None, :] <= positions[:, None]).astype(jnp.int32), axis=1, dtype=jnp.int32
    )
    select = jnp.arange(owner_count, dtype=jnp.int32)[None, :] == source_of[:, None]
    within = positions - jnp.sum(jnp.where(select, recv_start[None, :], 0), axis=1, dtype=jnp.int32)
    flat_slot = source_of * capacity + within
    target = incoming.reshape(owner_count * capacity, incoming.shape[2])[flat_slot]
    frame_mask = in_mask.reshape(owner_count * capacity)[flat_slot].astype(jnp.float32)
    full_in, full_out, full_head = (
        lax.all_gather(w_in, "dp", axis=0, tiled=True),
        lax.all_gather(w_out, "dp", axis=0, tiled=True),
        lax.all_gather(w_head, "dp", axis=0, tiled=True),
    )
    pre_act = jnp.dot(student_in, full_in, preferred_element_type=jnp.float32)
    activated = swoosh_low(pre_act).astype(jnp.bfloat16)
    features = (
        student_in.astype(jnp.float32)
        + jnp.dot(activated, full_out, preferred_element_type=jnp.float32)
    ).astype(jnp.bfloat16)
    predicted = jnp.dot(features, full_head, preferred_element_type=jnp.float32)
    err_grad = (
        (predicted - target.astype(jnp.float32)) * column_scale()[None, :] * frame_mask[:, None]
    ).astype(jnp.bfloat16)
    feat_grad = jnp.dot(err_grad, full_head.T, preferred_element_type=jnp.float32).astype(
        jnp.bfloat16
    )
    act_grad = jnp.dot(feat_grad, full_out.T, preferred_element_type=jnp.float32)
    pre_grad = (act_grad * swoosh_slope(pre_act)).astype(jnp.bfloat16)
    return reduce_grads(student_in, activated, features, pre_grad, feat_grad, err_grad)


def solution(mesh):
    in_specs = (
        P(("teacher", "dp"), None),
        P(("teacher", "dp"), None),
        P(("teacher", "dp"), None),
        P(None, "teacher"),
        P("teacher", None),
        P(None, "teacher"),
        P("teacher", None),
        P(None, "teacher"),
        P("teacher", None),
        P(("teacher", "dp")),
        P("teacher", None, None),
        P(("teacher", "dp"), None),
        P("dp", None),
        P("dp", None),
        P("dp", None),
    )
    out_specs = (P("dp", None), P("dp", None), P("dp", None))
    return jax.shard_map(body, mesh=mesh, in_specs=in_specs, out_specs=out_specs, check_vma=False)
```

```python
import jax
import jax.numpy as jnp
from jax import lax
from jax.experimental import pallas as pl
from jax.experimental.pallas import tpu as pltpu
from jax.sharding import PartitionSpec as P

WH = 1280
WB = 768
WL = 1024


EPS = 1e-05


def layer_norm(values):
    wide = values.astype(jnp.float32)
    center = wide - jnp.mean(wide, axis=-1, keepdims=True)
    spread = jnp.mean(center * center, axis=-1, keepdims=True)
    return center * lax.rsqrt(spread + EPS)


def swoosh_low(pre_act):
    return jax.nn.softplus(pre_act - 4.0) - 0.08 * pre_act - 0.035


def swoosh_slope(pre_act):
    return jax.nn.sigmoid(pre_act - 4.0) - 0.08


def column_scale():
    return jnp.concatenate(
        [
            jnp.full((WH,), 2.0 / WH, jnp.float32),
            jnp.full((WB,), 2.0 / WB, jnp.float32),
            jnp.full((WL,), 2.0 / WL, jnp.float32),
        ]
    )


GRAD_ROWS = 192
MESH_ID = pl.DeviceIdType.MESH


def grad_kernel(
    in_t, act_t, feat_t, pre, fgrad, err, out,
    lin, lact, lfeat, rpre, rfg, rerr,
    own1, send1, recv1, send2, recv2, send3, recv3, mine3,
    xs, xr, s1s, s1r, s2s, s2r, s3s, s3r, s4s, s4r,
):
    y = lax.axis_index("teacher")
    dp = lax.axis_index("dp")
    c = dp % 2
    z = (dp // 2) % 4
    x = dp // 8
    swap = c == 1
    first = jnp.where(swap, z, x)
    second = jnp.where(swap, x, z)

    def at_first(a):
        return {"dp": jnp.where(swap, (x * 4 + a) * 2 + 1, (a * 4 + z) * 2)}

    def at_second(b):
        return {"dp": jnp.where(swap, (b * 4 + z) * 2 + 1, (x * 4 + b) * 2)}

    def at_y(t):
        return {"teacher": t}

    pair = {"dp": (x * 4 + z) * 2 + (1 - c)}
    barrier = pltpu.get_barrier_semaphore()
    pl.semaphore_signal(barrier, inc=1, device_id=pair, device_id_type=MESH_ID)
    for d in range(1, 4):
        for dev in (at_first((first + d) % 4), at_second((second + d) % 4), at_y((y + d) % 4)):
            pl.semaphore_signal(barrier, inc=1, device_id=dev, device_id_type=MESH_ID)
    pl.semaphore_wait(barrier, 10)

    swaps = []
    for i, (src, dst) in enumerate((
        (fgrad, rfg.at[pl.ds(128, 128)]),
        (act_t.at[1 - c], lact.at[:, :, :, pl.ds(128, 128)]),
        (in_t.at[1 - c], lin.at[:, :, :, pl.ds(128, 128)]),
        (feat_t.at[1 - c], lfeat.at[:, :, :, pl.ds(128, 128)]),
        (pre, rpre.at[pl.ds(128, 128)]),
        (err, rerr.at[pl.ds(128, 128)]),
    )):
        cp = pltpu.make_async_remote_copy(
            src_ref=src, dst_ref=dst, send_sem=xs.at[i], recv_sem=xr.at[i],
            device_id=pair, device_id_type=MESH_ID)
        cp.start()
        swaps.append(cp)
    lin[:, :, :, 0:128] = in_t[c]
    lact[:, :, :, 0:128] = act_t[c]
    lfeat[:, :, :, 0:128] = feat_t[c]
    rpre[0:128] = pre[...]
    rfg[0:128] = fgrad[...]
    rerr[0:128] = err[...]
    for cp in swaps:
        cp.wait()

    def block(a, store):
        li = lin[a].reshape(64, 256)
        lo = lact[a].reshape(192, 256)
        lh = lfeat[a].reshape(64, 256)
        for n in range(3):
            v = jnp.dot(li, rpre[:, 512 * n:512 * n + 512], preferred_element_type=jnp.float32)
            store(16 * n, 16, v.reshape(4, 16, 512))
        v = jnp.dot(lo, rfg[...], preferred_element_type=jnp.float32)
        store(48, 48, v.reshape(4, 48, 512))
        for n in range(6):
            v = jnp.dot(lh, rerr[:, 512 * n:512 * n + 512], preferred_element_type=jnp.float32)
            store(96 + 16 * n, 16, v.reshape(4, 16, 512))

    def send(src, dst, ssem, rsem, dev):
        cp = pltpu.make_async_remote_copy(
            src_ref=src, dst_ref=dst, send_sem=ssem, recv_sem=rsem,
            device_id=dev, device_id_type=MESH_ID)
        cp.start()
        return cp

    copies = {}
    for d in (2, 1, 3):
        a = (first + d) % 4

        def put(r, h, v, d=d):
            send1[d - 1, :, r:r + h, :] = v.astype(send1.dtype)
        block(a, put)
        copies[d] = send(send1.at[d - 1], recv1.at[d - 1], s1s.at[d - 1], s1r.at[d - 1], at_first(a))

    def put_own(r, h, v):
        own1[:, r:r + h, :] = v
    block(first, put_own)
    for d in (1, 3, 2):
        copies[d].wait()

    def total1(b):
        return (own1[b] + recv1[0, b].astype(jnp.float32)
                + recv1[1, b].astype(jnp.float32) + recv1[2, b].astype(jnp.float32))

    for d in (2, 1, 3):
        b = (second + d) % 4
        send2[d - 1] = total1(b).astype(send2.dtype)
        copies[d] = send(send2.at[d - 1], recv2.at[d - 1], s2s.at[d - 1], s2r.at[d - 1], at_second(b))
    own2 = total1(second)
    for d in (1, 3, 2):
        copies[d].wait()
    total = (own2 + recv2[0].astype(jnp.float32) + recv2[1].astype(jnp.float32)
             + recv2[2].astype(jnp.float32))
    send3[...] = total.reshape(4, 48, 512)
    for d in (2, 1, 3):
        t = (y + d) % 4
        copies[d] = send(send3.at[t], recv3.at[d - 1], s3s.at[d - 1], s3r.at[d - 1], at_y(t))
    for d in (1, 3, 2):
        copies[d].wait()
    final = send3[y] + recv3[0] + recv3[1] + recv3[2]
    mine3[...] = final
    out[y] = final
    for d in (2, 1, 3):
        t = (y + d) % 4
        copies[d] = send(mine3, out.at[y], s4s.at[d - 1], s4r.at[d - 1], at_y(t))
    for d in (1, 3, 2):
        copies[d].wait()


def reduce_grads(student_in, activated, features, pre_grad, feat_grad, err_grad):
    def rows_of(values, h):
        t = values.T.reshape(4, 4, 2, h, values.shape[0])
        return jnp.stack([t[:, :, 0], t[:, :, 1].transpose(1, 0, 2, 3)])

    bf, f32 = jnp.bfloat16, jnp.float32
    vm = pl.BlockSpec(memory_space=pltpu.VMEM)
    dma = pltpu.SemaphoreType.DMA
    g = GRAD_ROWS
    out = pl.pallas_call(
        grad_kernel,
        out_shape=jax.ShapeDtypeStruct((4, 48, 512), f32),
        in_specs=[vm] * 6,
        out_specs=vm,
        scratch_shapes=[
            pltpu.VMEM((4, 4, 16, 256), bf), pltpu.VMEM((4, 4, 48, 256), bf), pltpu.VMEM((4, 4, 16, 256), bf),
            pltpu.VMEM((256, 1536), bf), pltpu.VMEM((256, 512), bf), pltpu.VMEM((256, 3072), bf),
            pltpu.VMEM((4, g, 512), f32), pltpu.VMEM((3, 4, g, 512), bf), pltpu.VMEM((3, 4, g, 512), bf),
            pltpu.VMEM((3, g, 512), bf), pltpu.VMEM((3, g, 512), bf),
            pltpu.VMEM((4, 48, 512), f32), pltpu.VMEM((3, 48, 512), f32), pltpu.VMEM((48, 512), f32),
            dma((6,)), dma((6,)), dma((3,)), dma((3,)), dma((3,)), dma((3,)), dma((3,)), dma((3,)), dma((3,)), dma((3,)),
        ],
        compiler_params=pltpu.CompilerParams(
            collective_id=0, has_side_effects=True, vmem_limit_bytes=40 * 1024 * 1024),
    )(rows_of(student_in, 16), rows_of(activated, 48), rows_of(features, 16), pre_grad, feat_grad, err_grad)
    flat = out.reshape(g, 512)
    wide = lambda v, n: v.reshape(n, 16, 512).transpose(1, 0, 2).reshape(16, n * 512)
    return wide(flat[0:48], 3), flat[48:96], wide(flat[96:192], 6)


TEACHERS = ((2, WL, WH + WB), (0, WH, 0), (1, WB, WH))


def gelu(values):
    return 0.5 * values * (1.0 + lax.erf(values * 0.7071067811865476))


def teacher_kernel(*refs):
    hid = refs[0:3]
    ups, downs = refs[3:9:2], refs[4:9:2]
    shards = refs[9:12]
    targets = refs[12]
    full = refs[13:16]
    scratch = refs[16:]
    vup, vdown, normed, keep, part, sopp, ropp, sside, rside = (scratch[3 * i:3 * i + 3] for i in range(9))
    hidden, wsem, ags, agr, fws, fwr, ops_, opr, sds, sdr, w1s, w1r, w2s, w2r, w3s, w3r = scratch[27:]
    y = lax.axis_index("teacher")
    dp = lax.axis_index("dp")
    c = dp % 2
    z = (dp // 2) % 4
    x = dp // 8
    swap = c == 1
    first = jnp.where(swap, z, x)
    second = jnp.where(swap, x, z)
    right, left = {"teacher": (y + 1) % 4}, {"teacher": (y + 3) % 4}
    pair = {"dp": (x * 4 + z) * 2 + (1 - c)}

    def at_first(a):
        return {"dp": jnp.where(swap, (x * 4 + a) * 2 + 1, (a * 4 + z) * 2)}

    def at_second(b):
        return {"dp": jnp.where(swap, (b * 4 + z) * 2 + 1, (x * 4 + b) * 2)}

    loads = {}
    for n, (k, _, _) in enumerate(TEACHERS):
        loads[k] = (pltpu.make_async_copy(ups[k], vup[k], wsem.at[2 * n]),
                    pltpu.make_async_copy(downs[k], vdown[k], wsem.at[2 * n + 1]))
        for cp in loads[k]:
            cp.start()

    barrier = pltpu.get_barrier_semaphore()
    for dev in (right, left, pair):
        pl.semaphore_signal(barrier, inc=1, device_id=dev, device_id_type=MESH_ID)
    for d in range(1, 4):
        for dev in (at_first((first + d) % 4), at_second((second + d) % 4)):
            pl.semaphore_signal(barrier, inc=1, device_id=dev, device_id_type=MESH_ID)
    for k in range(3):
        normed[k][0] = layer_norm(hid[k][...]).astype(jnp.bfloat16)
    for k in range(3):
        full[k][x, z, c] = shards[k][...]
    pl.semaphore_wait(barrier, 9)

    def send(src, dst, ssem, rsem, dev):
        cp = pltpu.make_async_remote_copy(
            src_ref=src, dst_ref=dst, send_sem=ssem, recv_sem=rsem,
            device_id=dev, device_id_type=MESH_ID)
        cp.start()
        return cp

    def gather_out(k):
        return (send(normed[k].at[0], normed[k].at[1], ags.at[k, 0], agr.at[k, 0], right),
                send(normed[k].at[0], normed[k].at[2], ags.at[k, 1], agr.at[k, 1], left))

    def forward(k):
        lo, hi = pl.ds(0, 64), pl.ds(64, 64)
        return (send(normed[k].at[1, lo], normed[k].at[3, lo], fws.at[k, 0], fwr.at[k, 0], right),
                send(normed[k].at[2, hi], normed[k].at[3, hi], fws.at[k, 1], fwr.at[k, 1], left))

    def ffn(k, width, slot, count, store):
        rows = count * 128

        def up_tile(j, carry):
            cols = pl.ds(pl.multiple_of(j * 256, 256), 256)
            values = normed[k][slot:slot + count].reshape(rows, width)
            wide = jnp.dot(values, vup[k][:, cols], preferred_element_type=jnp.float32)
            hidden[0:rows, cols] = gelu(wide).astype(jnp.bfloat16)
            return carry

        def down_tile(j, carry):
            cols = pl.ds(pl.multiple_of(j * 256, 256), 256)
            store(cols, jnp.dot(hidden[0:rows, 0:width], vdown[k][:, cols], preferred_element_type=jnp.float32))
            return carry

        lax.fori_loop(0, width // 256, up_tile, 0)
        lax.fori_loop(0, width // 256, down_tile, 0)

    order = [k for k, _, _ in TEACHERS]
    gathers = {order[0]: gather_out(order[0])}
    stage1 = []
    for d in (2, 1, 3):
        for m in range(3):
            stage1.append(send(shards[m], full[m].at[x, z, c], w1s.at[d - 1, m], w1r.at[d - 1, m],
                               at_first((first + d) % 4)))
    gathers[order[1]] = gather_out(order[1])
    stage2, stage3 = [], []

    def weights_second():
        for cp in stage1:
            cp.wait()
        for d in (2, 1, 3):
            dev = at_second((second + d) % 4)
            for m in range(3):
                for i in range(4):
                    slot = full[m].at[jnp.where(swap, x, i), jnp.where(swap, i, z), c]
                    stage2.append(send(slot, slot, w2s.at[d - 1, m, i], w2r.at[d - 1, m, i], dev))

    def weights_third():
        for cp in stage2:
            cp.wait()
        for m in range(3):
            half = full[m].at[:, :, c]
            stage3.append(send(half, half, w3s.at[m], w3r.at[m], pair))

    opposite, sides = {}, {}

    def send_sides(k):
        for cp in opposite[k]:
            cp.wait()
        sside[k][0, 0:64] = part[k][0, 0:64].astype(jnp.bfloat16)
        sside[k][0, 64:128] = (part[k][0, 64:128] + ropp[k][1].astype(jnp.float32)).astype(jnp.bfloat16)
        sside[k][1, 0:64] = (part[k][1, 0:64] + ropp[k][0].astype(jnp.float32)).astype(jnp.bfloat16)
        sside[k][1, 64:128] = part[k][1, 64:128].astype(jnp.bfloat16)
        sides[k] = (send(sside[k].at[1], rside[k].at[0], sds.at[k, 0], sdr.at[k, 0], right),
                    send(sside[k].at[0], rside[k].at[1], sds.at[k, 1], sdr.at[k, 1], left))

    for n, (k, width, _) in enumerate(TEACHERS):
        for cp in loads[k]:
            cp.wait()

        def put_keep(cols, v):
            keep[k][:, cols] = v
        ffn(k, width, 0, 1, put_keep)
        for cp in gathers[k]:
            cp.wait()
        passed = forward(k)
        if n + 2 < 3:
            gathers[order[n + 2]] = gather_out(order[n + 2])
        if n > 0:
            send_sides(order[n - 1])

        def put_part(cols, v):
            part[k][:, :, cols] = v.reshape(2, 128, 256)
        ffn(k, width, 1, 2, put_part)
        for cp in passed:
            cp.wait()

        def put_opp(cols, v):
            sopp[k][:, :, cols] = v.astype(jnp.bfloat16).reshape(2, 64, 256)
        ffn(k, width, 3, 1, put_opp)
        opposite[k] = (send(sopp[k].at[0], ropp[k].at[0], ops_.at[k, 0], opr.at[k, 0], right),
                       send(sopp[k].at[1], ropp[k].at[1], ops_.at[k, 1], opr.at[k, 1], left))
        if n == 0:
            weights_second()
        if n == 1:
            weights_third()
    send_sides(order[2])
    for k, width, start in TEACHERS:
        for cp in sides[k]:
            cp.wait()
        total = (hid[k][...].astype(jnp.float32) + keep[k][...]
                 + rside[k][0].astype(jnp.float32) + rside[k][1].astype(jnp.float32))
        targets[:, start:start + width] = total.astype(jnp.bfloat16)
    for cp in stage3:
        cp.wait()


def teacher_targets(hid, ups, downs, shards):
    bf, f32 = jnp.bfloat16, jnp.float32
    vm = pl.BlockSpec(memory_space=pltpu.VMEM)
    hbm = pl.BlockSpec(memory_space=pl.ANY)
    dma = pltpu.SemaphoreType.DMA
    widths = (WH, WB, WL)
    each = lambda shape, kind: [pltpu.VMEM(shape(w), kind) for w in widths]
    pairs = [m for up_down in zip(ups, downs) for m in up_down]
    outs = pl.pallas_call(
        teacher_kernel,
        out_shape=[jax.ShapeDtypeStruct((128, 3072), bf)]
        + [jax.ShapeDtypeStruct((4, 4, 2) + s.shape, bf) for s in shards],
        in_specs=[vm] * 3 + [hbm] * 6 + [vm] * 3,
        out_specs=[vm] * 4,
        scratch_shapes=each(lambda w: (w, w), bf) + each(lambda w: (w, w), bf)
        + each(lambda w: (4, 128, w), bf) + each(lambda w: (128, w), f32) + each(lambda w: (2, 128, w), f32)
        + each(lambda w: (2, 64, w), bf) + each(lambda w: (2, 64, w), bf)
        + each(lambda w: (2, 128, w), bf) + each(lambda w: (2, 128, w), bf)
        + [pltpu.VMEM((256, WH), bf), dma((6,))]
        + [dma((3, 2))] * 8
        + [dma((3, 3))] * 2 + [dma((3, 3, 4))] * 2 + [dma((3,))] * 2,
        compiler_params=pltpu.CompilerParams(
            collective_id=1, has_side_effects=True, vmem_limit_bytes=56 * 1024 * 1024),
    )(*hid, *pairs, *shards)
    return outs[0], [o.reshape(-1, o.shape[-1]) for o in outs[1:]]


def body(
    hid_whisper,
    hid_beats,
    hid_wavlm,
    up_whisper,
    down_whisper,
    up_beats,
    down_beats,
    up_wavlm,
    down_wavlm,
    clip_len,
    send_counts,
    student_in,
    w_in,
    w_out,
    w_head,
):
    owner_count = lax.axis_size("dp")
    owner_index = lax.axis_index("dp")
    frames = hid_whisper.shape[0]
    capacity = 2 * frames // owner_count
    positions = jnp.arange(frames, dtype=jnp.int32)
    clip_slots = frames // clip_len.shape[0]
    lengths = jnp.repeat(clip_len, clip_slots, total_repeat_length=frames)
    frame_mask = (positions % clip_slots < lengths).astype(jnp.float32)
    table = send_counts[0]
    send_row = lax.dynamic_index_in_dim(table, owner_index, 0, keepdims=False)
    recv_col = lax.dynamic_index_in_dim(table, owner_index, 1, keepdims=False)
    slots = jnp.arange(capacity, dtype=jnp.int32)

    def slot_rows(counts):
        start = jnp.cumsum(counts, dtype=jnp.int32) - counts
        rows = jnp.where(slots[None, :] < counts[:, None], start[:, None] + slots[None, :], -1)
        return rows.reshape(-1)

    pick = (slot_rows(recv_col)[:, None] == positions[None, :]).astype(jnp.bfloat16)
    outgoing = jnp.dot(pick, student_in, preferred_element_type=jnp.float32).astype(jnp.bfloat16)
    incoming = lax.all_to_all(
        outgoing.reshape(owner_count, capacity, -1), "dp", split_axis=0, concat_axis=0, tiled=True
    )
    place = (positions[:, None] == slot_rows(send_row)[None, :]).astype(jnp.bfloat16)
    student = jnp.dot(
        place, incoming.reshape(owner_count * capacity, -1), preferred_element_type=jnp.float32
    ).astype(jnp.bfloat16)
    target, (full_in, full_out, full_head) = teacher_targets(
        (hid_whisper, hid_beats, hid_wavlm),
        (up_whisper, up_beats, up_wavlm),
        (down_whisper, down_beats, down_wavlm),
        (w_in, w_out, w_head),
    )
    pre_act = jnp.dot(student, full_in, preferred_element_type=jnp.float32)
    activated = swoosh_low(pre_act).astype(jnp.bfloat16)
    features = (
        student.astype(jnp.float32)
        + jnp.dot(activated, full_out, preferred_element_type=jnp.float32)
    ).astype(jnp.bfloat16)
    predicted = jnp.dot(features, full_head, preferred_element_type=jnp.float32)
    err_grad = (
        (predicted - target.astype(jnp.float32)) * column_scale()[None, :] * frame_mask[:, None]
    ).astype(jnp.bfloat16)
    feat_grad = jnp.dot(err_grad, full_head.T, preferred_element_type=jnp.float32).astype(
        jnp.bfloat16
    )
    act_grad = jnp.dot(feat_grad, full_out.T, preferred_element_type=jnp.float32)
    pre_grad = (act_grad * swoosh_slope(pre_act)).astype(jnp.bfloat16)
    return reduce_grads(student, activated, features, pre_grad, feat_grad, err_grad)


def solution(mesh):
    in_specs = (
        P(("teacher", "dp"), None),
        P(("teacher", "dp"), None),
        P(("teacher", "dp"), None),
        P(None, "teacher"),
        P("teacher", None),
        P(None, "teacher"),
        P("teacher", None),
        P(None, "teacher"),
        P("teacher", None),
        P(("teacher", "dp")),
        P("teacher", None, None),
        P(("teacher", "dp"), None),
        P("dp", None),
        P("dp", None),
        P("dp", None),
    )
    out_specs = (P("dp", None), P("dp", None), P("dp", None))
    return jax.shard_map(body, mesh=mesh, in_specs=in_specs, out_specs=out_specs, check_vma=False)
```

```python
import functools

import jax
import jax.numpy as jnp
from jax import lax
from jax.experimental import pallas as pl
from jax.experimental.pallas import tpu as pltpu
from jax.sharding import PartitionSpec as P

WH = 1280
WB = 768
WL = 1024
EPS = 1e-05


def layer_norm(values):
    wide = values.astype(jnp.float32)
    center = wide - jnp.mean(wide, axis=-1, keepdims=True)
    spread = jnp.mean(center * center, axis=-1, keepdims=True)
    return center * lax.rsqrt(spread + EPS)


MESH_ID = pl.DeviceIdType.MESH
TEACHERS = ((2, WL, WH + WB), (0, WH, 0), (1, WB, WH))
SPAN = 6144
GROUP_COLUMNS = ((0, 1024), (1024, 1280), (2304, 3840))


def gelu(values):
    return 0.5 * values * (1.0 + lax.erf(values * 0.7071067811865476))


def dot(a, b):
    return jnp.dot(a, b, preferred_element_type=jnp.float32)


def dot_t(a, b):
    return lax.dot_general(a, b, (((1,), (1,)), ((), ())), preferred_element_type=jnp.float32)


def scratch_plan():
    bf, f32 = jnp.bfloat16, jnp.float32
    vm, dma = pltpu.VMEM, pltpu.SemaphoreType.DMA
    plan = {}
    for k, w in enumerate((WH, WB, WL)):
        plan[f"vup{k}"] = vm((w, w), bf)
        plan[f"vdown{k}"] = vm((w, w), bf)
        plan[f"normed{k}"] = vm((4, 128, w), bf)
        plan[f"keep{k}"] = vm((128, w), f32)
        plan[f"part{k}"] = vm((2, 128, w), f32)
        plan[f"sopp{k}"] = vm((2, 64, w), bf)
        plan[f"ropp{k}"] = vm((2, 64, w), bf)
        plan[f"sside{k}"] = vm((2, 128, w), bf)
        plan[f"rside{k}"] = vm((2, 128, w), bf)
    for m, (h, w) in enumerate(((16, 1536), (48, 512), (16, 3072))):
        plan[f"full{m}"] = vm((4, 4, 2, h, w), bf)
    plan.update(
        hidden=vm((256, WH), bf),
        outgoing=vm((32, 8, 512), HAND), incoming=vm((32, 8, 512), HAND),
        student=vm((128, 512), bf),
        slope=vm((128, 1536), f32), predicted=vm((128, 3072), f32), fgrad=vm((128, 512), f32),
        tin=vm((4, 4, 2, 16, 128), bf), tact=vm((4, 4, 2, 48, 128), bf), tfeat=vm((4, 4, 2, 16, 128), bf),
        lin=vm((4, 4, 16, 256), bf), lact=vm((4, 4, 48, 256), bf), lfeat=vm((4, 4, 16, 256), bf),
        rpre=vm((256, 1536), bf), rfg=vm((256, 512), bf), rerr=vm((256, 3072), bf),
        own1=vm((4, 16, SPAN), f32), send1=vm((3, 4, 16, SPAN), bf), recv1=vm((3, 4, 16, SPAN), bf),
        own2=vm((16, SPAN), f32), send2=vm((3, 16, SPAN), bf), recv2=vm((3, 16, SPAN), bf),
        send3=vm((4, 16, 1536), bf), recv3=vm((3, 16, 1536), bf), mine3=vm((16, 1536), f32),
        wsem=dma((6,)),
        ags=dma((3, 2)), agr=dma((3, 2)), fws=dma((3, 2)), fwr=dma((3, 2)),
        ops=dma((3, 2)), opr=dma((3, 2)), sds=dma((3, 2)), sdr=dma((3, 2)),
        w1s=dma((3, 3)), w1r=dma((3, 3)), w2s=dma((3, 3, 4)), w2r=dma((3, 3, 4)), w3s=dma((3,)), w3r=dma((3,)),
        hos=dma((32,)), hor=dma((32,)),
        xs=dma((8,)), xr=dma((8,)),
        s1s=dma((3, 3)), s1r=dma((3, 3)), s2s=dma((3, 3)), s2r=dma((3, 3)),
        s3s=dma((3,)), s3r=dma((3,)), s4s=dma((3,)), s4r=dma((3,)),
    )
    return plan


HAND = jnp.bfloat16


def step_kernel(names, *refs):
    hid = refs[0:3]
    ups, downs = refs[3:9:2], refs[4:9:2]
    shards = refs[9:12]
    student_in, counts_ref, clip_ref, out = refs[12:16]
    r = dict(zip(names, refs[16:]))
    per = lambda name: [r[f"{name}{k}"] for k in range(3)]
    vup, vdown, normed, keep, part = per("vup"), per("vdown"), per("normed"), per("keep"), per("part")
    sopp, ropp, sside, rside, full = per("sopp"), per("ropp"), per("sside"), per("rside"), per("full")
    hidden, rerr, rfg, rpre = r["hidden"], r["rerr"], r["rfg"], r["rpre"]
    bf, f32 = jnp.bfloat16, jnp.float32

    y = lax.axis_index("teacher")
    dp = lax.axis_index("dp")
    c = dp % 2
    z = (dp // 2) % 4
    x = dp // 8
    swap = c == 1
    first = jnp.where(swap, z, x)
    second = jnp.where(swap, x, z)
    at_y = lambda t: {"teacher": t % 4}
    right, left = at_y(y + 1), at_y(y + 3)
    pair = {"dp": (x * 4 + z) * 2 + (1 - c)}

    def at_first(a):
        return {"dp": jnp.where(swap, (x * 4 + a) * 2 + 1, (a * 4 + z) * 2)}

    def at_second(b):
        return {"dp": jnp.where(swap, (b * 4 + z) * 2 + 1, (x * 4 + b) * 2)}

    def send(src, dst, ssem, rsem, dev):
        cp = pltpu.make_async_remote_copy(
            src_ref=src, dst_ref=dst, send_sem=ssem, recv_sem=rsem,
            device_id=dev, device_id_type=MESH_ID)
        cp.start()
        return cp

    def finish_all(copies):
        for cp in copies:
            cp.wait()

    loads = {}
    for n, (k, _, _) in enumerate(TEACHERS):
        loads[k] = (pltpu.make_async_copy(ups[k], vup[k], r["wsem"].at[2 * n]),
                    pltpu.make_async_copy(downs[k], vdown[k], r["wsem"].at[2 * n + 1]))
        for cp in loads[k]:
            cp.start()

    barrier = pltpu.get_barrier_semaphore()
    for d in range(1, 4):
        pl.semaphore_signal(barrier, inc=1, device_id=at_y(y + d), device_id_type=MESH_ID)
    for d in range(1, 32):
        pl.semaphore_signal(barrier, inc=1, device_id={"dp": (dp + d) % 32}, device_id_type=MESH_ID)
    order = [k for k, _, _ in TEACHERS]
    normed[order[0]][0] = layer_norm(hid[order[0]][...]).astype(bf)

    counts = counts_ref[...].astype(f32)
    iota = lambda shape, axis: lax.broadcasted_iota(jnp.int32, shape, axis)
    src_at, own_at = iota((32, 32), 0), iota((32, 32), 1)
    one = lambda hit: jnp.where(hit, 1.0, 0.0)
    exact = lambda v: v.astype(bf)
    before_src = dot(exact(one(own_at < src_at)), exact(counts))
    before_own = dot(exact(counts), exact(one(src_at < own_at)))
    my_col, my_row = one(own_at == dp), one(src_at == dp)
    row_at, slot_at = iota((256, 32), 0), iota((256, 32), 1) * 8
    spread = exact(one((row_at >= slot_at) & (row_at < slot_at + 8)))
    wide_col = lambda v: dot(spread, exact(jnp.broadcast_to(jnp.sum(v * my_col, axis=1, keepdims=True), (32, 128))))
    slot = (iota((256, 128), 0) & 7).astype(f32)
    hit = (iota((256, 128), 1).astype(f32) == wide_col(before_src) + slot) & (slot < wide_col(counts))
    leaving = dot(exact(one(hit)), student_in[...])
    r["outgoing"][...] = leaving.reshape(32, 8, 512).astype(HAND)
    r["incoming"][dp] = r["outgoing"][dp]
    slot_at2, col_at = iota((32, 256), 0) * 8, iota((32, 256), 1)
    spread2 = exact(one((col_at >= slot_at2) & (col_at < slot_at2 + 8)))
    wide_row = lambda v: dot(exact(jnp.broadcast_to(jnp.sum(v * my_row, axis=0, keepdims=True), (128, 32))), spread2)
    slot2 = (iota((128, 256), 1) & 7).astype(f32)
    hit2 = (iota((128, 256), 0).astype(f32) == wide_row(before_own) + slot2) & (slot2 < wide_row(counts))
    place = exact(one(hit2))
    mask = one(iota((128, 1), 0) < clip_ref[0])

    for m in range(3):
        full[m][x, z, c] = shards[m][...]
    pl.semaphore_wait(barrier, 34)

    def gather_out(k):
        return (send(normed[k].at[0], normed[k].at[1], r["ags"].at[k, 0], r["agr"].at[k, 0], right),
                send(normed[k].at[0], normed[k].at[2], r["ags"].at[k, 1], r["agr"].at[k, 1], left))

    def forward(k):
        lo, hi = pl.ds(0, 64), pl.ds(64, 64)
        return (send(normed[k].at[1, lo], normed[k].at[3, lo], r["fws"].at[k, 0], r["fwr"].at[k, 0], right),
                send(normed[k].at[2, hi], normed[k].at[3, hi], r["fws"].at[k, 1], r["fwr"].at[k, 1], left))

    def ffn(k, width, at, count, store):
        rows = count * 128
        values = normed[k][at:at + count].reshape(rows, width)
        for j in range(width // 256):
            cols = slice(256 * j, 256 * j + 256)
            hidden[0:rows, cols] = gelu(dot(values, vup[k][:, cols])).astype(bf)
        for j in range(width // 256):
            cols = slice(256 * j, 256 * j + 256)
            store(cols, dot(hidden[0:rows, 0:width], vdown[k][:, cols]))

    gathers = {order[0]: gather_out(order[0])}
    hand = []
    for d in range(1, 32):
        to = (dp + d) % 32
        hand.append(send(r["outgoing"].at[to], r["incoming"].at[dp], r["hos"].at[d], r["hor"].at[d], {"dp": to}))
    stage1 = []
    for d in (2, 1, 3):
        for m in range(3):
            stage1.append(send(shards[m], full[m].at[x, z, c], r["w1s"].at[d - 1, m], r["w1r"].at[d - 1, m],
                               at_first((first + d) % 4)))
    for k in order[1:]:
        normed[k][0] = layer_norm(hid[k][...]).astype(bf)
    gathers[order[1]] = gather_out(order[1])
    stage2, stage3 = [], []

    def weights_second():
        finish_all(stage1)
        for d in (2, 1, 3):
            dev = at_second((second + d) % 4)
            for m in range(3):
                for i in range(4):
                    place_at = full[m].at[jnp.where(swap, x, i), jnp.where(swap, i, z), c]
                    stage2.append(send(place_at, place_at, r["w2s"].at[d - 1, m, i], r["w2r"].at[d - 1, m, i], dev))

    def weights_third():
        finish_all(stage2)
        for m in range(3):
            half = full[m].at[:, :, c]
            stage3.append(send(half, half, r["w3s"].at[m], r["w3r"].at[m], pair))

    opposite, sides = {}, {}

    def send_sides(k):
        finish_all(opposite[k])
        sside[k][0, 0:64] = part[k][0, 0:64].astype(bf)
        sside[k][0, 64:128] = (part[k][0, 64:128] + ropp[k][1].astype(f32)).astype(bf)
        sside[k][1, 0:64] = (part[k][1, 0:64] + ropp[k][0].astype(f32)).astype(bf)
        sside[k][1, 64:128] = part[k][1, 64:128].astype(bf)
        sides[k] = (send(sside[k].at[1], rside[k].at[0], r["sds"].at[k, 0], r["sdr"].at[k, 0], right),
                    send(sside[k].at[0], rside[k].at[1], r["sds"].at[k, 1], r["sdr"].at[k, 1], left))

    def pair_send(i, src, dst):
        return send(src, dst, r["xs"].at[i], r["xr"].at[i], pair)

    def share_rows(i, values, h, mine, joined):
        mine[...] = values.T.reshape(4, 4, 2, h, 128)
        joined[:, :, :, 0:128] = mine[:, :, c]
        return pair_send(i, mine.at[:, :, 1 - c], joined.at[:, :, :, pl.ds(128, 128)])

    shared = {}
    for n, (k, width, _) in enumerate(TEACHERS):
        finish_all(loads[k])

        def put_keep(cols, v):
            keep[k][:, cols] = v
        ffn(k, width, 0, 1, put_keep)
        finish_all(gathers[k])
        passed = forward(k)
        if n == 0:
            gathers[order[2]] = gather_out(order[2])
        if n == 1:
            send_sides(order[0])

        def put_part(cols, v):
            part[k][:, :, cols] = v.reshape(2, 128, 256)
        ffn(k, width, 1, 2, put_part)
        if n == 0:
            weights_second()
            finish_all(hand)
            student = dot(place, r["incoming"][...].reshape(256, 512).astype(bf)).astype(bf)
            r["student"][...] = student
            shared["in"] = share_rows(0, student, 16, r["tin"], r["lin"])
        if n == 1:
            weights_third()
        finish_all(passed)

        def put_opp(cols, v):
            sopp[k][:, :, cols] = v.astype(bf).reshape(2, 64, 256)
        ffn(k, width, 3, 1, put_opp)
        opposite[k] = (send(sopp[k].at[0], ropp[k].at[0], r["ops"].at[k, 0], r["opr"].at[k, 0], right),
                       send(sopp[k].at[1], ropp[k].at[1], r["ops"].at[k, 1], r["opr"].at[k, 1], left))
    send_sides(order[1])
    finish_all(stage3)
    student = r["student"][...]
    pre_act = dot(student, full[0][...].reshape(512, 1536))
    shifted = pre_act - 4.0
    soft = jnp.maximum(shifted, 0.0) + jnp.log1p(jnp.exp(-jnp.abs(shifted)))
    activated = (soft - 0.08 * pre_act - 0.035).astype(bf)
    r["slope"][...] = jax.nn.sigmoid(shifted) - 0.08
    features = (student.astype(f32) + dot(activated, full[1][...].reshape(1536, 512))).astype(bf)
    send_sides(order[2])
    shared["feat"] = share_rows(1, features, 16, r["tfeat"], r["lfeat"])
    shared["act"] = share_rows(2, activated, 48, r["tact"], r["lact"])
    for k, width, start in TEACHERS:
        r["predicted"][:, start:start + width] = dot(features, full[2][:, :, :, :, start:start + width].reshape(512, width))

    def error_of(n):
        k, width, start = TEACHERS[n]
        cols = slice(start, start + width)
        finish_all(sides[k])
        total = hid[k][...].astype(f32) + keep[k][...] + rside[k][0].astype(f32) + rside[k][1].astype(f32)
        target = total.astype(bf).astype(f32)
        err = ((r["predicted"][:, cols] - target) * (2.0 / width) * mask).astype(bf)
        rerr[0:128, cols] = err
        cp = pair_send(3 + n, rerr.at[pl.ds(0, 128), pl.ds(start, width)], rerr.at[pl.ds(128, 128), pl.ds(start, width)])
        back = dot_t(err, full[2][:, :, :, :, cols].reshape(512, width))
        if n == 0:
            r["fgrad"][...] = back
        elif n == 1:
            r["fgrad"][...] += back
        else:
            back = r["fgrad"][...] + back
        return cp, back

    def block_rows(joined, a):
        tiles = [joined[jnp.where(swap, b, a), jnp.where(swap, a, b)] for b in range(4)]
        return jnp.concatenate(tiles, axis=0)

    def products(n, a, store):
        heads = block_rows(r["lfeat"], a)
        if n < 2:
            _, width, start = TEACHERS[n]
            store(GROUP_COLUMNS[n][0], dot(heads, rerr[:, start:start + width]).reshape(4, 16, width))
        else:
            store(2304, dot(block_rows(r["lin"], a), rpre[...]).reshape(4, 16, 1536))
            store(3840, dot(heads, rerr[:, WH:WH + WB]).reshape(4, 16, WB))
            outs = dot(block_rows(r["lact"], a), rfg[...]).reshape(4, 48, 512)
            for m in range(3):
                store(4608 + 512 * m, outs[:, 16 * m:16 * m + 16])

    phase1, phase2 = {}, {}

    def start_group(n):
        start, width = GROUP_COLUMNS[n]
        cols = pl.ds(start, width)
        copies = []
        for d in (2, 1, 3):
            a = (first + d) % 4

            def put(at, v):
                r["send1"][d - 1, :, :, at:at + v.shape[2]] = v.astype(bf)
            products(n, a, put)
            copies.append(send(r["send1"].at[d - 1, :, :, cols], r["recv1"].at[d - 1, :, :, cols],
                               r["s1s"].at[n, d - 1], r["s1r"].at[n, d - 1], at_first(a)))

        def put_own(at, v):
            r["own1"][:, :, at:at + v.shape[2]] = v
        products(n, first, put_own)
        phase1[n] = copies

    def next_group(n):
        start, width = GROUP_COLUMNS[n]
        cols = slice(start, start + width)
        ref_cols = pl.ds(start, width)
        finish_all(phase1[n])

        def total1(b):
            v = r["own1"][b, :, cols]
            for i in range(3):
                v = v + r["recv1"][i, b, :, cols].astype(f32)
            return v
        copies = []
        for d in (2, 1, 3):
            b = (second + d) % 4
            r["send2"][d - 1, :, cols] = total1(b).astype(bf)
            copies.append(send(r["send2"].at[d - 1, :, ref_cols], r["recv2"].at[d - 1, :, ref_cols],
                               r["s2s"].at[n, d - 1], r["s2r"].at[n, d - 1], at_second(b)))
        r["own2"][:, cols] = total1(second)
        phase2[n] = copies

    cp, _ = error_of(0)
    finish_all([cp, shared["feat"]])
    start_group(0)
    cp, _ = error_of(1)
    cp.wait()
    start_group(1)
    finish_all([shared["in"], shared["act"]])
    next_group(0)
    cp, back = error_of(2)
    feat_grad = back.astype(bf)
    rfg[0:128] = feat_grad
    late = [cp, pair_send(6, rfg.at[pl.ds(0, 128)], rfg.at[pl.ds(128, 128)])]
    act_grad = dot_t(feat_grad, full[1][...].reshape(1536, 512))
    rpre[0:128] = (act_grad * r["slope"][...]).astype(bf)
    late.append(pair_send(7, rpre.at[pl.ds(0, 128)], rpre.at[pl.ds(128, 128)]))
    finish_all(late)
    start_group(2)
    next_group(1)
    next_group(2)
    for n in range(3):
        finish_all(phase2[n])
    total = r["own2"][...]
    for i in range(3):
        total = total + r["recv2"][i].astype(f32)
    r["own2"][...] = total
    for t in range(4):
        r["send3"][t] = total[:, 1536 * t:1536 * t + 1536].astype(bf)
    copies = []
    for d in (2, 1, 3):
        t = (y + d) % 4
        copies.append(send(r["send3"].at[t], r["recv3"].at[d - 1], r["s3s"].at[d - 1], r["s3r"].at[d - 1], at_y(t)))
    finish_all(copies)
    final = r["own2"][:, pl.ds(pl.multiple_of(y * 1536, 1536), 1536)]
    for i in range(3):
        final = final + r["recv3"][i].astype(f32)
    r["mine3"][...] = final
    out[y] = final
    copies = []
    for d in (2, 1, 3):
        t = (y + d) % 4
        copies.append(send(r["mine3"], out.at[y], r["s4s"].at[d - 1], r["s4r"].at[d - 1], at_y(t)))
    finish_all(copies)


def body(
    hid_whisper, hid_beats, hid_wavlm,
    up_whisper, down_whisper, up_beats, down_beats, up_wavlm, down_wavlm,
    clip_len, send_counts, student_in, w_in, w_out, w_head,
):
    vm = pl.BlockSpec(memory_space=pltpu.VMEM)
    hbm = pl.BlockSpec(memory_space=pl.ANY)
    plan = scratch_plan()
    out = pl.pallas_call(
        functools.partial(step_kernel, tuple(plan)),
        out_shape=jax.ShapeDtypeStruct((4, 16, 1536), jnp.float32),
        in_specs=[vm] * 3 + [hbm] * 6 + [vm] * 5 + [pl.BlockSpec(memory_space=pltpu.SMEM)],
        out_specs=vm,
        scratch_shapes=list(plan.values()),
        compiler_params=pltpu.CompilerParams(
            collective_id=0, has_side_effects=True, vmem_limit_bytes=60 * 1024 * 1024),
    )(
        hid_whisper, hid_beats, hid_wavlm,
        up_whisper, down_whisper, up_beats, down_beats, up_wavlm, down_wavlm,
        w_in, w_out, w_head, student_in, send_counts[0], clip_len,
    )
    flat = out.transpose(1, 0, 2).reshape(16, SPAN)
    grad_in = flat[:, 2304:3840]
    grad_out = flat[:, 4608:].reshape(16, 3, 512).transpose(1, 0, 2).reshape(48, 512)
    grad_head = jnp.concatenate([flat[:, 1024:2304], flat[:, 3840:4608], flat[:, 0:1024]], axis=1)
    return grad_in, grad_out, grad_head


def solution(mesh):
    in_specs = (
        P(("teacher", "dp"), None),
        P(("teacher", "dp"), None),
        P(("teacher", "dp"), None),
        P(None, "teacher"),
        P("teacher", None),
        P(None, "teacher"),
        P("teacher", None),
        P(None, "teacher"),
        P("teacher", None),
        P(("teacher", "dp")),
        P("teacher", None, None),
        P(("teacher", "dp"), None),
        P("dp", None),
        P("dp", None),
        P("dp", None),
    )
    out_specs = (P("dp", None), P("dp", None), P("dp", None))
    return jax.shard_map(body, mesh=mesh, in_specs=in_specs, out_specs=out_specs, check_vma=False)
```

```python
import functools

import jax
import jax.numpy as jnp
from jax import lax
from jax.experimental import pallas as pl
from jax.experimental.pallas import tpu as pltpu
from jax.sharding import PartitionSpec as P

WH = 1280
WB = 768
WL = 1024
EPS = 1e-05


def layer_norm(values):
    wide = values.astype(jnp.float32)
    center = wide - jnp.mean(wide, axis=-1, keepdims=True)
    spread = jnp.mean(center * center, axis=-1, keepdims=True)
    return center * lax.rsqrt(spread + EPS)


MESH_ID = pl.DeviceIdType.MESH
TEACHERS = ((2, WL, WH + WB), (0, WH, 0), (1, WB, WH))
SPAN = 6144
GROUP_COLUMNS = ((0, 1024), (1024, 1280), (2304, 2304), (4608, 1536))
SUM_COLUMNS = ((0, 1024), (1024, 3584), (4608, 1536))


def gelu(values):
    return 0.5 * values * (1.0 + lax.erf(values * 0.7071067811865476))


def dot(a, b):
    return jnp.dot(a, b, preferred_element_type=jnp.float32)


def dot_t(a, b):
    return lax.dot_general(a, b, (((1,), (1,)), ((), ())), preferred_element_type=jnp.float32)


def scratch_plan():
    bf, f32 = jnp.bfloat16, jnp.float32
    vm, dma = pltpu.VMEM, pltpu.SemaphoreType.DMA
    plan = {}
    for k, w in enumerate((WH, WB, WL)):
        plan[f"hid{k}"] = vm((128, w), bf)
        plan[f"vup{k}"] = vm((w, w), bf)
        plan[f"vdown{k}"] = vm((w, w), bf)
        plan[f"normed{k}"] = vm((4, 128, w), bf)
        plan[f"keep{k}"] = vm((128, w), f32)
        plan[f"part{k}"] = vm((2, 128, w), f32)
        plan[f"sopp{k}"] = vm((2, 64, w), bf)
        plan[f"ropp{k}"] = vm((2, 64, w), bf)
        plan[f"sside{k}"] = vm((2, 128, w), bf)
        plan[f"rside{k}"] = vm((2, 128, w), bf)
    for m, (h, w) in enumerate(((16, 1536), (48, 512), (16, 3072))):
        plan[f"full{m}"] = vm((4, 4, 2, h, w), bf)
    plan.update(
        hidden=vm((256, WH), bf),
        outgoing=vm((32, 8, 512), HAND), incoming=vm((32, 8, 512), HAND),
        student=vm((128, 512), bf),
        slope=vm((128, 1536), f32), predicted=vm((128, 3072), f32), fgrad=vm((128, 512), f32),
        tin=vm((4, 4, 2, 16, 128), bf), tact=vm((4, 4, 2, 48, 128), bf), tfeat=vm((4, 4, 2, 16, 128), bf),
        lin=vm((4, 4, 16, 256), bf), lact=vm((4, 4, 48, 256), bf), lfeat=vm((4, 4, 16, 256), bf),
        rpre=vm((256, 1536), bf), rfg=vm((256, 512), bf), rerr=vm((256, 3072), bf),
        own1=vm((4, 16, SPAN), f32), send1=vm((3, 4, 16, SPAN), bf), recv1=vm((3, 4, 16, SPAN), bf),
        own2=vm((16, SPAN), f32), send2=vm((3, 16, SPAN), bf), recv2=vm((3, 16, SPAN), bf),
        sums=vm((4, 16, SPAN), bf),
        rows_in=vm((128, 512), bf), counts=vm((32, 32), jnp.int32),
        wsem=dma((6,)), isem=dma((8,)),
        ags=dma((3, 2)), agr=dma((3, 2)), fws=dma((3, 2)), fwr=dma((3, 2)),
        ops=dma((3, 2)), opr=dma((3, 2)), sds=dma((3, 2)), sdr=dma((3, 2)),
        w1s=dma((3, 3)), w1r=dma((3, 3)), w2s=dma((3, 3, 4)), w2r=dma((3, 3, 4)), w3s=dma((3,)), w3r=dma((3,)),
        hos=dma((32,)), hor=dma((32,)),
        xs=dma((8,)), xr=dma((8,)),
        s1s=dma((4, 3)), s1r=dma((4, 3)), s2s=dma((4, 3)), s2r=dma((4, 3)), s3s=dma((3, 3)), s3r=dma((3, 3)),
    )
    return plan


HAND = jnp.bfloat16


def step_kernel(names, *refs):
    ups, downs = refs[3:9:2], refs[4:9:2]
    shards = refs[9:12]
    clip_ref, grad_in, grad_out, grad_head = refs[14:18]
    r = dict(zip(names, refs[18:]))
    per = lambda name: [r[f"{name}{k}"] for k in range(3)]
    hid = per("hid")
    vup, vdown, normed, keep, part = per("vup"), per("vdown"), per("normed"), per("keep"), per("part")
    sopp, ropp, sside, rside, full = per("sopp"), per("ropp"), per("sside"), per("rside"), per("full")
    hidden, rerr, rfg, rpre = r["hidden"], r["rerr"], r["rfg"], r["rpre"]
    bf, f32 = jnp.bfloat16, jnp.float32

    order = [k for k, _, _ in TEACHERS]
    y = lax.axis_index("teacher")
    dp = lax.axis_index("dp")
    c = dp % 2
    z = (dp // 2) % 4
    x = dp // 8
    swap = c == 1
    first = jnp.where(swap, z, x)
    second = jnp.where(swap, x, z)
    at_y = lambda t: {"teacher": t % 4}
    right, left = at_y(y + 1), at_y(y + 3)
    pair = {"dp": (x * 4 + z) * 2 + (1 - c)}

    def at_first(a):
        return {"dp": jnp.where(swap, (x * 4 + a) * 2 + 1, (a * 4 + z) * 2)}

    def at_second(b):
        return {"dp": jnp.where(swap, (b * 4 + z) * 2 + 1, (x * 4 + b) * 2)}

    def send(src, dst, ssem, rsem, dev):
        cp = pltpu.make_async_remote_copy(
            src_ref=src, dst_ref=dst, send_sem=ssem, recv_sem=rsem,
            device_id=dev, device_id_type=MESH_ID)
        cp.start()
        return cp

    def finish_all(copies):
        for cp in copies:
            cp.wait()

    ready = {}
    for i, (name, src, dst) in enumerate((
        (order[0], refs[order[0]], hid[order[0]]),
        ("counts", refs[13], r["counts"]),
        ("rows", refs[12], r["rows_in"]),
        ("in", shards[0], full[0].at[x, z, c]),
        ("out", shards[1], full[1].at[x, z, c]),
        ("head", shards[2], full[2].at[x, z, c]),
        (order[1], refs[order[1]], hid[order[1]]),
        (order[2], refs[order[2]], hid[order[2]]),
    )):
        ready[name] = pltpu.make_async_copy(src, dst, r["isem"].at[i])
        ready[name].start()
    loads = {}
    for n, (k, _, _) in enumerate(TEACHERS):
        loads[k] = (pltpu.make_async_copy(ups[k], vup[k], r["wsem"].at[2 * n]),
                    pltpu.make_async_copy(downs[k], vdown[k], r["wsem"].at[2 * n + 1]))
        for cp in loads[k]:
            cp.start()

    barrier = pltpu.get_barrier_semaphore()
    for d in range(1, 4):
        pl.semaphore_signal(barrier, inc=1, device_id=at_y(y + d), device_id_type=MESH_ID)
    for d in range(1, 32):
        pl.semaphore_signal(barrier, inc=1, device_id={"dp": (dp + d) % 32}, device_id_type=MESH_ID)
    ready[order[0]].wait()
    normed[order[0]][0] = layer_norm(hid[order[0]][...]).astype(bf)

    ready["counts"].wait()
    counts = r["counts"][...].astype(f32)
    iota = lambda shape, axis: lax.broadcasted_iota(jnp.int32, shape, axis)
    src_at, own_at = iota((32, 32), 0), iota((32, 32), 1)
    one = lambda hit: jnp.where(hit, 1.0, 0.0)
    exact = lambda v: v.astype(bf)
    before_src = dot(exact(one(own_at < src_at)), exact(counts))
    before_own = dot(exact(counts), exact(one(src_at < own_at)))
    my_col, my_row = one(own_at == dp), one(src_at == dp)
    row_at, slot_at = iota((256, 32), 0), iota((256, 32), 1) * 8
    spread = exact(one((row_at >= slot_at) & (row_at < slot_at + 8)))
    wide_col = lambda v: dot(spread, exact(jnp.broadcast_to(jnp.sum(v * my_col, axis=1, keepdims=True), (32, 128))))
    slot = (iota((256, 128), 0) & 7).astype(f32)
    hit = (iota((256, 128), 1).astype(f32) == wide_col(before_src) + slot) & (slot < wide_col(counts))
    ready["rows"].wait()
    leaving = dot(exact(one(hit)), r["rows_in"][...])
    r["outgoing"][...] = leaving.reshape(32, 8, 512).astype(HAND)
    r["incoming"][dp] = r["outgoing"][dp]
    slot_at2, col_at = iota((32, 256), 0) * 8, iota((32, 256), 1)
    spread2 = exact(one((col_at >= slot_at2) & (col_at < slot_at2 + 8)))
    wide_row = lambda v: dot(exact(jnp.broadcast_to(jnp.sum(v * my_row, axis=0, keepdims=True), (128, 32))), spread2)
    slot2 = (iota((128, 256), 1) & 7).astype(f32)
    hit2 = (iota((128, 256), 0).astype(f32) == wide_row(before_own) + slot2) & (slot2 < wide_row(counts))
    place = exact(one(hit2))
    mask = one(iota((128, 1), 0) < clip_ref[0])

    finish_all([ready["in"], ready["out"], ready["head"]])
    pl.semaphore_wait(barrier, 34)

    def gather_out(k):
        return (send(normed[k].at[0], normed[k].at[1], r["ags"].at[k, 0], r["agr"].at[k, 0], right),
                send(normed[k].at[0], normed[k].at[2], r["ags"].at[k, 1], r["agr"].at[k, 1], left))

    def forward(k):
        lo, hi = pl.ds(0, 64), pl.ds(64, 64)
        return (send(normed[k].at[1, lo], normed[k].at[3, lo], r["fws"].at[k, 0], r["fwr"].at[k, 0], right),
                send(normed[k].at[2, hi], normed[k].at[3, hi], r["fws"].at[k, 1], r["fwr"].at[k, 1], left))

    def ffn(k, width, at, count, store):
        rows = count * 128
        values = normed[k][at:at + count].reshape(rows, width)
        for j in range(width // 256):
            cols = slice(256 * j, 256 * j + 256)
            hidden[0:rows, cols] = gelu(dot(values, vup[k][:, cols])).astype(bf)
        for j in range(width // 256):
            cols = slice(256 * j, 256 * j + 256)
            store(cols, dot(hidden[0:rows, 0:width], vdown[k][:, cols]))

    gathers = {order[0]: gather_out(order[0])}
    hand = []
    for d in range(1, 32):
        to = (dp + d) % 32
        hand.append(send(r["outgoing"].at[to], r["incoming"].at[dp], r["hos"].at[d], r["hor"].at[d], {"dp": to}))
    stage1 = []
    for d in (2, 1, 3):
        for m in range(3):
            stage1.append(send(full[m].at[x, z, c], full[m].at[x, z, c], r["w1s"].at[d - 1, m], r["w1r"].at[d - 1, m],
                               at_first((first + d) % 4)))
    for k in order[1:]:
        ready[k].wait()
        normed[k][0] = layer_norm(hid[k][...]).astype(bf)
    gathers[order[1]] = gather_out(order[1])
    stage2, stage3 = [], []

    def weights_second():
        finish_all(stage1)
        for d in (2, 1, 3):
            dev = at_second((second + d) % 4)
            for m in range(3):
                for i in range(4):
                    place_at = full[m].at[jnp.where(swap, x, i), jnp.where(swap, i, z), c]
                    stage2.append(send(place_at, place_at, r["w2s"].at[d - 1, m, i], r["w2r"].at[d - 1, m, i], dev))

    def weights_third():
        finish_all(stage2)
        for m in range(3):
            half = full[m].at[:, :, c]
            stage3.append(send(half, half, r["w3s"].at[m], r["w3r"].at[m], pair))

    opposite, sides = {}, {}

    def send_sides(k):
        finish_all(opposite[k])
        sside[k][0, 0:64] = part[k][0, 0:64].astype(bf)
        sside[k][0, 64:128] = (part[k][0, 64:128] + ropp[k][1].astype(f32)).astype(bf)
        sside[k][1, 0:64] = (part[k][1, 0:64] + ropp[k][0].astype(f32)).astype(bf)
        sside[k][1, 64:128] = part[k][1, 64:128].astype(bf)
        sides[k] = (send(sside[k].at[1], rside[k].at[0], r["sds"].at[k, 0], r["sdr"].at[k, 0], right),
                    send(sside[k].at[0], rside[k].at[1], r["sds"].at[k, 1], r["sdr"].at[k, 1], left))

    def pair_send(i, src, dst):
        return send(src, dst, r["xs"].at[i], r["xr"].at[i], pair)

    def share_rows(i, values, h, mine, joined):
        mine[...] = values.T.reshape(4, 4, 2, h, 128)
        joined[:, :, :, 0:128] = mine[:, :, c]
        return pair_send(i, mine.at[:, :, 1 - c], joined.at[:, :, :, pl.ds(128, 128)])

    shared, passed = {}, {}
    widths = [width for _, width, _ in TEACHERS]

    def own_rows(n):
        k = order[n]
        finish_all(loads[k])

        def put(cols, v):
            keep[k][:, cols] = v
        ffn(k, widths[n], 0, 1, put)

    def side_rows(n):
        k = order[n]

        def put(cols, v):
            part[k][:, :, cols] = v.reshape(2, 128, 256)
        ffn(k, widths[n], 1, 2, put)

    def pass_on(n):
        finish_all(gathers[order[n]])
        passed[n] = forward(order[n])

    def far_rows(n):
        k = order[n]
        finish_all(passed[n])

        def put(cols, v):
            sopp[k][:, :, cols] = v.astype(bf).reshape(2, 64, 256)
        ffn(k, widths[n], 3, 1, put)
        opposite[k] = (send(sopp[k].at[0], ropp[k].at[0], r["ops"].at[k, 0], r["opr"].at[k, 0], right),
                       send(sopp[k].at[1], ropp[k].at[1], r["ops"].at[k, 1], r["opr"].at[k, 1], left))

    own_rows(0)
    pass_on(0)
    gathers[order[2]] = gather_out(order[2])
    side_rows(0)
    own_rows(1)
    pass_on(1)
    side_rows(1)
    far_rows(0)
    weights_second()
    finish_all(hand)
    student = dot(place, r["incoming"][...].reshape(256, 512).astype(bf)).astype(bf)
    r["student"][...] = student
    shared["in"] = share_rows(0, student, 16, r["tin"], r["lin"])
    own_rows(2)
    pass_on(2)
    side_rows(2)
    far_rows(1)
    send_sides(order[0])
    far_rows(2)
    send_sides(order[1])
    weights_third()
    finish_all(stage3)
    student = r["student"][...]
    pre_act = dot(student, full[0][...].reshape(512, 1536))
    shifted = pre_act - 4.0
    soft = jnp.maximum(shifted, 0.0) + jnp.log1p(jnp.exp(-jnp.abs(shifted)))
    activated = (soft - 0.08 * pre_act - 0.035).astype(bf)
    r["slope"][...] = jax.nn.sigmoid(shifted) - 0.08
    features = (student.astype(f32) + dot(activated, full[1][...].reshape(1536, 512))).astype(bf)
    send_sides(order[2])
    shared["feat"] = share_rows(1, features, 16, r["tfeat"], r["lfeat"])
    shared["act"] = share_rows(2, activated, 48, r["tact"], r["lact"])
    for k, width, start in TEACHERS:
        r["predicted"][:, start:start + width] = dot(features, full[2][:, :, :, :, start:start + width].reshape(512, width))

    def error_of(n):
        k, width, start = TEACHERS[n]
        cols = slice(start, start + width)
        finish_all(sides[k])
        total = hid[k][...].astype(f32) + keep[k][...] + rside[k][0].astype(f32) + rside[k][1].astype(f32)
        target = total.astype(bf).astype(f32)
        err = ((r["predicted"][:, cols] - target) * (2.0 / width) * mask).astype(bf)
        rerr[0:128, cols] = err
        cp = pair_send(3 + n, rerr.at[pl.ds(0, 128), pl.ds(start, width)], rerr.at[pl.ds(128, 128), pl.ds(start, width)])
        back = dot_t(err, full[2][:, :, :, :, cols].reshape(512, width))
        if n == 0:
            r["fgrad"][...] = back
        elif n == 1:
            r["fgrad"][...] += back
        else:
            back = r["fgrad"][...] + back
        return cp, back

    def block_rows(joined, a):
        tiles = [joined[jnp.where(swap, b, a), jnp.where(swap, a, b)] for b in range(4)]
        return jnp.concatenate(tiles, axis=0)

    def products(n, a, store):
        heads = block_rows(r["lfeat"], a) if n < 3 else None
        if n < 2:
            _, width, start = TEACHERS[n]
            store(GROUP_COLUMNS[n][0], dot(heads, rerr[:, start:start + width]).reshape(4, 16, width))
        elif n == 2:
            store(2304, dot(heads, rerr[:, WH:WH + WB]).reshape(4, 16, WB))
            outs = dot(block_rows(r["lact"], a), rfg[...]).reshape(4, 48, 512)
            for m in range(3):
                store(3072 + 512 * m, outs[:, 16 * m:16 * m + 16])
        else:
            store(4608, dot(block_rows(r["lin"], a), rpre[...]).reshape(4, 16, 1536))

    phase1, phase2 = {}, {}

    def start_group(n):
        start, width = GROUP_COLUMNS[n]
        cols = pl.ds(start, width)
        copies = []
        for d in (2, 1, 3):
            a = (first + d) % 4

            def put(at, v):
                r["send1"][d - 1, :, :, at:at + v.shape[2]] = v.astype(bf)
            products(n, a, put)
            copies.append(send(r["send1"].at[d - 1, :, :, cols], r["recv1"].at[d - 1, :, :, cols],
                               r["s1s"].at[n, d - 1], r["s1r"].at[n, d - 1], at_first(a)))

        def put_own(at, v):
            r["own1"][:, :, at:at + v.shape[2]] = v
        products(n, first, put_own)
        phase1[n] = copies

    def next_group(n):
        start, width = GROUP_COLUMNS[n]
        cols = slice(start, start + width)
        ref_cols = pl.ds(start, width)
        finish_all(phase1[n])

        def total1(b):
            v = r["own1"][b, :, cols]
            for i in range(3):
                v = v + r["recv1"][i, b, :, cols].astype(f32)
            return v
        copies = []
        for d in (2, 1, 3):
            b = (second + d) % 4
            r["send2"][d - 1, :, cols] = total1(b).astype(bf)
            copies.append(send(r["send2"].at[d - 1, :, ref_cols], r["recv2"].at[d - 1, :, ref_cols],
                               r["s2s"].at[n, d - 1], r["s2r"].at[n, d - 1], at_second(b)))
        r["own2"][:, cols] = total1(second)
        phase2[n] = copies

    cp, _ = error_of(0)
    finish_all([cp, shared["feat"]])
    start_group(0)
    cp, _ = error_of(1)
    cp.wait()
    start_group(1)
    finish_all([shared["in"], shared["act"]])
    next_group(0)
    cp, back = error_of(2)
    feat_grad = back.astype(bf)
    rfg[0:128] = feat_grad
    late = [cp, pair_send(6, rfg.at[pl.ds(0, 128)], rfg.at[pl.ds(128, 128)])]
    act_grad = dot_t(feat_grad, full[1][...].reshape(1536, 512))
    rpre[0:128] = (act_grad * r["slope"][...]).astype(bf)
    cp = pair_send(7, rpre.at[pl.ds(0, 128)], rpre.at[pl.ds(128, 128)])
    finish_all(late)
    start_group(2)
    cp.wait()
    start_group(3)

    summed = {}

    def send_sums(q):
        start, width = SUM_COLUMNS[q]
        cols, ref_cols = slice(start, start + width), pl.ds(start, width)
        total = r["own2"][:, cols]
        for i in range(3):
            total = total + r["recv2"][i, :, cols].astype(f32)
        r["sums"][y, :, cols] = total.astype(bf)
        mine = r["sums"].at[y, :, ref_cols]
        summed[q] = [send(mine, mine, r["s3s"].at[q, d - 1], r["s3r"].at[q, d - 1], at_y(y + d)) for d in (2, 1, 3)]

    def sum_of(start, width):
        cols = slice(start, start + width)
        total = r["sums"][0, :, cols].astype(f32)
        for t in range(1, 4):
            total = total + r["sums"][t, :, cols].astype(f32)
        return total

    next_group(1)
    finish_all(phase2[0])
    send_sums(0)
    next_group(2)
    finish_all(phase2[1])
    next_group(3)
    finish_all(phase2[2])
    send_sums(1)
    finish_all(summed[0])
    grad_head[:, WH + WB:] = sum_of(0, 1024)
    finish_all(phase2[3])
    send_sums(2)
    finish_all(summed[1])
    grad_head[:, 0:WH + WB] = sum_of(1024, 2048)
    for m in range(3):
        grad_out[16 * m:16 * m + 16] = sum_of(3072 + 512 * m, 512)
    finish_all(summed[2])
    grad_in[...] = sum_of(4608, 1536)


def body(
    hid_whisper, hid_beats, hid_wavlm,
    up_whisper, down_whisper, up_beats, down_beats, up_wavlm, down_wavlm,
    clip_len, send_counts, student_in, w_in, w_out, w_head,
):
    vm = pl.BlockSpec(memory_space=pltpu.VMEM)
    hbm = pl.BlockSpec(memory_space=pl.ANY)
    plan = scratch_plan()
    f32 = jnp.float32
    return tuple(pl.pallas_call(
        functools.partial(step_kernel, tuple(plan)),
        out_shape=[jax.ShapeDtypeStruct((16, 1536), f32), jax.ShapeDtypeStruct((48, 512), f32),
                   jax.ShapeDtypeStruct((16, 3072), f32)],
        in_specs=[hbm] * 14 + [pl.BlockSpec(memory_space=pltpu.SMEM)],
        out_specs=[vm] * 3,
        scratch_shapes=list(plan.values()),
        compiler_params=pltpu.CompilerParams(
            collective_id=0, has_side_effects=True, vmem_limit_bytes=60 * 1024 * 1024),
    )(
        hid_whisper, hid_beats, hid_wavlm,
        up_whisper, down_whisper, up_beats, down_beats, up_wavlm, down_wavlm,
        w_in, w_out, w_head, student_in, send_counts[0], clip_len,
    ))


def solution(mesh):
    in_specs = (
        P(("teacher", "dp"), None),
        P(("teacher", "dp"), None),
        P(("teacher", "dp"), None),
        P(None, "teacher"),
        P("teacher", None),
        P(None, "teacher"),
        P("teacher", None),
        P(None, "teacher"),
        P("teacher", None),
        P(("teacher", "dp")),
        P("teacher", None, None),
        P(("teacher", "dp"), None),
        P("dp", None),
        P("dp", None),
        P("dp", None),
    )
    out_specs = (P("dp", None), P("dp", None), P("dp", None))
    return jax.shard_map(body, mesh=mesh, in_specs=in_specs, out_specs=out_specs, check_vma=False)
```

```python
import functools

import jax
import jax.numpy as jnp
from jax import lax
from jax.experimental import pallas as pl
from jax.experimental.pallas import tpu as pltpu
from jax.sharding import PartitionSpec as P

WH = 1280
WB = 768
WL = 1024
EPS = 1e-05


def layer_norm(values):
    wide = values.astype(jnp.float32)
    center = wide - jnp.mean(wide, axis=-1, keepdims=True)
    spread = jnp.mean(center * center, axis=-1, keepdims=True)
    return center * lax.rsqrt(spread + EPS)


MESH_ID = pl.DeviceIdType.MESH
TEACHERS = ((2, WL, WH + WB), (0, WH, 0), (1, WB, WH))
SPAN = 6144
GROUP_COLUMNS = ((0, 1024), (1024, 1280), (2304, 2304), (4608, 1536))
SUM_COLUMNS = ((0, 1024), (1024, 3584), (4608, 1536))


def gelu(values):
    return 0.5 * values * (1.0 + lax.erf(values * 0.7071067811865476))


def dot(a, b):
    return jnp.dot(a, b, preferred_element_type=jnp.float32)


def dot_t(a, b):
    return lax.dot_general(a, b, (((1,), (1,)), ((), ())), preferred_element_type=jnp.float32)


def scratch_plan():
    bf, f32 = jnp.bfloat16, jnp.float32
    vm, dma = pltpu.VMEM, pltpu.SemaphoreType.DMA
    plan = {}
    for k, w in enumerate((WH, WB, WL)):
        plan[f"hid{k}"] = vm((128, w), bf)
        plan[f"vup{k}"] = vm((w, w), bf)
        plan[f"vdown{k}"] = vm((w, w), bf)
        plan[f"keep{k}"] = vm((128, w), f32)
        plan[f"normed{k}"] = vm((1 if k == 1 else 4, 128, w), bf)
    for k, w in ((0, WH), (2, WL)):
        plan[f"part{k}"] = vm((2, 128, w), f32)
        plan[f"sopp{k}"] = vm((2, 64, w), bf)
        plan[f"ropp{k}"] = vm((2, 64, w), bf)
        plan[f"sside{k}"] = vm((2, 128, w), bf)
        plan[f"rside{k}"] = vm((2, 128, w), bf)
    for m, (h, w) in enumerate(((16, 1536), (48, 512), (16, 3072))):
        plan[f"full{m}"] = vm((4, 4, 2, h, w), bf)
    plan.update(
        hidden=vm((256, WH), bf),
        outgoing=vm((32, 8, 512), HAND), incoming=vm((32, 8, 512), HAND),
        student=vm((128, 512), bf),
        slope=vm((128, 1536), f32), predicted=vm((128, 3072), f32), fgrad=vm((128, 512), f32),
        tin=vm((4, 4, 2, 16, 128), bf), tact=vm((4, 4, 2, 48, 128), bf), tfeat=vm((4, 4, 2, 16, 128), bf),
        lin=vm((4, 4, 16, 256), bf), lact=vm((4, 4, 48, 256), bf), lfeat=vm((4, 4, 16, 256), bf),
        rpre=vm((256, 1536), bf), rfg=vm((256, 512), bf), rerr=vm((256, 3072), bf),
        own1=vm((4, 16, SPAN), f32), send1=vm((3, 4, 16, SPAN), bf), recv1=vm((3, 4, 16, SPAN), bf),
        own2=vm((16, SPAN), f32), send2=vm((3, 16, SPAN), bf), recv2=vm((3, 16, SPAN), bf),
        rows_in=vm((128, 512), bf), counts=vm((32, 32), jnp.int32),
        wsem=dma((6,)), isem=dma((8,)),
        ags=dma((3, 2)), agr=dma((3, 2)), fws=dma((3, 2)), fwr=dma((3, 2)),
        ops=dma((3, 2)), opr=dma((3, 2)), sds=dma((3, 2)), sdr=dma((3, 2)),
        piece=vm((2, 48, WB), bf), others=vm((2, 4, 4, 3, 48, WB), bf),
        psem=dma((2,)), pys=dma((3,)), pyr=dma((3,)), gs=dma((96,)), gr=dma((96,)),
        hos=dma((32,)), hor=dma((32,)),
        xs=dma((8,)), xr=dma((8,)),
        s1s=dma((4, 3)), s1r=dma((4, 3)), s2s=dma((4, 3)), s2r=dma((4, 3)), s3s=dma((3, 3)), s3r=dma((3, 3)),
    )
    return plan


HAND = jnp.bfloat16


def step_kernel(names, *refs):
    ups, downs = refs[3:9:2], refs[4:9:2]
    shards = refs[9:12]
    clip_ref, sums = refs[14:16]
    r = dict(zip(names, refs[16:]))
    per = lambda name: [r.get(f"{name}{k}") for k in range(3)]
    hid = per("hid")
    vup, vdown, normed, keep, part = per("vup"), per("vdown"), per("normed"), per("keep"), per("part")
    sopp, ropp, sside, rside, full = per("sopp"), per("ropp"), per("sside"), per("rside"), per("full")
    hidden, rerr, rfg, rpre = r["hidden"], r["rerr"], r["rfg"], r["rpre"]
    bf, f32 = jnp.bfloat16, jnp.float32

    order = [k for k, _, _ in TEACHERS]
    y = lax.axis_index("teacher")
    dp = lax.axis_index("dp")
    c = dp % 2
    z = (dp // 2) % 4
    x = dp // 8
    swap = c == 1
    first = jnp.where(swap, z, x)
    second = jnp.where(swap, x, z)
    at_y = lambda t: {"teacher": t % 4}
    right, left = at_y(y + 1), at_y(y + 3)
    pair = {"dp": (x * 4 + z) * 2 + (1 - c)}

    def at_first(a):
        return {"dp": jnp.where(swap, (x * 4 + a) * 2 + 1, (a * 4 + z) * 2)}

    def at_second(b):
        return {"dp": jnp.where(swap, (b * 4 + z) * 2 + 1, (x * 4 + b) * 2)}

    def send(src, dst, ssem, rsem, dev):
        cp = pltpu.make_async_remote_copy(
            src_ref=src, dst_ref=dst, send_sem=ssem, recv_sem=rsem,
            device_id=dev, device_id_type=MESH_ID)
        cp.start()
        return cp

    def finish_all(copies):
        for cp in copies:
            cp.wait()

    ready = {}
    for i, (name, src, dst) in enumerate((
        (order[0], refs[order[0]], hid[order[0]]),
        ("counts", refs[13], r["counts"]),
        ("rows", refs[12], r["rows_in"]),
        ("in", shards[0], full[0].at[x, z, c]),
        ("out", shards[1], full[1].at[x, z, c]),
        ("head", shards[2], full[2].at[x, z, c]),
        (order[1], refs[order[1]], hid[order[1]]),
        (order[2], refs[order[2]], hid[order[2]]),
    )):
        ready[name] = pltpu.make_async_copy(src, dst, r["isem"].at[i])
        ready[name].start()
    piece_rows = pl.ds(pl.multiple_of((x * 4 + z) * 48, 48), 48)
    pieces = [pltpu.make_async_copy(src.at[piece_rows], r["piece"].at[i], r["psem"].at[i])
              for i, src in enumerate((ups[1], downs[1]))]
    for cp in pieces:
        cp.start()
    loads = {}
    for n, (k, _, _) in enumerate(TEACHERS):
        loads[k] = (pltpu.make_async_copy(ups[k], vup[k], r["wsem"].at[2 * n]),
                    pltpu.make_async_copy(downs[k], vdown[k], r["wsem"].at[2 * n + 1]))
        for cp in loads[k]:
            cp.start()

    barrier = pltpu.get_barrier_semaphore()
    for d in range(1, 4):
        pl.semaphore_signal(barrier, inc=1, device_id=at_y(y + d), device_id_type=MESH_ID)
    for d in range(1, 32):
        pl.semaphore_signal(barrier, inc=1, device_id={"dp": (dp + d) % 32}, device_id_type=MESH_ID)
    ready[order[0]].wait()
    normed[order[0]][0] = layer_norm(hid[order[0]][...]).astype(bf)

    ready["counts"].wait()
    counts = r["counts"][...].astype(f32)
    iota = lambda shape, axis: lax.broadcasted_iota(jnp.int32, shape, axis)
    src_at, own_at = iota((32, 32), 0), iota((32, 32), 1)
    one = lambda hit: jnp.where(hit, 1.0, 0.0)
    exact = lambda v: v.astype(bf)
    before_src = dot(exact(one(own_at < src_at)), exact(counts))
    before_own = dot(exact(counts), exact(one(src_at < own_at)))
    my_col, my_row = one(own_at == dp), one(src_at == dp)
    row_at, slot_at = iota((256, 32), 0), iota((256, 32), 1) * 8
    spread = exact(one((row_at >= slot_at) & (row_at < slot_at + 8)))
    wide_col = lambda v: dot(spread, exact(jnp.broadcast_to(jnp.sum(v * my_col, axis=1, keepdims=True), (32, 128))))
    slot = (iota((256, 128), 0) & 7).astype(f32)
    hit = (iota((256, 128), 1).astype(f32) == wide_col(before_src) + slot) & (slot < wide_col(counts))
    ready["rows"].wait()
    leaving = dot(exact(one(hit)), r["rows_in"][...])
    r["outgoing"][...] = leaving.reshape(32, 8, 512).astype(HAND)
    r["incoming"][dp] = r["outgoing"][dp]
    slot_at2, col_at = iota((32, 256), 0) * 8, iota((32, 256), 1)
    spread2 = exact(one((col_at >= slot_at2) & (col_at < slot_at2 + 8)))
    wide_row = lambda v: dot(exact(jnp.broadcast_to(jnp.sum(v * my_row, axis=0, keepdims=True), (128, 32))), spread2)
    slot2 = (iota((128, 256), 1) & 7).astype(f32)
    hit2 = (iota((128, 256), 0).astype(f32) == wide_row(before_own) + slot2) & (slot2 < wide_row(counts))
    place = exact(one(hit2))
    mask = one(iota((128, 1), 0) < clip_ref[0])

    finish_all([ready["in"], ready["out"], ready["head"]])
    pl.semaphore_wait(barrier, 34)

    def gather_out(k):
        return (send(normed[k].at[0], normed[k].at[1], r["ags"].at[k, 0], r["agr"].at[k, 0], right),
                send(normed[k].at[0], normed[k].at[2], r["ags"].at[k, 1], r["agr"].at[k, 1], left))

    def forward(k):
        lo, hi = pl.ds(0, 64), pl.ds(64, 64)
        return (send(normed[k].at[1, lo], normed[k].at[3, lo], r["fws"].at[k, 0], r["fwr"].at[k, 0], right),
                send(normed[k].at[2, hi], normed[k].at[3, hi], r["fws"].at[k, 1], r["fwr"].at[k, 1], left))

    def ffn(k, width, at, count, store):
        rows = count * 128
        values = normed[k][at:at + count].reshape(rows, width)
        for j in range(width // 256):
            cols = slice(256 * j, 256 * j + 256)
            hidden[0:rows, cols] = gelu(dot(values, vup[k][:, cols])).astype(bf)
        for j in range(width // 256):
            cols = slice(256 * j, 256 * j + 256)
            store(cols, dot(hidden[0:rows, 0:width], vdown[k][:, cols]))

    counter = iter(range(96))
    others = r["others"]

    def ring_send(ref, dev):
        i = next(counter)
        return send(ref, ref, r["gs"].at[i], r["gr"].at[i], dev)

    def slot_of(f, s):
        return jnp.where(swap, s, f), jnp.where(swap, f, s)

    def student_slot(f, s):
        i, j = slot_of(f, s)
        return [full[m].at[i, j, c] for m in range(3)]

    def beats_slot(f, s):
        i, j = slot_of(f, s)
        return others.at[c, i, j]

    up1, down1 = (first + 1) % 4, (first + 3) % 4
    up2, down2 = (second + 1) % 4, (second + 3) % 4
    up1_dev, down1_dev, up2_dev, down2_dev = at_first(up1), at_first(down1), at_second(up2), at_second(down2)

    gathers = {order[0]: gather_out(order[0])}
    stage = {}
    stage["s1"] = [ring_send(ref, dev) for ref in student_slot(first, second) for dev in (up1_dev, down1_dev)]
    finish_all(pieces)
    stage["py"] = [send(r["piece"].at[c], others.at[c, x, z, 3 - o], r["pys"].at[o - 1], r["pyr"].at[o - 1], at_y(y + o))
                   for o in (2, 1, 3)]
    ready[order[1]].wait()
    normed[order[1]][0] = layer_norm(hid[order[1]][...]).astype(bf)
    gathers[order[1]] = gather_out(order[1])
    hand = []
    for d in range(1, 32):
        to = (dp + d) % 32
        hand.append(send(r["outgoing"].at[to], r["incoming"].at[dp], r["hos"].at[d], r["hor"].at[d], {"dp": to}))
    ready[order[2]].wait()
    normed[order[2]][0] = layer_norm(hid[order[2]][...]).astype(bf)

    def student_first_forward():
        finish_all(stage["s1"])
        low, high = student_slot(down1, second), student_slot(up1, second)
        stage["s1f"] = [ring_send(low[2], up1_dev), ring_send(high[0], down1_dev), ring_send(high[1], down1_dev)]

    def student_second():
        finish_all(stage["s1f"])
        stage["s2"] = [ring_send(ref, dev) for i in range(4) for ref in student_slot(i, second)
                       for dev in (up2_dev, down2_dev)]

    def student_second_forward():
        finish_all(stage["s2"])
        stage["s2f"] = [ring_send(ref, up2_dev) for i in (0, 1) for ref in student_slot(i, down2)]
        stage["s2f"] += [ring_send(ref, down2_dev) for i in (2, 3) for ref in student_slot(i, up2)]

    def student_pair():
        finish_all(stage["s2f"])
        stage["s3"] = [ring_send(full[m].at[:, :, c], pair) for m in range(3)]

    def beats_first():
        finish_all(stage["py"])
        stage["b1"] = [ring_send(beats_slot(first, second), dev) for dev in (up1_dev, down1_dev)]

    def beats_first_forward():
        finish_all(stage["b1"])
        stage["b1f"] = [ring_send(beats_slot(down1, second).at[pl.ds(0, 2)], up1_dev),
                        ring_send(beats_slot(up1, second).at[pl.ds(2, 1)], down1_dev)]

    def beats_second():
        finish_all(stage["b1f"])
        stage["b2"] = [ring_send(beats_slot(i, second), dev) for i in range(4) for dev in (up2_dev, down2_dev)]
        stage["b3"] = [ring_send(beats_slot(i, second), pair) for i in range(4)]

    def beats_second_forward():
        finish_all(stage["b2"])
        stage["b2f"] = [ring_send(beats_slot(i, down2), up2_dev) for i in (0, 1)]
        stage["b2f"] += [ring_send(beats_slot(i, up2), down2_dev) for i in (2, 3)]
        stage["b3"] += [ring_send(beats_slot(i, s), pair) for s in (down2, up2) for i in range(4)]

    def beats_pair():
        finish_all(stage["b2f"])
        stage["b3"] += [ring_send(beats_slot(i, (second + 2) % 4), pair) for i in range(4)]
        finish_all(stage["b3"])

    def beats_rest():
        values = normed[1][0]
        for d in range(3):
            for j in range(WB // 256):
                cols = slice(256 * j, 256 * j + 256)
                hidden[0:128, cols] = gelu(dot(values, others[0, :, :, d, :, cols].reshape(WB, 256))).astype(bf)
            for j in range(WB // 256):
                cols = slice(256 * j, 256 * j + 256)
                keep[1][:, cols] += dot(hidden[0:128, 0:WB], others[1, :, :, d, :, cols].reshape(WB, 256))

    opposite, sides = {}, {}

    def send_sides(k):
        finish_all(opposite[k])
        sside[k][0, 0:64] = part[k][0, 0:64].astype(bf)
        sside[k][0, 64:128] = (part[k][0, 64:128] + ropp[k][1].astype(f32)).astype(bf)
        sside[k][1, 0:64] = (part[k][1, 0:64] + ropp[k][0].astype(f32)).astype(bf)
        sside[k][1, 64:128] = part[k][1, 64:128].astype(bf)
        sides[k] = (send(sside[k].at[1], rside[k].at[0], r["sds"].at[k, 0], r["sdr"].at[k, 0], right),
                    send(sside[k].at[0], rside[k].at[1], r["sds"].at[k, 1], r["sdr"].at[k, 1], left))

    def pair_send(i, src, dst):
        return send(src, dst, r["xs"].at[i], r["xr"].at[i], pair)

    def share_rows(i, values, h, mine, joined):
        mine[...] = values.T.reshape(4, 4, 2, h, 128)
        joined[:, :, :, 0:128] = mine[:, :, c]
        return pair_send(i, mine.at[:, :, 1 - c], joined.at[:, :, :, pl.ds(128, 128)])

    shared, passed = {}, {}
    widths = [width for _, width, _ in TEACHERS]

    def own_rows(n):
        k = order[n]
        finish_all(loads[k])

        def put(cols, v):
            keep[k][:, cols] = v
        ffn(k, widths[n], 0, 1, put)

    def side_rows(n):
        k = order[n]

        def put(cols, v):
            part[k][:, :, cols] = v.reshape(2, 128, 256)
        ffn(k, widths[n], 1, 2, put)

    def pass_on(n):
        finish_all(gathers[order[n]])
        passed[n] = forward(order[n])

    def far_rows(n):
        k = order[n]
        finish_all(passed[n])

        def put(cols, v):
            sopp[k][:, :, cols] = v.astype(bf).reshape(2, 64, 256)
        ffn(k, widths[n], 3, 1, put)
        opposite[k] = (send(sopp[k].at[0], ropp[k].at[0], r["ops"].at[k, 0], r["opr"].at[k, 0], right),
                       send(sopp[k].at[1], ropp[k].at[1], r["ops"].at[k, 1], r["opr"].at[k, 1], left))

    own_rows(0)
    student_first_forward()
    pass_on(0)
    own_rows(1)
    student_second()
    beats_first()
    side_rows(0)
    pass_on(1)
    side_rows(1)
    beats_first_forward()
    far_rows(0)
    student_second_forward()
    beats_second()
    finish_all(hand)
    student = dot(place, r["incoming"][...].reshape(256, 512).astype(bf)).astype(bf)
    r["student"][...] = student
    shared["in"] = share_rows(0, student, 16, r["tin"], r["lin"])
    own_rows(2)
    far_rows(1)
    send_sides(order[0])
    student_pair()
    send_sides(order[1])
    finish_all(stage["s3"])
    beats_second_forward()
    student = r["student"][...]
    pre_act = dot(student, full[0][...].reshape(512, 1536))
    shifted = pre_act - 4.0
    soft = jnp.maximum(shifted, 0.0) + jnp.log1p(jnp.exp(-jnp.abs(shifted)))
    activated = (soft - 0.08 * pre_act - 0.035).astype(bf)
    r["slope"][...] = jax.nn.sigmoid(shifted) - 0.08
    features = (student.astype(f32) + dot(activated, full[1][...].reshape(1536, 512))).astype(bf)
    shared["feat"] = share_rows(1, features, 16, r["tfeat"], r["lfeat"])
    shared["act"] = share_rows(2, activated, 48, r["tact"], r["lact"])
    for k, width, start in TEACHERS:
        r["predicted"][:, start:start + width] = dot(features, full[2][:, :, :, :, start:start + width].reshape(512, width))

    def error_of(n):
        k, width, start = TEACHERS[n]
        cols = slice(start, start + width)
        total = hid[k][...].astype(f32) + keep[k][...]
        if n < 2:
            finish_all(sides[k])
            total = total + rside[k][0].astype(f32) + rside[k][1].astype(f32)
        target = total.astype(bf).astype(f32)
        err = ((r["predicted"][:, cols] - target) * (2.0 / width) * mask).astype(bf)
        rerr[0:128, cols] = err
        cp = pair_send(3 + n, rerr.at[pl.ds(0, 128), pl.ds(start, width)], rerr.at[pl.ds(128, 128), pl.ds(start, width)])
        back = dot_t(err, full[2][:, :, :, :, cols].reshape(512, width))
        if n == 0:
            r["fgrad"][...] = back
        elif n == 1:
            r["fgrad"][...] += back
        else:
            back = r["fgrad"][...] + back
        return cp, back

    def block_rows(joined, a):
        tiles = [joined[jnp.where(swap, b, a), jnp.where(swap, a, b)] for b in range(4)]
        return jnp.concatenate(tiles, axis=0)

    def products(n, a, store):
        heads = block_rows(r["lfeat"], a) if n < 3 else None
        if n < 2:
            _, width, start = TEACHERS[n]
            store(GROUP_COLUMNS[n][0], dot(heads, rerr[:, start:start + width]).reshape(4, 16, width))
        elif n == 2:
            store(2304, dot(heads, rerr[:, WH:WH + WB]).reshape(4, 16, WB))
            outs = dot(block_rows(r["lact"], a), rfg[...]).reshape(4, 48, 512)
            for m in range(3):
                store(3072 + 512 * m, outs[:, 16 * m:16 * m + 16])
        else:
            store(4608, dot(block_rows(r["lin"], a), rpre[...]).reshape(4, 16, 1536))

    phase1, phase2 = {}, {}

    def start_group(n):
        start, width = GROUP_COLUMNS[n]
        cols = pl.ds(start, width)
        copies = []
        for d in (2, 1, 3):
            a = (first + d) % 4

            def put(at, v):
                r["send1"][d - 1, :, :, at:at + v.shape[2]] = v.astype(bf)
            products(n, a, put)
            copies.append(send(r["send1"].at[d - 1, :, :, cols], r["recv1"].at[d - 1, :, :, cols],
                               r["s1s"].at[n, d - 1], r["s1r"].at[n, d - 1], at_first(a)))

        def put_own(at, v):
            r["own1"][:, :, at:at + v.shape[2]] = v
        products(n, first, put_own)
        phase1[n] = copies

    def next_group(n):
        start, width = GROUP_COLUMNS[n]
        cols = slice(start, start + width)
        ref_cols = pl.ds(start, width)
        finish_all(phase1[n])

        def total1(b):
            v = r["own1"][b, :, cols]
            for i in range(3):
                v = v + r["recv1"][i, b, :, cols].astype(f32)
            return v
        copies = []
        for d in (2, 1, 3):
            b = (second + d) % 4
            r["send2"][d - 1, :, cols] = total1(b).astype(bf)
            copies.append(send(r["send2"].at[d - 1, :, ref_cols], r["recv2"].at[d - 1, :, ref_cols],
                               r["s2s"].at[n, d - 1], r["s2r"].at[n, d - 1], at_second(b)))
        r["own2"][:, cols] = total1(second)
        phase2[n] = copies

    cp, _ = error_of(0)
    finish_all([cp, shared["feat"]])
    start_group(0)
    beats_pair()
    beats_rest()
    cp, _ = error_of(1)
    cp.wait()
    start_group(1)
    finish_all([shared["in"], shared["act"]])
    next_group(0)
    cp, back = error_of(2)
    feat_grad = back.astype(bf)
    rfg[0:128] = feat_grad
    late = [cp, pair_send(6, rfg.at[pl.ds(0, 128)], rfg.at[pl.ds(128, 128)])]
    act_grad = dot_t(feat_grad, full[1][...].reshape(1536, 512))
    rpre[0:128] = (act_grad * r["slope"][...]).astype(bf)
    cp = pair_send(7, rpre.at[pl.ds(0, 128)], rpre.at[pl.ds(128, 128)])
    finish_all(late)
    start_group(2)
    cp.wait()
    start_group(3)

    summed = {}

    def send_sums(q):
        start, width = SUM_COLUMNS[q]
        cols, ref_cols = slice(start, start + width), pl.ds(start, width)
        total = r["own2"][:, cols]
        for i in range(3):
            total = total + r["recv2"][i, :, cols].astype(f32)
        sums[y, :, cols] = total.astype(bf)
        mine = sums.at[y, :, ref_cols]
        summed[q] = [send(mine, mine, r["s3s"].at[q, d - 1], r["s3r"].at[q, d - 1], at_y(y + d)) for d in (2, 1, 3)]

    next_group(1)
    finish_all(phase2[0])
    send_sums(0)
    next_group(2)
    finish_all(phase2[1])
    next_group(3)
    finish_all(phase2[2])
    send_sums(1)
    finish_all(phase2[3])
    send_sums(2)
    for q in range(3):
        finish_all(summed[q])


def sum_kernel(sums, grad_in, grad_out, grad_head):
    def sum_of(start, width):
        cols = slice(start, start + width)
        total = sums[0, :, cols].astype(jnp.float32)
        for t in range(1, 4):
            total = total + sums[t, :, cols].astype(jnp.float32)
        return total

    grad_head[:, WH + WB:] = sum_of(0, 1024)
    grad_head[:, 0:WH + WB] = sum_of(1024, 2048)
    for m in range(3):
        grad_out[16 * m:16 * m + 16] = sum_of(3072 + 512 * m, 512)
    grad_in[...] = sum_of(4608, 1536)


def body(
    hid_whisper, hid_beats, hid_wavlm,
    up_whisper, down_whisper, up_beats, down_beats, up_wavlm, down_wavlm,
    clip_len, send_counts, student_in, w_in, w_out, w_head,
):
    vm = pl.BlockSpec(memory_space=pltpu.VMEM)
    hbm = pl.BlockSpec(memory_space=pl.ANY)
    plan = scratch_plan()
    f32 = jnp.float32
    sums = pl.pallas_call(
        functools.partial(step_kernel, tuple(plan)),
        out_shape=jax.ShapeDtypeStruct((4, 16, SPAN), jnp.bfloat16),
        in_specs=[hbm] * 14 + [pl.BlockSpec(memory_space=pltpu.SMEM)],
        out_specs=vm,
        scratch_shapes=list(plan.values()),
        compiler_params=pltpu.CompilerParams(
            collective_id=0, has_side_effects=True, vmem_limit_bytes=62 * 1024 * 1024),
    )(
        hid_whisper, hid_beats, hid_wavlm,
        up_whisper, down_whisper, up_beats, down_beats, up_wavlm, down_wavlm,
        w_in, w_out, w_head, student_in, send_counts[0], clip_len,
    )
    return tuple(pl.pallas_call(
        sum_kernel,
        out_shape=[jax.ShapeDtypeStruct((16, 1536), f32), jax.ShapeDtypeStruct((48, 512), f32),
                   jax.ShapeDtypeStruct((16, 3072), f32)],
        in_specs=[vm],
        out_specs=[vm] * 3,
    )(sums))


def solution(mesh):
    in_specs = (
        P(("teacher", "dp"), None),
        P(("teacher", "dp"), None),
        P(("teacher", "dp"), None),
        P(None, "teacher"),
        P("teacher", None),
        P(None, "teacher"),
        P("teacher", None),
        P(None, "teacher"),
        P("teacher", None),
        P(("teacher", "dp")),
        P("teacher", None, None),
        P(("teacher", "dp"), None),
        P("dp", None),
        P("dp", None),
        P("dp", None),
    )
    out_specs = (P("dp", None), P("dp", None), P("dp", None))
    return jax.shard_map(body, mesh=mesh, in_specs=in_specs, out_specs=out_specs, check_vma=False)
```

```python
import functools

import jax
import jax.numpy as jnp
from jax import lax
from jax.experimental import pallas as pl
from jax.experimental.pallas import tpu as pltpu
from jax.sharding import PartitionSpec as P

WH = 1280
WB = 768
WL = 1024
EPS = 1e-05


def layer_norm(values):
    wide = values.astype(jnp.float32)
    center = wide - jnp.mean(wide, axis=-1, keepdims=True)
    spread = jnp.mean(center * center, axis=-1, keepdims=True)
    return center * lax.rsqrt(spread + EPS)


MESH_ID = pl.DeviceIdType.MESH
TEACHERS = ((2, WL, WH + WB), (0, WH, 0), (1, WB, WH))
SPAN = 6144
GROUP_COLUMNS = ((0, 1024), (1024, 1280), (2304, 2304), (4608, 1536))
SUM_COLUMNS = ((0, 1024), (1024, 3584), (4608, 1536))


def gelu(values):
    return 0.5 * values * (1.0 + lax.erf(values * 0.7071067811865476))


def dot(a, b):
    return jnp.dot(a, b, preferred_element_type=jnp.float32)


def dot_t(a, b):
    return lax.dot_general(a, b, (((1,), (1,)), ((), ())), preferred_element_type=jnp.float32)


def scratch_plan():
    bf, f32 = jnp.bfloat16, jnp.float32
    vm, dma = pltpu.VMEM, pltpu.SemaphoreType.DMA
    plan = {}
    for k, w in enumerate((WH, WB, WL)):
        plan[f"hid{k}"] = vm((128, w), bf)
        plan[f"vup{k}"] = vm((w, w), bf)
        plan[f"vdown{k}"] = vm((w, w), bf)
        plan[f"keep{k}"] = vm((128, w), f32)
        plan[f"normed{k}"] = vm((1 if k == 1 else 4, 128, w), bf)
    for k, w in ((0, WH), (2, WL)):
        plan[f"part{k}"] = vm((2, 128, w), f32)
        plan[f"sopp{k}"] = vm((2, 64, w), bf)
        plan[f"ropp{k}"] = vm((2, 64, w), bf)
        plan[f"sside{k}"] = vm((2, 128, w), bf)
        plan[f"rside{k}"] = vm((2, 128, w), bf)
    for m, (h, w) in enumerate(((16, 1536), (48, 512), (16, 3072))):
        plan[f"full{m}"] = vm((4, 4, 2, h, w), bf)
    plan.update(
        hidden=vm((256, WH), bf),
        outgoing=vm((32, 8, 512), HAND), incoming=vm((32, 8, 512), HAND),
        student=vm((128, 512), bf),
        slope=vm((128, 1536), f32), predicted=vm((128, 3072), f32), fgrad=vm((128, 512), f32),
        tin=vm((4, 4, 2, 16, 128), bf), tact=vm((4, 4, 2, 48, 128), bf), tfeat=vm((4, 4, 2, 16, 128), bf),
        lin=vm((4, 4, 16, 256), bf), lact=vm((4, 4, 48, 256), bf), lfeat=vm((4, 4, 16, 256), bf),
        rpre=vm((256, 1536), bf), rfg=vm((256, 512), bf), rerr=vm((256, 3072), bf),
        own1=vm((4, 16, SPAN), f32), send1=vm((3, 4, 16, SPAN), bf), recv1=vm((3, 4, 16, SPAN), bf),
        own2=vm((16, SPAN), f32), send2=vm((3, 16, SPAN), bf), recv2=vm((3, 16, SPAN), bf),
        rows_in=vm((128, 512), bf), counts=vm((32, 32), jnp.int32),
        wsem=dma((6,)), isem=dma((8,)),
        ags=dma((3, 2)), agr=dma((3, 2)), fws=dma((3, 2)), fwr=dma((3, 2)),
        ops=dma((3, 2)), opr=dma((3, 2)), sds=dma((3, 2)), sdr=dma((3, 2)),
        piece=vm((2, 48, WB), bf), others=vm((2, 4, 4, 3, 48, WB), bf),
        psem=dma((2,)), pys=dma((3,)), pyr=dma((3,)), gs=dma((96,)), gr=dma((96,)),
        hos=dma((32,)), hor=dma((32,)),
        xs=dma((8,)), xr=dma((8,)),
        s1s=dma((4, 3)), s1r=dma((4, 3)), s2s=dma((4, 3)), s2r=dma((4, 3)), s3s=dma((3, 3)), s3r=dma((3, 3)),
    )
    return plan


HAND = jnp.bfloat16


def step_kernel(names, *refs):
    ups, downs = refs[3:9:2], refs[4:9:2]
    shards = refs[9:12]
    clip_ref, sums = refs[14:16]
    r = dict(zip(names, refs[16:]))
    per = lambda name: [r.get(f"{name}{k}") for k in range(3)]
    hid = per("hid")
    vup, vdown, normed, keep, part = per("vup"), per("vdown"), per("normed"), per("keep"), per("part")
    sopp, ropp, sside, rside, full = per("sopp"), per("ropp"), per("sside"), per("rside"), per("full")
    hidden, rerr, rfg, rpre = r["hidden"], r["rerr"], r["rfg"], r["rpre"]
    bf, f32 = jnp.bfloat16, jnp.float32

    order = [k for k, _, _ in TEACHERS]
    y = lax.axis_index("teacher")
    dp = lax.axis_index("dp")
    c = dp % 2
    z = (dp // 2) % 4
    x = dp // 8
    swap = c == 1
    first = jnp.where(swap, z, x)
    second = jnp.where(swap, x, z)
    at_y = lambda t: {"teacher": t % 4}
    right, left = at_y(y + 1), at_y(y + 3)
    pair = {"dp": (x * 4 + z) * 2 + (1 - c)}

    def at_first(a):
        return {"dp": jnp.where(swap, (x * 4 + a) * 2 + 1, (a * 4 + z) * 2)}

    def at_second(b):
        return {"dp": jnp.where(swap, (b * 4 + z) * 2 + 1, (x * 4 + b) * 2)}

    def send(src, dst, ssem, rsem, dev):
        cp = pltpu.make_async_remote_copy(
            src_ref=src, dst_ref=dst, send_sem=ssem, recv_sem=rsem,
            device_id=dev, device_id_type=MESH_ID)
        cp.start()
        return cp

    def finish_all(copies):
        for cp in copies:
            cp.wait()

    ready = {}
    for i, (name, src, dst) in enumerate((
        (order[0], refs[order[0]], hid[order[0]]),
        ("counts", refs[13], r["counts"]),
        ("rows", refs[12], r["rows_in"]),
        ("in", shards[0], full[0].at[x, z, c]),
        ("out", shards[1], full[1].at[x, z, c]),
        ("head", shards[2], full[2].at[x, z, c]),
        (order[1], refs[order[1]], hid[order[1]]),
        (order[2], refs[order[2]], hid[order[2]]),
    )):
        ready[name] = pltpu.make_async_copy(src, dst, r["isem"].at[i])
        ready[name].start()
    piece_rows = pl.ds(pl.multiple_of((x * 4 + z) * 48, 48), 48)
    pieces = [pltpu.make_async_copy(src.at[piece_rows], r["piece"].at[i], r["psem"].at[i])
              for i, src in enumerate((ups[1], downs[1]))]
    for cp in pieces:
        cp.start()
    loads = {}
    for n, (k, _, _) in enumerate(TEACHERS):
        loads[k] = (pltpu.make_async_copy(ups[k], vup[k], r["wsem"].at[2 * n]),
                    pltpu.make_async_copy(downs[k], vdown[k], r["wsem"].at[2 * n + 1]))
        for cp in loads[k]:
            cp.start()

    barrier = pltpu.get_barrier_semaphore()
    for d in range(1, 4):
        pl.semaphore_signal(barrier, inc=1, device_id=at_y(y + d), device_id_type=MESH_ID)
    for d in range(1, 32):
        pl.semaphore_signal(barrier, inc=1, device_id={"dp": (dp + d) % 32}, device_id_type=MESH_ID)
    ready[order[0]].wait()
    normed[order[0]][0] = layer_norm(hid[order[0]][...]).astype(bf)

    ready["counts"].wait()
    counts = r["counts"][...].astype(f32)
    iota = lambda shape, axis: lax.broadcasted_iota(jnp.int32, shape, axis)
    src_at, own_at = iota((32, 32), 0), iota((32, 32), 1)
    one = lambda hit: jnp.where(hit, 1.0, 0.0)
    exact = lambda v: v.astype(bf)
    before_src = dot(exact(one(own_at < src_at)), exact(counts))
    before_own = dot(exact(counts), exact(one(src_at < own_at)))
    my_col, my_row = one(own_at == dp), one(src_at == dp)
    row_at, slot_at = iota((256, 32), 0), iota((256, 32), 1) * 8
    spread = exact(one((row_at >= slot_at) & (row_at < slot_at + 8)))
    wide_col = lambda v: dot(spread, exact(jnp.broadcast_to(jnp.sum(v * my_col, axis=1, keepdims=True), (32, 128))))
    slot = (iota((256, 128), 0) & 7).astype(f32)
    hit = (iota((256, 128), 1).astype(f32) == wide_col(before_src) + slot) & (slot < wide_col(counts))
    ready["rows"].wait()
    leaving = dot(exact(one(hit)), r["rows_in"][...])
    r["outgoing"][...] = leaving.reshape(32, 8, 512).astype(HAND)
    r["incoming"][dp] = r["outgoing"][dp]
    slot_at2, col_at = iota((32, 256), 0) * 8, iota((32, 256), 1)
    spread2 = exact(one((col_at >= slot_at2) & (col_at < slot_at2 + 8)))
    wide_row = lambda v: dot(exact(jnp.broadcast_to(jnp.sum(v * my_row, axis=0, keepdims=True), (128, 32))), spread2)
    slot2 = (iota((128, 256), 1) & 7).astype(f32)
    hit2 = (iota((128, 256), 0).astype(f32) == wide_row(before_own) + slot2) & (slot2 < wide_row(counts))
    place = exact(one(hit2))
    mask = one(iota((128, 1), 0) < clip_ref[0])

    finish_all([ready["in"], ready["out"], ready["head"]])
    pl.semaphore_wait(barrier, 34)

    def gather_out(k):
        return (send(normed[k].at[0], normed[k].at[1], r["ags"].at[k, 0], r["agr"].at[k, 0], right),
                send(normed[k].at[0], normed[k].at[2], r["ags"].at[k, 1], r["agr"].at[k, 1], left))

    def forward(k):
        lo, hi = pl.ds(0, 64), pl.ds(64, 64)
        return (send(normed[k].at[1, lo], normed[k].at[3, lo], r["fws"].at[k, 0], r["fwr"].at[k, 0], right),
                send(normed[k].at[2, hi], normed[k].at[3, hi], r["fws"].at[k, 1], r["fwr"].at[k, 1], left))

    def ffn(k, width, at, count, store):
        rows = count * 128
        values = normed[k][at:at + count].reshape(rows, width)
        for j in range(width // 256):
            cols = slice(256 * j, 256 * j + 256)
            hidden[0:rows, cols] = gelu(dot(values, vup[k][:, cols])).astype(bf)
        for j in range(width // 256):
            cols = slice(256 * j, 256 * j + 256)
            store(cols, dot(hidden[0:rows, 0:width], vdown[k][:, cols]))

    counter = iter(range(96))
    others = r["others"]

    def ring_send(ref, dev):
        i = next(counter)
        return send(ref, ref, r["gs"].at[i], r["gr"].at[i], dev)

    def slot_of(f, s):
        return jnp.where(swap, s, f), jnp.where(swap, f, s)

    def student_slot(f, s):
        i, j = slot_of(f, s)
        return [full[m].at[i, j, c] for m in range(3)]

    def beats_slot(f, s):
        i, j = slot_of(f, s)
        return others.at[c, i, j]

    up2, down2 = (second + 1) % 4, (second + 3) % 4
    up2_dev, down2_dev = at_second(up2), at_second(down2)
    row_devs = [at_first((first + d) % 4) for d in (2, 1, 3)]

    gathers = {order[0]: gather_out(order[0])}
    stage = {}
    stage["s1"] = [ring_send(ref, dev) for dev in row_devs for ref in student_slot(first, second)]
    finish_all(pieces)
    stage["py"] = [send(r["piece"].at[c], others.at[c, x, z, 3 - o], r["pys"].at[o - 1], r["pyr"].at[o - 1], at_y(y + o))
                   for o in (2, 1, 3)]
    ready[order[1]].wait()
    normed[order[1]][0] = layer_norm(hid[order[1]][...]).astype(bf)
    gathers[order[1]] = gather_out(order[1])
    hand = []
    for d in range(1, 32):
        to = (dp + d) % 32
        hand.append(send(r["outgoing"].at[to], r["incoming"].at[dp], r["hos"].at[d], r["hor"].at[d], {"dp": to}))
    ready[order[2]].wait()
    normed[order[2]][0] = layer_norm(hid[order[2]][...]).astype(bf)

    def spread_second(name, slots):
        stage[name + "a"], stage[name + "b"] = [], []
        for part, ups_first in ((name + "a", ((0, 2), (1, 3))), (name + "b", ((2, 0), (3, 1)))):
            for i, j in ups_first:
                stage[part] += [ring_send(ref, up2_dev) for ref in slots(i, second)]
                stage[part] += [ring_send(ref, down2_dev) for ref in slots(j, second)]

    def relay_second(name, slots):
        finish_all(stage[name + "a"])
        stage[name + "f"] = [ring_send(ref, up2_dev) for i in (0, 1) for ref in slots(i, down2)]
        stage[name + "f"] += [ring_send(ref, down2_dev) for i in (2, 3) for ref in slots(i, up2)]

    def student_second():
        finish_all(stage["s1"])
        spread_second("s2", student_slot)

    def student_pair():
        finish_all(stage["s2b"] + stage["s2f"])
        stage["s3"] = [ring_send(full[m].at[:, :, c], pair) for m in range(3)]

    def beats_slots(f, s):
        return [beats_slot(f, s)]

    def beats_first():
        finish_all(stage["py"])
        stage["b1"] = [ring_send(beats_slot(first, second), dev) for dev in row_devs]

    def beats_second():
        finish_all(stage["b1"])
        spread_second("b2", beats_slots)
        stage["b3"] = [ring_send(beats_slot(i, second), pair) for i in range(4)]

    def beats_share():
        finish_all(stage["b2b"])
        stage["b3"] += [ring_send(beats_slot(i, s), pair) for s in (down2, up2) for i in range(4)]

    def beats_pair():
        finish_all(stage["b2f"])
        stage["b3"] += [ring_send(beats_slot(i, (second + 2) % 4), pair) for i in range(4)]

    def beats_rest():
        values = normed[1][0]
        for d in range(3):
            for j in range(WB // 256):
                cols = slice(256 * j, 256 * j + 256)
                hidden[0:128, cols] = gelu(dot(values, others[0, :, :, d, :, cols].reshape(WB, 256))).astype(bf)
            for j in range(WB // 256):
                cols = slice(256 * j, 256 * j + 256)
                keep[1][:, cols] += dot(hidden[0:128, 0:WB], others[1, :, :, d, :, cols].reshape(WB, 256))

    opposite, sides = {}, {}

    def send_sides(k):
        finish_all(opposite[k])
        sside[k][0, 0:64] = part[k][0, 0:64].astype(bf)
        sside[k][0, 64:128] = (part[k][0, 64:128] + ropp[k][1].astype(f32)).astype(bf)
        sside[k][1, 0:64] = (part[k][1, 0:64] + ropp[k][0].astype(f32)).astype(bf)
        sside[k][1, 64:128] = part[k][1, 64:128].astype(bf)
        sides[k] = (send(sside[k].at[1], rside[k].at[0], r["sds"].at[k, 0], r["sdr"].at[k, 0], right),
                    send(sside[k].at[0], rside[k].at[1], r["sds"].at[k, 1], r["sdr"].at[k, 1], left))

    def pair_send(i, src, dst):
        return send(src, dst, r["xs"].at[i], r["xr"].at[i], pair)

    def share_rows(i, values, h, mine, joined):
        mine[...] = values.T.reshape(4, 4, 2, h, 128)
        joined[:, :, :, 0:128] = mine[:, :, c]
        return pair_send(i, mine.at[:, :, 1 - c], joined.at[:, :, :, pl.ds(128, 128)])

    shared, passed = {}, {}
    widths = [width for _, width, _ in TEACHERS]

    def own_rows(n):
        k = order[n]
        finish_all(loads[k])

        def put(cols, v):
            keep[k][:, cols] = v
        ffn(k, widths[n], 0, 1, put)

    def side_rows(n):
        k = order[n]

        def put(cols, v):
            part[k][:, :, cols] = v.reshape(2, 128, 256)
        ffn(k, widths[n], 1, 2, put)

    def pass_on(n):
        finish_all(gathers[order[n]])
        passed[n] = forward(order[n])

    def far_rows(n):
        k = order[n]
        finish_all(passed[n])

        def put(cols, v):
            sopp[k][:, :, cols] = v.astype(bf).reshape(2, 64, 256)
        ffn(k, widths[n], 3, 1, put)
        opposite[k] = (send(sopp[k].at[0], ropp[k].at[0], r["ops"].at[k, 0], r["opr"].at[k, 0], right),
                       send(sopp[k].at[1], ropp[k].at[1], r["ops"].at[k, 1], r["opr"].at[k, 1], left))

    own_rows(0)
    student_second()
    pass_on(0)
    own_rows(1)
    side_rows(0)
    own_rows(2)
    beats_first()
    pass_on(1)
    side_rows(1)
    relay_second("s2", student_slot)
    far_rows(0)
    beats_second()
    finish_all(hand)
    student = dot(place, r["incoming"][...].reshape(256, 512).astype(bf)).astype(bf)
    r["student"][...] = student
    shared["in"] = share_rows(0, student, 16, r["tin"], r["lin"])
    far_rows(1)
    send_sides(order[0])
    student_pair()
    relay_second("b2", beats_slots)
    send_sides(order[1])
    finish_all(stage["s3"])
    student = r["student"][...]
    pre_act = dot(student, full[0][...].reshape(512, 1536))
    shifted = pre_act - 4.0
    soft = jnp.maximum(shifted, 0.0) + jnp.log1p(jnp.exp(-jnp.abs(shifted)))
    activated = (soft - 0.08 * pre_act - 0.035).astype(bf)
    r["slope"][...] = jax.nn.sigmoid(shifted) - 0.08
    features = (student.astype(f32) + dot(activated, full[1][...].reshape(1536, 512))).astype(bf)
    shared["feat"] = share_rows(1, features, 16, r["tfeat"], r["lfeat"])
    shared["act"] = share_rows(2, activated, 48, r["tact"], r["lact"])
    beats_share()
    for k, width, start in TEACHERS:
        r["predicted"][:, start:start + width] = dot(features, full[2][:, :, :, :, start:start + width].reshape(512, width))

    def error_of(n):
        k, width, start = TEACHERS[n]
        cols = slice(start, start + width)
        total = hid[k][...].astype(f32) + keep[k][...]
        if n < 2:
            finish_all(sides[k])
            total = total + rside[k][0].astype(f32) + rside[k][1].astype(f32)
        target = total.astype(bf).astype(f32)
        err = ((r["predicted"][:, cols] - target) * (2.0 / width) * mask).astype(bf)
        rerr[0:128, cols] = err
        cp = pair_send(3 + n, rerr.at[pl.ds(0, 128), pl.ds(start, width)], rerr.at[pl.ds(128, 128), pl.ds(start, width)])
        back = dot_t(err, full[2][:, :, :, :, cols].reshape(512, width))
        if n == 0:
            r["fgrad"][...] = back
        elif n == 1:
            r["fgrad"][...] += back
        else:
            back = r["fgrad"][...] + back
        return cp, back

    def block_rows(joined, a):
        tiles = [joined[jnp.where(swap, b, a), jnp.where(swap, a, b)] for b in range(4)]
        return jnp.concatenate(tiles, axis=0)

    def products(n, a, store):
        heads = block_rows(r["lfeat"], a) if n < 3 else None
        if n < 2:
            _, width, start = TEACHERS[n]
            store(GROUP_COLUMNS[n][0], dot(heads, rerr[:, start:start + width]).reshape(4, 16, width))
        elif n == 2:
            store(2304, dot(heads, rerr[:, WH:WH + WB]).reshape(4, 16, WB))
            outs = dot(block_rows(r["lact"], a), rfg[...]).reshape(4, 48, 512)
            for m in range(3):
                store(3072 + 512 * m, outs[:, 16 * m:16 * m + 16])
        else:
            store(4608, dot(block_rows(r["lin"], a), rpre[...]).reshape(4, 16, 1536))

    phase1, phase2 = {}, {}

    def start_group(n):
        start, width = GROUP_COLUMNS[n]
        cols = pl.ds(start, width)
        copies = []
        for d in (2, 1, 3):
            a = (first + d) % 4

            def put(at, v):
                r["send1"][d - 1, :, :, at:at + v.shape[2]] = v.astype(bf)
            products(n, a, put)
            copies.append(send(r["send1"].at[d - 1, :, :, cols], r["recv1"].at[d - 1, :, :, cols],
                               r["s1s"].at[n, d - 1], r["s1r"].at[n, d - 1], at_first(a)))

        def put_own(at, v):
            r["own1"][:, :, at:at + v.shape[2]] = v
        products(n, first, put_own)
        phase1[n] = copies

    def next_group(n):
        start, width = GROUP_COLUMNS[n]
        cols = slice(start, start + width)
        ref_cols = pl.ds(start, width)
        finish_all(phase1[n])

        def total1(b):
            v = r["own1"][b, :, cols]
            for i in range(3):
                v = v + r["recv1"][i, b, :, cols].astype(f32)
            return v
        copies = []
        for d in (2, 1, 3):
            b = (second + d) % 4
            r["send2"][d - 1, :, cols] = total1(b).astype(bf)
            copies.append(send(r["send2"].at[d - 1, :, ref_cols], r["recv2"].at[d - 1, :, ref_cols],
                               r["s2s"].at[n, d - 1], r["s2r"].at[n, d - 1], at_second(b)))
        r["own2"][:, cols] = total1(second)
        phase2[n] = copies

    cp, _ = error_of(0)
    finish_all([cp, shared["feat"]])
    start_group(0)
    beats_pair()
    cp, _ = error_of(1)
    finish_all([shared["in"], shared["act"]])
    next_group(0)
    cp.wait()
    start_group(1)
    finish_all(stage["b3"])
    beats_rest()
    cp, back = error_of(2)
    feat_grad = back.astype(bf)
    rfg[0:128] = feat_grad
    late = [cp, pair_send(6, rfg.at[pl.ds(0, 128)], rfg.at[pl.ds(128, 128)])]
    act_grad = dot_t(feat_grad, full[1][...].reshape(1536, 512))
    rpre[0:128] = (act_grad * r["slope"][...]).astype(bf)
    cp = pair_send(7, rpre.at[pl.ds(0, 128)], rpre.at[pl.ds(128, 128)])
    finish_all(late)
    start_group(2)
    cp.wait()
    start_group(3)

    summed = {}

    def send_sums(q):
        start, width = SUM_COLUMNS[q]
        cols, ref_cols = slice(start, start + width), pl.ds(start, width)
        total = r["own2"][:, cols]
        for i in range(3):
            total = total + r["recv2"][i, :, cols].astype(f32)
        sums[y, :, cols] = total.astype(bf)
        mine = sums.at[y, :, ref_cols]
        summed[q] = [send(mine, mine, r["s3s"].at[q, d - 1], r["s3r"].at[q, d - 1], at_y(y + d)) for d in (2, 1, 3)]

    next_group(1)
    finish_all(phase2[0])
    send_sums(0)
    next_group(2)
    finish_all(phase2[1])
    next_group(3)
    finish_all(phase2[2])
    send_sums(1)
    finish_all(phase2[3])
    send_sums(2)
    for q in range(3):
        finish_all(summed[q])


def sum_kernel(sums, grad_in, grad_out, grad_head):
    def sum_of(start, width):
        cols = slice(start, start + width)
        total = sums[0, :, cols].astype(jnp.float32)
        for t in range(1, 4):
            total = total + sums[t, :, cols].astype(jnp.float32)
        return total

    grad_head[:, WH + WB:] = sum_of(0, 1024)
    grad_head[:, 0:WH + WB] = sum_of(1024, 2048)
    for m in range(3):
        grad_out[16 * m:16 * m + 16] = sum_of(3072 + 512 * m, 512)
    grad_in[...] = sum_of(4608, 1536)


def body(
    hid_whisper, hid_beats, hid_wavlm,
    up_whisper, down_whisper, up_beats, down_beats, up_wavlm, down_wavlm,
    clip_len, send_counts, student_in, w_in, w_out, w_head,
):
    vm = pl.BlockSpec(memory_space=pltpu.VMEM)
    hbm = pl.BlockSpec(memory_space=pl.ANY)
    plan = scratch_plan()
    f32 = jnp.float32
    sums = pl.pallas_call(
        functools.partial(step_kernel, tuple(plan)),
        out_shape=jax.ShapeDtypeStruct((4, 16, SPAN), jnp.bfloat16),
        in_specs=[hbm] * 14 + [pl.BlockSpec(memory_space=pltpu.SMEM)],
        out_specs=vm,
        scratch_shapes=list(plan.values()),
        compiler_params=pltpu.CompilerParams(
            collective_id=0, has_side_effects=True, vmem_limit_bytes=62 * 1024 * 1024),
    )(
        hid_whisper, hid_beats, hid_wavlm,
        up_whisper, down_whisper, up_beats, down_beats, up_wavlm, down_wavlm,
        w_in, w_out, w_head, student_in, send_counts[0], clip_len,
    )
    return tuple(pl.pallas_call(
        sum_kernel,
        out_shape=[jax.ShapeDtypeStruct((16, 1536), f32), jax.ShapeDtypeStruct((48, 512), f32),
                   jax.ShapeDtypeStruct((16, 3072), f32)],
        in_specs=[vm],
        out_specs=[vm] * 3,
    )(sums))


def solution(mesh):
    in_specs = (
        P(("teacher", "dp"), None),
        P(("teacher", "dp"), None),
        P(("teacher", "dp"), None),
        P(None, "teacher"),
        P("teacher", None),
        P(None, "teacher"),
        P("teacher", None),
        P(None, "teacher"),
        P("teacher", None),
        P(("teacher", "dp")),
        P("teacher", None, None),
        P(("teacher", "dp"), None),
        P("dp", None),
        P("dp", None),
        P("dp", None),
    )
    out_specs = (P("dp", None), P("dp", None), P("dp", None))
    return jax.shard_map(body, mesh=mesh, in_specs=in_specs, out_specs=out_specs, check_vma=False)
```

```python
import functools

import jax
import jax.numpy as jnp
from jax import lax
from jax.experimental import pallas as pl
from jax.experimental.pallas import tpu as pltpu
from jax.sharding import PartitionSpec as P

WH = 1280
WB = 768
WL = 1024
EPS = 1e-05


def layer_norm(values):
    wide = values.astype(jnp.float32)
    center = wide - jnp.mean(wide, axis=-1, keepdims=True)
    spread = jnp.mean(center * center, axis=-1, keepdims=True)
    return center * lax.rsqrt(spread + EPS)


MESH_ID = pl.DeviceIdType.MESH
TEACHERS = ((2, WL, WH + WB), (0, WH, 0), (1, WB, WH))
SPAN = 6144
GROUP_COLUMNS = ((0, 1024), (1024, 1280), (2304, 2304), (4608, 1536))


def gelu(values):
    return 0.5 * values * (1.0 + lax.erf(values * 0.7071067811865476))


def dot(a, b):
    return jnp.dot(a, b, preferred_element_type=jnp.float32)


def dot_t(a, b):
    return lax.dot_general(a, b, (((1,), (1,)), ((), ())), preferred_element_type=jnp.float32)


def scratch_plan():
    bf, f32 = jnp.bfloat16, jnp.float32
    vm, dma = pltpu.VMEM, pltpu.SemaphoreType.DMA
    plan = {}
    for k, w in enumerate((WH, WB, WL)):
        plan[f"hid{k}"] = vm((128, w), bf)
        plan[f"vup{k}"] = vm((w, w), bf)
        plan[f"vdown{k}"] = vm((w, w), bf)
        plan[f"keep{k}"] = vm((128, w), f32)
        plan[f"normed{k}"] = vm((1 if k == 1 else 4, 128, w), bf)
    for k, w in ((0, WH), (2, WL)):
        plan[f"part{k}"] = vm((2, 128, w), f32)
        plan[f"sopp{k}"] = vm((2, 64, w), bf)
        plan[f"ropp{k}"] = vm((2, 64, w), bf)
        plan[f"sside{k}"] = vm((2, 128, w), bf)
        plan[f"rside{k}"] = vm((2, 128, w), bf)
    for m, (h, w) in enumerate(((16, 1536), (48, 512), (16, 3072))):
        plan[f"full{m}"] = vm((4, 4, 2, h, w), bf)
    plan.update(
        hidden=vm((256, WH), bf),
        outgoing=vm((32, 8, 512), HAND), incoming=vm((32, 8, 512), HAND),
        student=vm((128, 512), bf),
        slope=vm((128, 1536), f32), predicted=vm((128, 3072), f32), fgrad=vm((128, 512), f32),
        tin=vm((4, 4, 2, 16, 128), bf), tact=vm((4, 4, 2, 48, 128), bf), tfeat=vm((4, 4, 2, 16, 128), bf),
        lin=vm((4, 4, 16, 256), bf), lact=vm((4, 4, 48, 256), bf), lfeat=vm((4, 4, 16, 256), bf),
        rpre=vm((256, 1536), bf), rfg=vm((256, 512), bf), rerr=vm((256, 3072), bf),
        own1=vm((4, 16, SPAN), f32), send1=vm((3, 4, 16, SPAN), bf), recv1=vm((3, 4, 16, SPAN), bf),
        own2=vm((16, SPAN), f32), send2=vm((3, 16, SPAN), bf), recv2=vm((3, 16, SPAN), bf),
        rows_in=vm((128, 512), bf), counts=vm((32, 32), jnp.int32),
        wsem=dma((6,)), isem=dma((8,)),
        ags=dma((3, 2)), agr=dma((3, 2)), fws=dma((3, 2)), fwr=dma((3, 2)),
        ops=dma((3, 2)), opr=dma((3, 2)), sds=dma((3, 2)), sdr=dma((3, 2)),
        piece=vm((2, 48, WB), bf), others=vm((2, 4, 4, 3, 48, WB), bf),
        psem=dma((2,)), pys=dma((3,)), pyr=dma((3,)), gs=dma((96,)), gr=dma((96,)),
        hos=dma((32,)), hor=dma((32,)),
        xs=dma((8,)), xr=dma((8,)),
        s1s=dma((4, 3)), s1r=dma((4, 3)), s2s=dma((4, 3)), s2r=dma((4, 3)), s3s=dma((4, 3)), s3r=dma((4, 3)),
    )
    return plan


HAND = jnp.bfloat16


def step_kernel(names, *refs):
    ups, downs = refs[3:9:2], refs[4:9:2]
    shards = refs[9:12]
    clip_ref, sums = refs[14:16]
    r = dict(zip(names, refs[16:]))
    per = lambda name: [r.get(f"{name}{k}") for k in range(3)]
    hid = per("hid")
    vup, vdown, normed, keep, part = per("vup"), per("vdown"), per("normed"), per("keep"), per("part")
    sopp, ropp, sside, rside, full = per("sopp"), per("ropp"), per("sside"), per("rside"), per("full")
    hidden, rerr, rfg, rpre = r["hidden"], r["rerr"], r["rfg"], r["rpre"]
    bf, f32 = jnp.bfloat16, jnp.float32

    order = [k for k, _, _ in TEACHERS]
    y = lax.axis_index("teacher")
    dp = lax.axis_index("dp")
    c = dp % 2
    z = (dp // 2) % 4
    x = dp // 8
    swap = c == 1
    first = jnp.where(swap, z, x)
    second = jnp.where(swap, x, z)
    at_y = lambda t: {"teacher": t % 4}
    right, left = at_y(y + 1), at_y(y + 3)
    pair = {"dp": (x * 4 + z) * 2 + (1 - c)}

    def at_first(a):
        return {"dp": jnp.where(swap, (x * 4 + a) * 2 + 1, (a * 4 + z) * 2)}

    def at_second(b):
        return {"dp": jnp.where(swap, (b * 4 + z) * 2 + 1, (x * 4 + b) * 2)}

    def send(src, dst, ssem, rsem, dev):
        cp = pltpu.make_async_remote_copy(
            src_ref=src, dst_ref=dst, send_sem=ssem, recv_sem=rsem,
            device_id=dev, device_id_type=MESH_ID)
        cp.start()
        return cp

    def finish_all(copies):
        for cp in copies:
            cp.wait()

    ready = {}
    for i, (name, src, dst) in enumerate((
        (order[0], refs[order[0]], hid[order[0]]),
        ("counts", refs[13], r["counts"]),
        ("rows", refs[12], r["rows_in"]),
        ("in", shards[0], full[0].at[x, z, c]),
        ("out", shards[1], full[1].at[x, z, c]),
        ("head", shards[2], full[2].at[x, z, c]),
        (order[1], refs[order[1]], hid[order[1]]),
        (order[2], refs[order[2]], hid[order[2]]),
    )):
        ready[name] = pltpu.make_async_copy(src, dst, r["isem"].at[i])
        ready[name].start()
    piece_rows = pl.ds(pl.multiple_of((x * 4 + z) * 48, 48), 48)
    pieces = [pltpu.make_async_copy(src.at[piece_rows], r["piece"].at[i], r["psem"].at[i])
              for i, src in enumerate((ups[1], downs[1]))]
    for cp in pieces:
        cp.start()
    loads = {}
    for n, (k, _, _) in enumerate(TEACHERS):
        loads[k] = (pltpu.make_async_copy(ups[k], vup[k], r["wsem"].at[2 * n]),
                    pltpu.make_async_copy(downs[k], vdown[k], r["wsem"].at[2 * n + 1]))
        for cp in loads[k]:
            cp.start()

    barrier = pltpu.get_barrier_semaphore()
    for d in range(1, 4):
        pl.semaphore_signal(barrier, inc=1, device_id=at_y(y + d), device_id_type=MESH_ID)
    for d in range(1, 32):
        pl.semaphore_signal(barrier, inc=1, device_id={"dp": (dp + d) % 32}, device_id_type=MESH_ID)
    ready[order[0]].wait()
    normed[order[0]][0] = layer_norm(hid[order[0]][...]).astype(bf)

    ready["counts"].wait()
    counts = r["counts"][...].astype(f32)
    iota = lambda shape, axis: lax.broadcasted_iota(jnp.int32, shape, axis)
    src_at, own_at = iota((32, 32), 0), iota((32, 32), 1)
    one = lambda hit: jnp.where(hit, 1.0, 0.0)
    exact = lambda v: v.astype(bf)
    before_src = dot(exact(one(own_at < src_at)), exact(counts))
    before_own = dot(exact(counts), exact(one(src_at < own_at)))
    my_col, my_row = one(own_at == dp), one(src_at == dp)
    row_at, slot_at = iota((256, 32), 0), iota((256, 32), 1) * 8
    spread = exact(one((row_at >= slot_at) & (row_at < slot_at + 8)))
    wide_col = lambda v: dot(spread, exact(jnp.broadcast_to(jnp.sum(v * my_col, axis=1, keepdims=True), (32, 128))))
    slot = (iota((256, 128), 0) & 7).astype(f32)
    hit = (iota((256, 128), 1).astype(f32) == wide_col(before_src) + slot) & (slot < wide_col(counts))
    ready["rows"].wait()
    leaving = dot(exact(one(hit)), r["rows_in"][...])
    r["outgoing"][...] = leaving.reshape(32, 8, 512).astype(HAND)
    r["incoming"][dp] = r["outgoing"][dp]
    slot_at2, col_at = iota((32, 256), 0) * 8, iota((32, 256), 1)
    spread2 = exact(one((col_at >= slot_at2) & (col_at < slot_at2 + 8)))
    wide_row = lambda v: dot(exact(jnp.broadcast_to(jnp.sum(v * my_row, axis=0, keepdims=True), (128, 32))), spread2)
    slot2 = (iota((128, 256), 1) & 7).astype(f32)
    hit2 = (iota((128, 256), 0).astype(f32) == wide_row(before_own) + slot2) & (slot2 < wide_row(counts))
    place = exact(one(hit2))
    mask = one(iota((128, 1), 0) < clip_ref[0])

    finish_all([ready["in"], ready["out"], ready["head"]])
    pl.semaphore_wait(barrier, 34)

    def gather_out(k):
        return (send(normed[k].at[0], normed[k].at[1], r["ags"].at[k, 0], r["agr"].at[k, 0], right),
                send(normed[k].at[0], normed[k].at[2], r["ags"].at[k, 1], r["agr"].at[k, 1], left))

    def forward(k):
        lo, hi = pl.ds(0, 64), pl.ds(64, 64)
        return (send(normed[k].at[1, lo], normed[k].at[3, lo], r["fws"].at[k, 0], r["fwr"].at[k, 0], right),
                send(normed[k].at[2, hi], normed[k].at[3, hi], r["fws"].at[k, 1], r["fwr"].at[k, 1], left))

    def ffn(k, width, at, count, store):
        rows = count * 128
        values = normed[k][at:at + count].reshape(rows, width)
        for j in range(width // 256):
            cols = slice(256 * j, 256 * j + 256)
            hidden[0:rows, cols] = gelu(dot(values, vup[k][:, cols])).astype(bf)
        for j in range(width // 256):
            cols = slice(256 * j, 256 * j + 256)
            store(cols, dot(hidden[0:rows, 0:width], vdown[k][:, cols]))

    counter = iter(range(96))
    others = r["others"]

    def ring_send(ref, dev):
        i = next(counter)
        return send(ref, ref, r["gs"].at[i], r["gr"].at[i], dev)

    def slot_of(f, s):
        return jnp.where(swap, s, f), jnp.where(swap, f, s)

    def student_slot(f, s):
        i, j = slot_of(f, s)
        return [full[m].at[i, j, c] for m in range(3)]

    def beats_slot(f, s):
        i, j = slot_of(f, s)
        return others.at[c, i, j]

    up2, down2 = (second + 1) % 4, (second + 3) % 4
    up2_dev, down2_dev = at_second(up2), at_second(down2)
    row_devs = [at_first((first + d) % 4) for d in (2, 1, 3)]

    gathers = {order[0]: gather_out(order[0])}
    stage = {}
    stage["s1"] = [ring_send(ref, dev) for dev in row_devs for ref in student_slot(first, second)]
    finish_all(pieces)
    stage["py"] = [send(r["piece"].at[c], others.at[c, x, z, 3 - o], r["pys"].at[o - 1], r["pyr"].at[o - 1], at_y(y + o))
                   for o in (2, 1, 3)]
    ready[order[1]].wait()
    normed[order[1]][0] = layer_norm(hid[order[1]][...]).astype(bf)
    gathers[order[1]] = gather_out(order[1])
    hand = []
    for d in range(1, 32):
        to = (dp + d) % 32
        hand.append(send(r["outgoing"].at[to], r["incoming"].at[dp], r["hos"].at[d], r["hor"].at[d], {"dp": to}))
    ready[order[2]].wait()
    normed[order[2]][0] = layer_norm(hid[order[2]][...]).astype(bf)

    def spread_second(name, slots):
        stage[name + "a"], stage[name + "b"] = [], []
        for part, ups_first in ((name + "a", ((0, 2), (1, 3))), (name + "b", ((2, 0), (3, 1)))):
            for i, j in ups_first:
                stage[part] += [ring_send(ref, up2_dev) for ref in slots(i, second)]
                stage[part] += [ring_send(ref, down2_dev) for ref in slots(j, second)]

    def relay_second(name, slots):
        finish_all(stage[name + "a"])
        stage[name + "f"] = [ring_send(ref, up2_dev) for i in (0, 1) for ref in slots(i, down2)]
        stage[name + "f"] += [ring_send(ref, down2_dev) for i in (2, 3) for ref in slots(i, up2)]

    def student_second():
        finish_all(stage["s1"])
        spread_second("s2", student_slot)

    def student_pair():
        finish_all(stage["s2b"] + stage["s2f"])
        stage["s3"] = [ring_send(full[m].at[:, :, c], pair) for m in range(3)]

    def beats_slots(f, s):
        return [beats_slot(f, s)]

    def beats_first():
        finish_all(stage["py"])
        stage["b1"] = [ring_send(beats_slot(first, second), dev) for dev in row_devs]

    def beats_second():
        finish_all(stage["b1"])
        spread_second("b2", beats_slots)
        stage["b3"] = [ring_send(beats_slot(i, second), pair) for i in range(4)]

    def beats_share():
        finish_all(stage["b2b"])
        stage["b3"] += [ring_send(beats_slot(i, s), pair) for s in (down2, up2) for i in range(4)]

    def beats_pair():
        finish_all(stage["b2f"])
        stage["b3"] += [ring_send(beats_slot(i, (second + 2) % 4), pair) for i in range(4)]

    def beats_rest():
        values = normed[1][0]
        for d in range(3):
            for j in range(WB // 256):
                cols = slice(256 * j, 256 * j + 256)
                hidden[0:128, cols] = gelu(dot(values, others[0, :, :, d, :, cols].reshape(WB, 256))).astype(bf)
            for j in range(WB // 256):
                cols = slice(256 * j, 256 * j + 256)
                keep[1][:, cols] += dot(hidden[0:128, 0:WB], others[1, :, :, d, :, cols].reshape(WB, 256))

    opposite, sides = {}, {}

    def send_sides(k):
        finish_all(opposite[k])
        sside[k][0, 0:64] = part[k][0, 0:64].astype(bf)
        sside[k][0, 64:128] = (part[k][0, 64:128] + ropp[k][1].astype(f32)).astype(bf)
        sside[k][1, 0:64] = (part[k][1, 0:64] + ropp[k][0].astype(f32)).astype(bf)
        sside[k][1, 64:128] = part[k][1, 64:128].astype(bf)
        sides[k] = (send(sside[k].at[1], rside[k].at[0], r["sds"].at[k, 0], r["sdr"].at[k, 0], right),
                    send(sside[k].at[0], rside[k].at[1], r["sds"].at[k, 1], r["sdr"].at[k, 1], left))

    def pair_send(i, src, dst):
        return send(src, dst, r["xs"].at[i], r["xr"].at[i], pair)

    def share_rows(i, values, h, mine, joined):
        mine[...] = values.T.reshape(4, 4, 2, h, 128)
        joined[:, :, :, 0:128] = mine[:, :, c]
        return pair_send(i, mine.at[:, :, 1 - c], joined.at[:, :, :, pl.ds(128, 128)])

    shared, passed = {}, {}
    widths = [width for _, width, _ in TEACHERS]

    def own_rows(n):
        k = order[n]
        finish_all(loads[k])

        def put(cols, v):
            keep[k][:, cols] = v
        ffn(k, widths[n], 0, 1, put)

    def side_rows(n):
        k = order[n]

        def put(cols, v):
            part[k][:, :, cols] = v.reshape(2, 128, 256)
        ffn(k, widths[n], 1, 2, put)

    def pass_on(n):
        finish_all(gathers[order[n]])
        passed[n] = forward(order[n])

    def far_rows(n):
        k = order[n]
        finish_all(passed[n])

        def put(cols, v):
            sopp[k][:, :, cols] = v.astype(bf).reshape(2, 64, 256)
        ffn(k, widths[n], 3, 1, put)
        opposite[k] = (send(sopp[k].at[0], ropp[k].at[0], r["ops"].at[k, 0], r["opr"].at[k, 0], right),
                       send(sopp[k].at[1], ropp[k].at[1], r["ops"].at[k, 1], r["opr"].at[k, 1], left))

    own_rows(0)
    student_second()
    pass_on(0)
    own_rows(1)
    side_rows(0)
    own_rows(2)
    relay_second("s2", student_slot)
    beats_first()
    pass_on(1)
    side_rows(1)
    far_rows(0)
    student_pair()
    finish_all(hand)
    student = dot(place, r["incoming"][...].reshape(256, 512).astype(bf)).astype(bf)
    r["student"][...] = student
    shared["in"] = share_rows(0, student, 16, r["tin"], r["lin"])
    far_rows(1)
    send_sides(order[0])
    beats_second()
    finish_all(stage["s3"])
    student = r["student"][...]
    pre_act = dot(student, full[0][...].reshape(512, 1536))
    shifted = pre_act - 4.0
    soft = jnp.maximum(shifted, 0.0) + jnp.log1p(jnp.exp(-jnp.abs(shifted)))
    activated = (soft - 0.08 * pre_act - 0.035).astype(bf)
    r["slope"][...] = jax.nn.sigmoid(shifted) - 0.08
    features = (student.astype(f32) + dot(activated, full[1][...].reshape(1536, 512))).astype(bf)
    send_sides(order[1])
    shared["feat"] = share_rows(1, features, 16, r["tfeat"], r["lfeat"])
    shared["act"] = share_rows(2, activated, 48, r["tact"], r["lact"])
    relay_second("b2", beats_slots)
    for k, width, start in TEACHERS:
        r["predicted"][:, start:start + width] = dot(features, full[2][:, :, :, :, start:start + width].reshape(512, width))

    def error_of(n):
        k, width, start = TEACHERS[n]
        cols = slice(start, start + width)
        total = hid[k][...].astype(f32) + keep[k][...]
        if n < 2:
            finish_all(sides[k])
            total = total + rside[k][0].astype(f32) + rside[k][1].astype(f32)
        target = total.astype(bf).astype(f32)
        err = ((r["predicted"][:, cols] - target) * (2.0 / width) * mask).astype(bf)
        rerr[0:128, cols] = err
        cp = pair_send(3 + n, rerr.at[pl.ds(0, 128), pl.ds(start, width)], rerr.at[pl.ds(128, 128), pl.ds(start, width)])
        back = dot_t(err, full[2][:, :, :, :, cols].reshape(512, width))
        if n == 0:
            r["fgrad"][...] = back
        elif n == 1:
            r["fgrad"][...] += back
        else:
            back = r["fgrad"][...] + back
        return cp, back

    def block_rows(joined, a):
        tiles = [joined[jnp.where(swap, b, a), jnp.where(swap, a, b)] for b in range(4)]
        return jnp.concatenate(tiles, axis=0)

    def products(n, a, store):
        heads = block_rows(r["lfeat"], a) if n < 3 else None
        if n < 2:
            _, width, start = TEACHERS[n]
            store(GROUP_COLUMNS[n][0], dot(heads, rerr[:, start:start + width]).reshape(4, 16, width))
        elif n == 2:
            store(2304, dot(heads, rerr[:, WH:WH + WB]).reshape(4, 16, WB))
            outs = dot(block_rows(r["lact"], a), rfg[...]).reshape(4, 48, 512)
            for m in range(3):
                store(3072 + 512 * m, outs[:, 16 * m:16 * m + 16])
        else:
            store(4608, dot(block_rows(r["lin"], a), rpre[...]).reshape(4, 16, 1536))

    phase1, phase2 = {}, {}

    def start_group(n):
        start, width = GROUP_COLUMNS[n]
        cols = pl.ds(start, width)
        copies = []
        for d in (2, 1, 3):
            a = (first + d) % 4

            def put(at, v):
                r["send1"][d - 1, :, :, at:at + v.shape[2]] = v.astype(bf)
            products(n, a, put)
            copies.append(send(r["send1"].at[d - 1, :, :, cols], r["recv1"].at[d - 1, :, :, cols],
                               r["s1s"].at[n, d - 1], r["s1r"].at[n, d - 1], at_first(a)))

        def put_own(at, v):
            r["own1"][:, :, at:at + v.shape[2]] = v
        products(n, first, put_own)
        phase1[n] = copies

    def next_group(n):
        start, width = GROUP_COLUMNS[n]
        cols = slice(start, start + width)
        ref_cols = pl.ds(start, width)
        finish_all(phase1[n])

        def total1(b):
            v = r["own1"][b, :, cols]
            for i in range(3):
                v = v + r["recv1"][i, b, :, cols].astype(f32)
            return v
        copies = []
        for d in (2, 1, 3):
            b = (second + d) % 4
            r["send2"][d - 1, :, cols] = total1(b).astype(bf)
            copies.append(send(r["send2"].at[d - 1, :, ref_cols], r["recv2"].at[d - 1, :, ref_cols],
                               r["s2s"].at[n, d - 1], r["s2r"].at[n, d - 1], at_second(b)))
        r["own2"][:, cols] = total1(second)
        phase2[n] = copies

    cp, _ = error_of(0)
    beats_share()
    finish_all([cp, shared["feat"]])
    start_group(0)
    beats_pair()
    cp, _ = error_of(1)
    finish_all([shared["in"], shared["act"]])
    next_group(0)
    cp.wait()
    start_group(1)
    finish_all(stage["b3"])
    beats_rest()
    cp, back = error_of(2)
    feat_grad = back.astype(bf)
    rfg[0:128] = feat_grad
    late = [cp, pair_send(6, rfg.at[pl.ds(0, 128)], rfg.at[pl.ds(128, 128)])]
    act_grad = dot_t(feat_grad, full[1][...].reshape(1536, 512))
    rpre[0:128] = (act_grad * r["slope"][...]).astype(bf)
    cp = pair_send(7, rpre.at[pl.ds(0, 128)], rpre.at[pl.ds(128, 128)])
    next_group(1)
    finish_all(late)
    start_group(2)
    cp.wait()
    start_group(3)

    summed = {}

    def send_sums(q):
        start, width = GROUP_COLUMNS[q]
        cols, ref_cols = slice(start, start + width), pl.ds(start, width)
        total = r["own2"][:, cols]
        for i in range(3):
            total = total + r["recv2"][i, :, cols].astype(f32)
        sums[y, :, cols] = total.astype(bf)
        mine = sums.at[y, :, ref_cols]
        summed[q] = [send(mine, mine, r["s3s"].at[q, d - 1], r["s3r"].at[q, d - 1], at_y(y + d)) for d in (2, 1, 3)]

    finish_all(phase2[0])
    send_sums(0)
    finish_all(phase2[1])
    send_sums(1)
    next_group(2)
    next_group(3)
    finish_all(phase2[2])
    send_sums(2)
    finish_all(phase2[3])
    send_sums(3)
    for q in range(4):
        finish_all(summed[q])


def sum_kernel(sums, grad_in, grad_out, grad_head):
    def sum_of(start, width):
        cols = slice(start, start + width)
        total = sums[0, :, cols].astype(jnp.float32)
        for t in range(1, 4):
            total = total + sums[t, :, cols].astype(jnp.float32)
        return total

    grad_head[:, WH + WB:] = sum_of(0, 1024)
    grad_head[:, 0:WH + WB] = sum_of(1024, 2048)
    for m in range(3):
        grad_out[16 * m:16 * m + 16] = sum_of(3072 + 512 * m, 512)
    grad_in[...] = sum_of(4608, 1536)


def body(
    hid_whisper, hid_beats, hid_wavlm,
    up_whisper, down_whisper, up_beats, down_beats, up_wavlm, down_wavlm,
    clip_len, send_counts, student_in, w_in, w_out, w_head,
):
    vm = pl.BlockSpec(memory_space=pltpu.VMEM)
    hbm = pl.BlockSpec(memory_space=pl.ANY)
    plan = scratch_plan()
    f32 = jnp.float32
    sums = pl.pallas_call(
        functools.partial(step_kernel, tuple(plan)),
        out_shape=jax.ShapeDtypeStruct((4, 16, SPAN), jnp.bfloat16),
        in_specs=[hbm] * 14 + [pl.BlockSpec(memory_space=pltpu.SMEM)],
        out_specs=vm,
        scratch_shapes=list(plan.values()),
        compiler_params=pltpu.CompilerParams(
            collective_id=0, has_side_effects=True, vmem_limit_bytes=62 * 1024 * 1024),
    )(
        hid_whisper, hid_beats, hid_wavlm,
        up_whisper, down_whisper, up_beats, down_beats, up_wavlm, down_wavlm,
        w_in, w_out, w_head, student_in, send_counts[0], clip_len,
    )
    return tuple(pl.pallas_call(
        sum_kernel,
        out_shape=[jax.ShapeDtypeStruct((16, 1536), f32), jax.ShapeDtypeStruct((48, 512), f32),
                   jax.ShapeDtypeStruct((16, 3072), f32)],
        in_specs=[vm],
        out_specs=[vm] * 3,
    )(sums))


def solution(mesh):
    in_specs = (
        P(("teacher", "dp"), None),
        P(("teacher", "dp"), None),
        P(("teacher", "dp"), None),
        P(None, "teacher"),
        P("teacher", None),
        P(None, "teacher"),
        P("teacher", None),
        P(None, "teacher"),
        P("teacher", None),
        P(("teacher", "dp")),
        P("teacher", None, None),
        P(("teacher", "dp"), None),
        P("dp", None),
        P("dp", None),
        P("dp", None),
    )
    out_specs = (P("dp", None), P("dp", None), P("dp", None))
    return jax.shard_map(body, mesh=mesh, in_specs=in_specs, out_specs=out_specs, check_vma=False)
```

```python
import functools

import jax
import jax.numpy as jnp
from jax import lax
from jax.experimental import pallas as pl
from jax.experimental.pallas import tpu as pltpu
from jax.sharding import PartitionSpec as P

WH = 1280
WB = 768
WL = 1024
EPS = 1e-05


def layer_norm(values):
    wide = values.astype(jnp.float32)
    center = wide - jnp.mean(wide, axis=-1, keepdims=True)
    spread = jnp.mean(center * center, axis=-1, keepdims=True)
    return center * lax.rsqrt(spread + EPS)


MESH_ID = pl.DeviceIdType.MESH
TEACHERS = ((2, WL, WH + WB), (0, WH, 0), (1, WB, WH))
SPAN = 6144
GROUP_COLUMNS = ((0, 1024), (1024, 1280), (2304, 2304), (4608, 1536))


def gelu(values):
    return 0.5 * values * (1.0 + lax.erf(values * 0.7071067811865476))


def dot(a, b):
    return jnp.dot(a, b, preferred_element_type=jnp.float32)


def dot_t(a, b):
    return lax.dot_general(a, b, (((1,), (1,)), ((), ())), preferred_element_type=jnp.float32)


def scratch_plan():
    bf, f32 = jnp.bfloat16, jnp.float32
    vm, dma = pltpu.VMEM, pltpu.SemaphoreType.DMA
    plan = {}
    for k, w in enumerate((WH, WB, WL)):
        plan[f"hid{k}"] = vm((128, w), bf)
        plan[f"vup{k}"] = vm((w, w), bf)
        plan[f"vdown{k}"] = vm((w, w), bf)
        plan[f"keep{k}"] = vm((128, w), f32)
        plan[f"normed{k}"] = vm((1 if k == 1 else 4, 128, w), bf)
    for k, w in ((0, WH), (2, WL)):
        plan[f"part{k}"] = vm((2, 128, w), f32)
        plan[f"sopp{k}"] = vm((2, 64, w), bf)
        plan[f"ropp{k}"] = vm((2, 64, w), bf)
        plan[f"sside{k}"] = vm((2, 128, w), bf)
        plan[f"rside{k}"] = vm((2, 128, w), bf)
    for m, (h, w) in enumerate(((16, 1536), (48, 512), (16, 3072))):
        plan[f"full{m}"] = vm((4, 4, 2, h, w), bf)
    plan.update(
        hidden=vm((256, WH), bf),
        outgoing=vm((32, 8, 512), HAND), incoming=vm((32, 8, 512), HAND),
        student=vm((128, 512), bf), active=vm((128, 1536), bf),
        slope=vm((128, 1536), f32), predicted=vm((128, 3072), f32), fgrad=vm((128, 512), f32),
        tin=vm((4, 4, 2, 16, 128), bf), tact=vm((4, 4, 2, 48, 128), bf), tfeat=vm((4, 4, 2, 16, 128), bf),
        lin=vm((4, 4, 16, 256), bf), lact=vm((4, 4, 48, 256), bf), lfeat=vm((4, 4, 16, 256), bf),
        rpre=vm((256, 1536), bf), rfg=vm((256, 512), bf), rerr=vm((256, 3072), bf),
        own1=vm((4, 16, SPAN), f32), send1=vm((3, 4, 16, SPAN), bf), recv1=vm((3, 4, 16, SPAN), bf),
        own2=vm((16, SPAN), f32), send2=vm((3, 16, SPAN), bf), recv2=vm((3, 16, SPAN), bf),
        rows_in=vm((128, 512), bf), counts=vm((32, 32), jnp.int32),
        wsem=dma((6,)), isem=dma((8,)),
        ags=dma((3, 2)), agr=dma((3, 2)), fws=dma((3, 2)), fwr=dma((3, 2)),
        ops=dma((3, 2)), opr=dma((3, 2)), sds=dma((3, 2)), sdr=dma((3, 2)),
        piece=vm((2, 48, WB), bf), others=vm((2, 4, 4, 3, 48, WB), bf),
        psem=dma((2,)), pys=dma((3,)), pyr=dma((3,)), gs=dma((96,)), gr=dma((96,)),
        hos=dma((32,)), hor=dma((32,)),
        xs=dma((8,)), xr=dma((8,)),
        s1s=dma((4, 3)), s1r=dma((4, 3)), s2s=dma((4, 3)), s2r=dma((4, 3)), s3s=dma((4, 3)), s3r=dma((4, 3)),
    )
    return plan


HAND = jnp.bfloat16


def step_kernel(names, *refs):
    ups, downs = refs[3:9:2], refs[4:9:2]
    shards = refs[9:12]
    clip_ref, sums = refs[14:16]
    r = dict(zip(names, refs[16:]))
    per = lambda name: [r.get(f"{name}{k}") for k in range(3)]
    hid = per("hid")
    vup, vdown, normed, keep, part = per("vup"), per("vdown"), per("normed"), per("keep"), per("part")
    sopp, ropp, sside, rside, full = per("sopp"), per("ropp"), per("sside"), per("rside"), per("full")
    hidden, rerr, rfg, rpre = r["hidden"], r["rerr"], r["rfg"], r["rpre"]
    bf, f32 = jnp.bfloat16, jnp.float32

    order = [k for k, _, _ in TEACHERS]
    y = lax.axis_index("teacher")
    dp = lax.axis_index("dp")
    c = dp % 2
    z = (dp // 2) % 4
    x = dp // 8
    swap = c == 1
    first = jnp.where(swap, z, x)
    second = jnp.where(swap, x, z)
    at_y = lambda t: {"teacher": t % 4}
    right, left = at_y(y + 1), at_y(y + 3)
    pair = {"dp": (x * 4 + z) * 2 + (1 - c)}

    def at_first(a):
        return {"dp": jnp.where(swap, (x * 4 + a) * 2 + 1, (a * 4 + z) * 2)}

    def at_second(b):
        return {"dp": jnp.where(swap, (b * 4 + z) * 2 + 1, (x * 4 + b) * 2)}

    def send(src, dst, ssem, rsem, dev):
        cp = pltpu.make_async_remote_copy(
            src_ref=src, dst_ref=dst, send_sem=ssem, recv_sem=rsem,
            device_id=dev, device_id_type=MESH_ID)
        cp.start()
        return cp

    def finish_all(copies):
        for cp in copies:
            cp.wait()

    ready = {}
    for i, (name, src, dst) in enumerate((
        (order[0], refs[order[0]], hid[order[0]]),
        ("counts", refs[13], r["counts"]),
        ("rows", refs[12], r["rows_in"]),
        ("in", shards[0], full[0].at[x, z, c]),
        ("out", shards[1], full[1].at[x, z, c]),
        ("head", shards[2], full[2].at[x, z, c]),
        (order[1], refs[order[1]], hid[order[1]]),
        (order[2], refs[order[2]], hid[order[2]]),
    )):
        ready[name] = pltpu.make_async_copy(src, dst, r["isem"].at[i])
        ready[name].start()
    piece_rows = pl.ds(pl.multiple_of((x * 4 + z) * 48, 48), 48)
    pieces = [pltpu.make_async_copy(src.at[piece_rows], r["piece"].at[i], r["psem"].at[i])
              for i, src in enumerate((ups[1], downs[1]))]
    for cp in pieces:
        cp.start()
    loads = {}
    for n, (k, _, _) in enumerate(TEACHERS):
        loads[k] = (pltpu.make_async_copy(ups[k], vup[k], r["wsem"].at[2 * n]),
                    pltpu.make_async_copy(downs[k], vdown[k], r["wsem"].at[2 * n + 1]))
        for cp in loads[k]:
            cp.start()

    barrier = pltpu.get_barrier_semaphore()
    for d in range(1, 4):
        pl.semaphore_signal(barrier, inc=1, device_id=at_y(y + d), device_id_type=MESH_ID)
    for d in range(1, 32):
        pl.semaphore_signal(barrier, inc=1, device_id={"dp": (dp + d) % 32}, device_id_type=MESH_ID)
    ready[order[0]].wait()
    normed[order[0]][0] = layer_norm(hid[order[0]][...]).astype(bf)

    ready["counts"].wait()
    counts = r["counts"][...].astype(f32)
    iota = lambda shape, axis: lax.broadcasted_iota(jnp.int32, shape, axis)
    src_at, own_at = iota((32, 32), 0), iota((32, 32), 1)
    one = lambda hit: jnp.where(hit, 1.0, 0.0)
    exact = lambda v: v.astype(bf)
    before_src = dot(exact(one(own_at < src_at)), exact(counts))
    before_own = dot(exact(counts), exact(one(src_at < own_at)))
    my_col, my_row = one(own_at == dp), one(src_at == dp)
    row_at, slot_at = iota((256, 32), 0), iota((256, 32), 1) * 8
    spread = exact(one((row_at >= slot_at) & (row_at < slot_at + 8)))
    wide_col = lambda v: dot(spread, exact(jnp.broadcast_to(jnp.sum(v * my_col, axis=1, keepdims=True), (32, 128))))
    slot = (iota((256, 128), 0) & 7).astype(f32)
    hit = (iota((256, 128), 1).astype(f32) == wide_col(before_src) + slot) & (slot < wide_col(counts))
    ready["rows"].wait()
    leaving = dot(exact(one(hit)), r["rows_in"][...])
    r["outgoing"][...] = leaving.reshape(32, 8, 512).astype(HAND)
    r["incoming"][dp] = r["outgoing"][dp]
    slot_at2, col_at = iota((32, 256), 0) * 8, iota((32, 256), 1)
    spread2 = exact(one((col_at >= slot_at2) & (col_at < slot_at2 + 8)))
    wide_row = lambda v: dot(exact(jnp.broadcast_to(jnp.sum(v * my_row, axis=0, keepdims=True), (128, 32))), spread2)
    slot2 = (iota((128, 256), 1) & 7).astype(f32)
    hit2 = (iota((128, 256), 0).astype(f32) == wide_row(before_own) + slot2) & (slot2 < wide_row(counts))
    place = exact(one(hit2))
    mask = one(iota((128, 1), 0) < clip_ref[0])

    finish_all([ready["in"], ready["out"], ready["head"]])
    pl.semaphore_wait(barrier, 34)

    def gather_out(k):
        return (send(normed[k].at[0], normed[k].at[1], r["ags"].at[k, 0], r["agr"].at[k, 0], right),
                send(normed[k].at[0], normed[k].at[2], r["ags"].at[k, 1], r["agr"].at[k, 1], left))

    def forward(k):
        lo, hi = pl.ds(0, 64), pl.ds(64, 64)
        return (send(normed[k].at[1, lo], normed[k].at[3, lo], r["fws"].at[k, 0], r["fwr"].at[k, 0], right),
                send(normed[k].at[2, hi], normed[k].at[3, hi], r["fws"].at[k, 1], r["fwr"].at[k, 1], left))

    def ffn(k, width, at, count, store):
        rows = count * 128
        values = normed[k][at:at + count].reshape(rows, width)
        for j in range(width // 256):
            cols = slice(256 * j, 256 * j + 256)
            hidden[0:rows, cols] = gelu(dot(values, vup[k][:, cols])).astype(bf)
        for j in range(width // 256):
            cols = slice(256 * j, 256 * j + 256)
            store(cols, dot(hidden[0:rows, 0:width], vdown[k][:, cols]))

    counter = iter(range(96))
    others = r["others"]

    def ring_send(ref, dev):
        i = next(counter)
        return send(ref, ref, r["gs"].at[i], r["gr"].at[i], dev)

    def slot_of(f, s):
        return jnp.where(swap, s, f), jnp.where(swap, f, s)

    def student_slot(f, s):
        i, j = slot_of(f, s)
        return [full[m].at[i, j, c] for m in range(3)]

    def beats_slot(f, s):
        i, j = slot_of(f, s)
        return others.at[c, i, j]

    up2, down2 = (second + 1) % 4, (second + 3) % 4
    up2_dev, down2_dev = at_second(up2), at_second(down2)
    row_devs = [at_first((first + d) % 4) for d in (2, 1, 3)]

    gathers = {order[0]: gather_out(order[0])}
    stage = {}
    stage["s1"] = [ring_send(ref, dev) for dev in row_devs for ref in student_slot(first, second)]
    finish_all(pieces)
    stage["py"] = [send(r["piece"].at[c], others.at[c, x, z, 3 - o], r["pys"].at[o - 1], r["pyr"].at[o - 1], at_y(y + o))
                   for o in (2, 1, 3)]
    ready[order[1]].wait()
    normed[order[1]][0] = layer_norm(hid[order[1]][...]).astype(bf)
    gathers[order[1]] = gather_out(order[1])
    hand = []
    for d in range(1, 32):
        to = (dp + d) % 32
        hand.append(send(r["outgoing"].at[to], r["incoming"].at[dp], r["hos"].at[d], r["hor"].at[d], {"dp": to}))
    ready[order[2]].wait()
    normed[order[2]][0] = layer_norm(hid[order[2]][...]).astype(bf)

    def spread_second(name, slots):
        stage[name + "a"], stage[name + "b"] = [], []
        for part, ups_first in ((name + "a", ((0, 2), (1, 3))), (name + "b", ((2, 0), (3, 1)))):
            for i, j in ups_first:
                stage[part] += [ring_send(ref, up2_dev) for ref in slots(i, second)]
                stage[part] += [ring_send(ref, down2_dev) for ref in slots(j, second)]

    def relay_second(name, slots):
        finish_all(stage[name + "a"])
        stage[name + "f"] = [ring_send(ref, up2_dev) for i in (0, 1) for ref in slots(i, down2)]
        stage[name + "f"] += [ring_send(ref, down2_dev) for i in (2, 3) for ref in slots(i, up2)]

    def student_second():
        finish_all(stage["s1"])
        spread_second("s2", student_slot)

    def student_pair():
        finish_all(stage["s2b"] + stage["s2f"])
        stage["s3"] = [ring_send(full[m].at[:, :, c], pair) for m in range(3)]

    def beats_slots(f, s):
        return [beats_slot(f, s)]

    def beats_first():
        finish_all(stage["py"])
        stage["b1"] = [ring_send(beats_slot(first, second), dev) for dev in row_devs]

    def beats_second():
        finish_all(stage["b1"])
        spread_second("b2", beats_slots)
        stage["b3"] = [ring_send(beats_slot(i, second), pair) for i in range(4)]

    def beats_share():
        finish_all(stage["b2b"])
        stage["b3"] += [ring_send(beats_slot(i, s), pair) for s in (down2, up2) for i in range(4)]

    def beats_pair():
        finish_all(stage["b2f"])
        stage["b3"] += [ring_send(beats_slot(i, (second + 2) % 4), pair) for i in range(4)]

    def beats_rest():
        values = normed[1][0]
        for d in range(3):
            for j in range(WB // 256):
                cols = slice(256 * j, 256 * j + 256)
                hidden[0:128, cols] = gelu(dot(values, others[0, :, :, d, :, cols].reshape(WB, 256))).astype(bf)
            for j in range(WB // 256):
                cols = slice(256 * j, 256 * j + 256)
                keep[1][:, cols] += dot(hidden[0:128, 0:WB], others[1, :, :, d, :, cols].reshape(WB, 256))

    opposite, sides = {}, {}

    def send_sides(k):
        finish_all(opposite[k])
        sside[k][0, 0:64] = part[k][0, 0:64].astype(bf)
        sside[k][0, 64:128] = (part[k][0, 64:128] + ropp[k][1].astype(f32)).astype(bf)
        sside[k][1, 0:64] = (part[k][1, 0:64] + ropp[k][0].astype(f32)).astype(bf)
        sside[k][1, 64:128] = part[k][1, 64:128].astype(bf)
        sides[k] = (send(sside[k].at[1], rside[k].at[0], r["sds"].at[k, 0], r["sdr"].at[k, 0], right),
                    send(sside[k].at[0], rside[k].at[1], r["sds"].at[k, 1], r["sdr"].at[k, 1], left))

    def pair_send(i, src, dst):
        return send(src, dst, r["xs"].at[i], r["xr"].at[i], pair)

    def share_rows(i, values, h, mine, joined):
        mine[...] = values.T.reshape(4, 4, 2, h, 128)
        joined[:, :, :, 0:128] = mine[:, :, c]
        return pair_send(i, mine.at[:, :, 1 - c], joined.at[:, :, :, pl.ds(128, 128)])

    shared, passed = {}, {}
    widths = [width for _, width, _ in TEACHERS]

    def own_rows(n):
        k = order[n]
        finish_all(loads[k])

        def put(cols, v):
            keep[k][:, cols] = v
        ffn(k, widths[n], 0, 1, put)

    def side_rows(n):
        k = order[n]

        def put(cols, v):
            part[k][:, :, cols] = v.reshape(2, 128, 256)
        ffn(k, widths[n], 1, 2, put)

    def pass_on(n):
        finish_all(gathers[order[n]])
        passed[n] = forward(order[n])

    def far_rows(n):
        k = order[n]
        finish_all(passed[n])

        def put(cols, v):
            sopp[k][:, :, cols] = v.astype(bf).reshape(2, 64, 256)
        ffn(k, widths[n], 3, 1, put)
        opposite[k] = (send(sopp[k].at[0], ropp[k].at[0], r["ops"].at[k, 0], r["opr"].at[k, 0], right),
                       send(sopp[k].at[1], ropp[k].at[1], r["ops"].at[k, 1], r["opr"].at[k, 1], left))

    own_rows(0)
    student_second()
    pass_on(0)
    own_rows(1)
    side_rows(0)
    own_rows(2)
    beats_first()
    pass_on(1)
    side_rows(1)
    relay_second("s2", student_slot)
    far_rows(0)
    beats_second()
    finish_all(hand)
    student = dot(place, r["incoming"][...].reshape(256, 512).astype(bf)).astype(bf)
    r["student"][...] = student
    shared["in"] = share_rows(0, student, 16, r["tin"], r["lin"])
    far_rows(1)
    student_pair()
    send_sides(order[0])
    stage["s3"][0].wait()
    student = r["student"][...]
    pre_act = dot(student, full[0][...].reshape(512, 1536))
    shifted = pre_act - 4.0
    decay = jnp.exp(-jnp.abs(shifted))
    soft = jnp.maximum(shifted, 0.0) + jnp.log1p(decay)
    activated = (soft - 0.08 * pre_act - 0.035).astype(bf)
    r["slope"][...] = jnp.where(shifted >= 0.0, 1.0, decay) / (1.0 + decay) - 0.08
    r["active"][...] = activated
    relay_second("b2", beats_slots)
    send_sides(order[1])
    stage["s3"][1].wait()
    features = (student.astype(f32) + dot(r["active"][...], full[1][...].reshape(1536, 512))).astype(bf)
    shared["feat"] = share_rows(1, features, 16, r["tfeat"], r["lfeat"])
    beats_share()
    stage["s3"][2].wait()
    for k, width, start in TEACHERS:
        r["predicted"][:, start:start + width] = dot(features, full[2][:, :, :, :, start:start + width].reshape(512, width))

    def error_of(n):
        k, width, start = TEACHERS[n]
        cols = slice(start, start + width)
        total = hid[k][...].astype(f32) + keep[k][...]
        if n < 2:
            finish_all(sides[k])
            total = total + rside[k][0].astype(f32) + rside[k][1].astype(f32)
        target = total.astype(bf).astype(f32)
        err = ((r["predicted"][:, cols] - target) * (2.0 / width) * mask).astype(bf)
        rerr[0:128, cols] = err
        cp = pair_send(3 + n, rerr.at[pl.ds(0, 128), pl.ds(start, width)], rerr.at[pl.ds(128, 128), pl.ds(start, width)])
        back = dot_t(err, full[2][:, :, :, :, cols].reshape(512, width))
        if n == 0:
            r["fgrad"][...] = back
        elif n == 1:
            r["fgrad"][...] += back
        else:
            back = r["fgrad"][...] + back
        return cp, back

    def block_rows(joined, a):
        tiles = [joined[jnp.where(swap, b, a), jnp.where(swap, a, b)] for b in range(4)]
        return jnp.concatenate(tiles, axis=0)

    def products(n, a, store):
        heads = block_rows(r["lfeat"], a) if n < 3 else None
        if n < 2:
            _, width, start = TEACHERS[n]
            store(GROUP_COLUMNS[n][0], dot(heads, rerr[:, start:start + width]).reshape(4, 16, width))
        elif n == 2:
            store(2304, dot(heads, rerr[:, WH:WH + WB]).reshape(4, 16, WB))
            outs = dot(block_rows(r["lact"], a), rfg[...]).reshape(4, 48, 512)
            for m in range(3):
                store(3072 + 512 * m, outs[:, 16 * m:16 * m + 16])
        else:
            store(4608, dot(block_rows(r["lin"], a), rpre[...]).reshape(4, 16, 1536))

    phase1, phase2 = {}, {}

    def start_group(n):
        start, width = GROUP_COLUMNS[n]
        cols = pl.ds(start, width)
        copies = []
        for d in (2, 1, 3):
            a = (first + d) % 4

            def put(at, v):
                r["send1"][d - 1, :, :, at:at + v.shape[2]] = v.astype(bf)
            products(n, a, put)
            copies.append(send(r["send1"].at[d - 1, :, :, cols], r["recv1"].at[d - 1, :, :, cols],
                               r["s1s"].at[n, d - 1], r["s1r"].at[n, d - 1], at_first(a)))

        def put_own(at, v):
            r["own1"][:, :, at:at + v.shape[2]] = v
        products(n, first, put_own)
        phase1[n] = copies

    def next_group(n):
        start, width = GROUP_COLUMNS[n]
        cols = slice(start, start + width)
        ref_cols = pl.ds(start, width)
        finish_all(phase1[n])

        def total1(b):
            v = r["own1"][b, :, cols]
            for i in range(3):
                v = v + r["recv1"][i, b, :, cols].astype(f32)
            return v
        copies = []
        for d in (2, 1, 3):
            b = (second + d) % 4
            r["send2"][d - 1, :, cols] = total1(b).astype(bf)
            copies.append(send(r["send2"].at[d - 1, :, ref_cols], r["recv2"].at[d - 1, :, ref_cols],
                               r["s2s"].at[n, d - 1], r["s2r"].at[n, d - 1], at_second(b)))
        r["own2"][:, cols] = total1(second)
        phase2[n] = copies

    cp, _ = error_of(0)
    shared["act"] = share_rows(2, r["active"][...], 48, r["tact"], r["lact"])
    finish_all([cp, shared["feat"]])
    start_group(0)
    beats_pair()
    cp, _ = error_of(1)
    finish_all([shared["in"], shared["act"]])
    next_group(0)
    cp.wait()
    start_group(1)
    finish_all(stage["b3"])
    beats_rest()
    cp, back = error_of(2)
    feat_grad = back.astype(bf)
    rfg[0:128] = feat_grad
    late = [cp, pair_send(6, rfg.at[pl.ds(0, 128)], rfg.at[pl.ds(128, 128)])]
    act_grad = dot_t(feat_grad, full[1][...].reshape(1536, 512))
    rpre[0:128] = (act_grad * r["slope"][...]).astype(bf)
    cp = pair_send(7, rpre.at[pl.ds(0, 128)], rpre.at[pl.ds(128, 128)])
    finish_all(late)
    start_group(2)
    next_group(1)
    cp.wait()
    start_group(3)

    summed = {}

    def send_sums(q):
        start, width = GROUP_COLUMNS[q]
        cols, ref_cols = slice(start, start + width), pl.ds(start, width)
        total = r["own2"][:, cols]
        for i in range(3):
            total = total + r["recv2"][i, :, cols].astype(f32)
        sums[y, :, cols] = total.astype(bf)
        mine = sums.at[y, :, ref_cols]
        summed[q] = [send(mine, mine, r["s3s"].at[q, d - 1], r["s3r"].at[q, d - 1], at_y(y + d)) for d in (2, 1, 3)]

    finish_all(phase2[0])
    send_sums(0)
    finish_all(phase2[1])
    send_sums(1)
    next_group(2)
    next_group(3)
    finish_all(phase2[2])
    send_sums(2)
    finish_all(phase2[3])
    send_sums(3)
    for q in range(4):
        finish_all(summed[q])


def sum_kernel(sums, grad_in, grad_out, grad_head):
    def sum_of(start, width):
        cols = slice(start, start + width)
        total = sums[0, :, cols].astype(jnp.float32)
        for t in range(1, 4):
            total = total + sums[t, :, cols].astype(jnp.float32)
        return total

    grad_head[:, WH + WB:] = sum_of(0, 1024)
    grad_head[:, 0:WH + WB] = sum_of(1024, 2048)
    for m in range(3):
        grad_out[16 * m:16 * m + 16] = sum_of(3072 + 512 * m, 512)
    grad_in[...] = sum_of(4608, 1536)


def body(
    hid_whisper, hid_beats, hid_wavlm,
    up_whisper, down_whisper, up_beats, down_beats, up_wavlm, down_wavlm,
    clip_len, send_counts, student_in, w_in, w_out, w_head,
):
    vm = pl.BlockSpec(memory_space=pltpu.VMEM)
    hbm = pl.BlockSpec(memory_space=pl.ANY)
    plan = scratch_plan()
    f32 = jnp.float32
    sums = pl.pallas_call(
        functools.partial(step_kernel, tuple(plan)),
        out_shape=jax.ShapeDtypeStruct((4, 16, SPAN), jnp.bfloat16),
        in_specs=[hbm] * 14 + [pl.BlockSpec(memory_space=pltpu.SMEM)],
        out_specs=vm,
        scratch_shapes=list(plan.values()),
        compiler_params=pltpu.CompilerParams(
            collective_id=0, has_side_effects=True, vmem_limit_bytes=62 * 1024 * 1024),
    )(
        hid_whisper, hid_beats, hid_wavlm,
        up_whisper, down_whisper, up_beats, down_beats, up_wavlm, down_wavlm,
        w_in, w_out, w_head, student_in, send_counts[0], clip_len,
    )
    return tuple(pl.pallas_call(
        sum_kernel,
        out_shape=[jax.ShapeDtypeStruct((16, 1536), f32), jax.ShapeDtypeStruct((48, 512), f32),
                   jax.ShapeDtypeStruct((16, 3072), f32)],
        in_specs=[vm],
        out_specs=[vm] * 3,
    )(sums))


def solution(mesh):
    in_specs = (
        P(("teacher", "dp"), None),
        P(("teacher", "dp"), None),
        P(("teacher", "dp"), None),
        P(None, "teacher"),
        P("teacher", None),
        P(None, "teacher"),
        P("teacher", None),
        P(None, "teacher"),
        P("teacher", None),
        P(("teacher", "dp")),
        P("teacher", None, None),
        P(("teacher", "dp"), None),
        P("dp", None),
        P("dp", None),
        P("dp", None),
    )
    out_specs = (P("dp", None), P("dp", None), P("dp", None))
    return jax.shard_map(body, mesh=mesh, in_specs=in_specs, out_specs=out_specs, check_vma=False)
```

```python
import functools

import jax
import jax.numpy as jnp
from jax import lax
from jax.experimental import pallas as pl
from jax.experimental.pallas import tpu as pltpu
from jax.sharding import PartitionSpec as P

WH = 1280
WB = 768
WL = 1024
EPS = 1e-05


def layer_norm(values):
    wide = values.astype(jnp.float32)
    center = wide - jnp.mean(wide, axis=-1, keepdims=True)
    spread = jnp.mean(center * center, axis=-1, keepdims=True)
    return center * lax.rsqrt(spread + EPS)


MESH_ID = pl.DeviceIdType.MESH
TEACHERS = ((2, WL, WH + WB), (0, WH, 0), (1, WB, WH))
SPAN = 6144
GROUP_COLUMNS = ((0, 1024), (1024, 1280), (2304, 768), (3072, 1536), (4608, 1536))


def gelu(values):
    return 0.5 * values * (1.0 + lax.erf(values * 0.7071067811865476))


def dot(a, b):
    return jnp.dot(a, b, preferred_element_type=jnp.float32)


def dot_t(a, b):
    return lax.dot_general(a, b, (((1,), (1,)), ((), ())), preferred_element_type=jnp.float32)


def scratch_plan():
    bf, f32 = jnp.bfloat16, jnp.float32
    vm, dma = pltpu.VMEM, pltpu.SemaphoreType.DMA
    plan = {}
    for k, w in enumerate((WH, WB, WL)):
        plan[f"hid{k}"] = vm((128, w), bf)
        plan[f"vup{k}"] = vm((w, w), bf)
        plan[f"vdown{k}"] = vm((w, w), bf)
        plan[f"keep{k}"] = vm((128, w), f32)
        plan[f"normed{k}"] = vm((1 if k == 1 else 4, 128, w), bf)
    for k, w in ((0, WH), (2, WL)):
        plan[f"part{k}"] = vm((2, 128, w), f32)
        plan[f"sopp{k}"] = vm((2, 64, w), bf)
        plan[f"ropp{k}"] = vm((2, 64, w), bf)
        plan[f"sside{k}"] = vm((2, 128, w), bf)
        plan[f"rside{k}"] = vm((2, 128, w), bf)
    for m, (h, w) in enumerate(((16, 1536), (48, 512), (16, 3072))):
        plan[f"full{m}"] = vm((4, 4, 2, h, w), bf)
    plan.update(
        hidden=vm((256, WH), bf),
        outgoing=vm((32, 8, 512), HAND), incoming=vm((32, 8, 512), HAND),
        student=vm((128, 512), bf), active=vm((128, 1536), bf),
        slope=vm((128, 1536), f32), predicted=vm((128, 3072), f32), fgrad=vm((128, 512), f32),
        tin=vm((4, 4, 2, 16, 128), bf), tact=vm((4, 4, 2, 48, 128), bf), tfeat=vm((4, 4, 2, 16, 128), bf),
        lin=vm((4, 4, 16, 256), bf), lact=vm((4, 4, 48, 256), bf), lfeat=vm((4, 4, 16, 256), bf),
        rpre=vm((256, 1536), bf), rfg=vm((256, 512), bf), rerr=vm((256, 3072), bf),
        own1=vm((4, 16, SPAN), f32), send1=vm((3, 4, 16, SPAN), bf), recv1=vm((3, 4, 16, SPAN), bf),
        own2=vm((16, SPAN), f32), send2=vm((3, 16, SPAN), bf), recv2=vm((3, 16, SPAN), bf),
        rows_in=vm((128, 512), bf), counts=vm((32, 32), jnp.int32),
        wsem=dma((6,)), isem=dma((8,)),
        ags=dma((3, 2)), agr=dma((3, 2)), fws=dma((3, 2)), fwr=dma((3, 2)),
        ops=dma((3, 2)), opr=dma((3, 2)), sds=dma((3, 2)), sdr=dma((3, 2)),
        piece=vm((2, 48, WB), bf), others=vm((2, 4, 4, 3, 48, WB), bf),
        psem=dma((2,)), pys=dma((3,)), pyr=dma((3,)), gs=dma((96,)), gr=dma((96,)),
        hos=dma((32,)), hor=dma((32,)),
        xs=dma((8,)), xr=dma((8,)),
        s1s=dma((5, 3)), s1r=dma((5, 3)), s2s=dma((5, 3)), s2r=dma((5, 3)), s3s=dma((5, 3)), s3r=dma((5, 3)),
    )
    return plan


HAND = jnp.bfloat16


def step_kernel(names, *refs):
    ups, downs = refs[3:9:2], refs[4:9:2]
    shards = refs[9:12]
    clip_ref, sums = refs[14:16]
    r = dict(zip(names, refs[16:]))
    per = lambda name: [r.get(f"{name}{k}") for k in range(3)]
    hid = per("hid")
    vup, vdown, normed, keep, part = per("vup"), per("vdown"), per("normed"), per("keep"), per("part")
    sopp, ropp, sside, rside, full = per("sopp"), per("ropp"), per("sside"), per("rside"), per("full")
    hidden, rerr, rfg, rpre = r["hidden"], r["rerr"], r["rfg"], r["rpre"]
    bf, f32 = jnp.bfloat16, jnp.float32

    order = [k for k, _, _ in TEACHERS]
    y = lax.axis_index("teacher")
    dp = lax.axis_index("dp")
    c = dp % 2
    z = (dp // 2) % 4
    x = dp // 8
    swap = c == 1
    first = jnp.where(swap, z, x)
    second = jnp.where(swap, x, z)
    at_y = lambda t: {"teacher": t % 4}
    right, left = at_y(y + 1), at_y(y + 3)
    pair = {"dp": (x * 4 + z) * 2 + (1 - c)}

    def at_first(a):
        return {"dp": jnp.where(swap, (x * 4 + a) * 2 + 1, (a * 4 + z) * 2)}

    def at_second(b):
        return {"dp": jnp.where(swap, (b * 4 + z) * 2 + 1, (x * 4 + b) * 2)}

    def send(src, dst, ssem, rsem, dev):
        cp = pltpu.make_async_remote_copy(
            src_ref=src, dst_ref=dst, send_sem=ssem, recv_sem=rsem,
            device_id=dev, device_id_type=MESH_ID)
        cp.start()
        return cp

    def finish_all(copies):
        for cp in copies:
            cp.wait()

    ready = {}
    for i, (name, src, dst) in enumerate((
        (order[0], refs[order[0]], hid[order[0]]),
        ("counts", refs[13], r["counts"]),
        ("rows", refs[12], r["rows_in"]),
        ("in", shards[0], full[0].at[x, z, c]),
        ("out", shards[1], full[1].at[x, z, c]),
        ("head", shards[2], full[2].at[x, z, c]),
        (order[1], refs[order[1]], hid[order[1]]),
        (order[2], refs[order[2]], hid[order[2]]),
    )):
        ready[name] = pltpu.make_async_copy(src, dst, r["isem"].at[i])
        ready[name].start()
    piece_rows = pl.ds(pl.multiple_of((x * 4 + z) * 48, 48), 48)
    pieces = [pltpu.make_async_copy(src.at[piece_rows], r["piece"].at[i], r["psem"].at[i])
              for i, src in enumerate((ups[1], downs[1]))]
    for cp in pieces:
        cp.start()
    loads = {}
    for n, (k, _, _) in enumerate(TEACHERS):
        loads[k] = (pltpu.make_async_copy(ups[k], vup[k], r["wsem"].at[2 * n]),
                    pltpu.make_async_copy(downs[k], vdown[k], r["wsem"].at[2 * n + 1]))
        for cp in loads[k]:
            cp.start()

    barrier = pltpu.get_barrier_semaphore()
    for d in range(1, 4):
        pl.semaphore_signal(barrier, inc=1, device_id=at_y(y + d), device_id_type=MESH_ID)
    for d in range(1, 32):
        pl.semaphore_signal(barrier, inc=1, device_id={"dp": (dp + d) % 32}, device_id_type=MESH_ID)
    ready[order[0]].wait()
    normed[order[0]][0] = layer_norm(hid[order[0]][...]).astype(bf)

    ready["counts"].wait()
    counts = r["counts"][...].astype(f32)
    iota = lambda shape, axis: lax.broadcasted_iota(jnp.int32, shape, axis)
    src_at, own_at = iota((32, 32), 0), iota((32, 32), 1)
    one = lambda hit: jnp.where(hit, 1.0, 0.0)
    exact = lambda v: v.astype(bf)
    before_src = dot(exact(one(own_at < src_at)), exact(counts))
    before_own = dot(exact(counts), exact(one(src_at < own_at)))
    my_col, my_row = one(own_at == dp), one(src_at == dp)
    row_at, slot_at = iota((256, 32), 0), iota((256, 32), 1) * 8
    spread = exact(one((row_at >= slot_at) & (row_at < slot_at + 8)))
    wide_col = lambda v: dot(spread, exact(jnp.broadcast_to(jnp.sum(v * my_col, axis=1, keepdims=True), (32, 128))))
    slot = (iota((256, 128), 0) & 7).astype(f32)
    hit = (iota((256, 128), 1).astype(f32) == wide_col(before_src) + slot) & (slot < wide_col(counts))
    ready["rows"].wait()
    leaving = dot(exact(one(hit)), r["rows_in"][...])
    r["outgoing"][...] = leaving.reshape(32, 8, 512).astype(HAND)
    r["incoming"][dp] = r["outgoing"][dp]
    slot_at2, col_at = iota((32, 256), 0) * 8, iota((32, 256), 1)
    spread2 = exact(one((col_at >= slot_at2) & (col_at < slot_at2 + 8)))
    wide_row = lambda v: dot(exact(jnp.broadcast_to(jnp.sum(v * my_row, axis=0, keepdims=True), (128, 32))), spread2)
    slot2 = (iota((128, 256), 1) & 7).astype(f32)
    hit2 = (iota((128, 256), 0).astype(f32) == wide_row(before_own) + slot2) & (slot2 < wide_row(counts))
    place = exact(one(hit2))
    mask = one(iota((128, 1), 0) < clip_ref[0])

    finish_all([ready["in"], ready["out"], ready["head"]])
    pl.semaphore_wait(barrier, 34)

    def gather_out(k):
        return (send(normed[k].at[0], normed[k].at[1], r["ags"].at[k, 0], r["agr"].at[k, 0], right),
                send(normed[k].at[0], normed[k].at[2], r["ags"].at[k, 1], r["agr"].at[k, 1], left))

    def forward(k):
        lo, hi = pl.ds(0, 64), pl.ds(64, 64)
        return (send(normed[k].at[1, lo], normed[k].at[3, lo], r["fws"].at[k, 0], r["fwr"].at[k, 0], right),
                send(normed[k].at[2, hi], normed[k].at[3, hi], r["fws"].at[k, 1], r["fwr"].at[k, 1], left))

    def ffn(k, width, at, count, store):
        rows = count * 128
        values = normed[k][at:at + count].reshape(rows, width)
        for j in range(width // 256):
            cols = slice(256 * j, 256 * j + 256)
            hidden[0:rows, cols] = gelu(dot(values, vup[k][:, cols])).astype(bf)
        for j in range(width // 256):
            cols = slice(256 * j, 256 * j + 256)
            store(cols, dot(hidden[0:rows, 0:width], vdown[k][:, cols]))

    counter = iter(range(96))
    others = r["others"]

    def ring_send(ref, dev):
        i = next(counter)
        return send(ref, ref, r["gs"].at[i], r["gr"].at[i], dev)

    def slot_of(f, s):
        return jnp.where(swap, s, f), jnp.where(swap, f, s)

    def student_slot(f, s):
        i, j = slot_of(f, s)
        return [full[m].at[i, j, c] for m in range(3)]

    def beats_slot(f, s):
        i, j = slot_of(f, s)
        return others.at[c, i, j]

    up2, down2 = (second + 1) % 4, (second + 3) % 4
    up2_dev, down2_dev = at_second(up2), at_second(down2)
    row_devs = [at_first((first + d) % 4) for d in (2, 1, 3)]

    gathers = {order[0]: gather_out(order[0])}
    stage = {}
    stage["s1"] = [ring_send(ref, dev) for dev in row_devs for ref in student_slot(first, second)]
    finish_all(pieces)
    stage["py"] = [send(r["piece"].at[c], others.at[c, x, z, 3 - o], r["pys"].at[o - 1], r["pyr"].at[o - 1], at_y(y + o))
                   for o in (2, 1, 3)]
    ready[order[1]].wait()
    normed[order[1]][0] = layer_norm(hid[order[1]][...]).astype(bf)
    gathers[order[1]] = gather_out(order[1])
    hand = []
    for d in range(1, 32):
        to = (dp + d) % 32
        hand.append(send(r["outgoing"].at[to], r["incoming"].at[dp], r["hos"].at[d], r["hor"].at[d], {"dp": to}))
    ready[order[2]].wait()
    normed[order[2]][0] = layer_norm(hid[order[2]][...]).astype(bf)

    def spread_second(name, slots):
        stage[name + "a"], stage[name + "b"] = [], []
        for part, ups_first in ((name + "a", ((0, 2), (1, 3))), (name + "b", ((2, 0), (3, 1)))):
            for i, j in ups_first:
                stage[part] += [ring_send(ref, up2_dev) for ref in slots(i, second)]
                stage[part] += [ring_send(ref, down2_dev) for ref in slots(j, second)]

    def relay_second(name, slots):
        finish_all(stage[name + "a"])
        stage[name + "f"] = [ring_send(ref, up2_dev) for i in (0, 1) for ref in slots(i, down2)]
        stage[name + "f"] += [ring_send(ref, down2_dev) for i in (2, 3) for ref in slots(i, up2)]

    def student_second():
        finish_all(stage["s1"])
        spread_second("s2", student_slot)

    def student_pair():
        finish_all(stage["s2b"] + stage["s2f"])
        stage["s3"] = [ring_send(full[m].at[:, :, c], pair) for m in range(3)]

    def beats_slots(f, s):
        return [beats_slot(f, s)]

    def beats_first():
        finish_all(stage["py"])
        stage["b1"] = [ring_send(beats_slot(first, second), dev) for dev in row_devs]

    def beats_second():
        finish_all(stage["b1"])
        spread_second("b2", beats_slots)
        stage["b3"] = [ring_send(beats_slot(i, second), pair) for i in range(4)]

    def beats_share():
        finish_all(stage["b2b"])
        stage["b3"] += [ring_send(beats_slot(i, s), pair) for s in (down2, up2) for i in range(4)]

    def beats_pair():
        finish_all(stage["b2f"])
        stage["b3"] += [ring_send(beats_slot(i, (second + 2) % 4), pair) for i in range(4)]

    def beats_rest():
        values = normed[1][0]
        for d in range(3):
            for j in range(WB // 256):
                cols = slice(256 * j, 256 * j + 256)
                hidden[0:128, cols] = gelu(dot(values, others[0, :, :, d, :, cols].reshape(WB, 256))).astype(bf)
            for j in range(WB // 256):
                cols = slice(256 * j, 256 * j + 256)
                keep[1][:, cols] += dot(hidden[0:128, 0:WB], others[1, :, :, d, :, cols].reshape(WB, 256))

    opposite, sides = {}, {}

    def send_sides(k):
        finish_all(opposite[k])
        sside[k][0, 0:64] = part[k][0, 0:64].astype(bf)
        sside[k][0, 64:128] = (part[k][0, 64:128] + ropp[k][1].astype(f32)).astype(bf)
        sside[k][1, 0:64] = (part[k][1, 0:64] + ropp[k][0].astype(f32)).astype(bf)
        sside[k][1, 64:128] = part[k][1, 64:128].astype(bf)
        sides[k] = (send(sside[k].at[1], rside[k].at[0], r["sds"].at[k, 0], r["sdr"].at[k, 0], right),
                    send(sside[k].at[0], rside[k].at[1], r["sds"].at[k, 1], r["sdr"].at[k, 1], left))

    def pair_send(i, src, dst):
        return send(src, dst, r["xs"].at[i], r["xr"].at[i], pair)

    def share_rows(i, values, h, mine, joined):
        mine[...] = values.T.reshape(4, 4, 2, h, 128)
        joined[:, :, :, 0:128] = mine[:, :, c]
        return pair_send(i, mine.at[:, :, 1 - c], joined.at[:, :, :, pl.ds(128, 128)])

    shared, passed = {}, {}
    widths = [width for _, width, _ in TEACHERS]

    def own_rows(n):
        k = order[n]
        finish_all(loads[k])

        def put(cols, v):
            keep[k][:, cols] = v
        ffn(k, widths[n], 0, 1, put)

    def side_rows(n):
        k = order[n]

        def put(cols, v):
            part[k][:, :, cols] = v.reshape(2, 128, 256)
        ffn(k, widths[n], 1, 2, put)

    def pass_on(n):
        finish_all(gathers[order[n]])
        passed[n] = forward(order[n])

    def far_rows(n):
        k = order[n]
        finish_all(passed[n])

        def put(cols, v):
            sopp[k][:, :, cols] = v.astype(bf).reshape(2, 64, 256)
        ffn(k, widths[n], 3, 1, put)
        opposite[k] = (send(sopp[k].at[0], ropp[k].at[0], r["ops"].at[k, 0], r["opr"].at[k, 0], right),
                       send(sopp[k].at[1], ropp[k].at[1], r["ops"].at[k, 1], r["opr"].at[k, 1], left))

    own_rows(0)
    student_second()
    pass_on(0)
    own_rows(1)
    side_rows(0)
    own_rows(2)
    beats_first()
    pass_on(1)
    side_rows(1)
    relay_second("s2", student_slot)
    far_rows(0)
    beats_second()
    finish_all(hand)
    student = dot(place, r["incoming"][...].reshape(256, 512).astype(bf)).astype(bf)
    r["student"][...] = student
    shared["in"] = share_rows(0, student, 16, r["tin"], r["lin"])
    far_rows(1)
    student_pair()
    send_sides(order[0])
    stage["s3"][0].wait()
    student = r["student"][...]
    pre_act = dot(student, full[0][...].reshape(512, 1536))
    shifted = pre_act - 4.0
    decay = jnp.exp(-jnp.abs(shifted))
    soft = jnp.maximum(shifted, 0.0) + jnp.log1p(decay)
    activated = (soft - 0.08 * pre_act - 0.035).astype(bf)
    r["slope"][...] = jnp.where(shifted >= 0.0, 1.0, decay) / (1.0 + decay) - 0.08
    r["active"][...] = activated
    relay_second("b2", beats_slots)
    send_sides(order[1])
    stage["s3"][1].wait()
    features = (student.astype(f32) + dot(r["active"][...], full[1][...].reshape(1536, 512))).astype(bf)
    shared["feat"] = share_rows(1, features, 16, r["tfeat"], r["lfeat"])
    beats_share()
    stage["s3"][2].wait()
    for k, width, start in TEACHERS:
        r["predicted"][:, start:start + width] = dot(features, full[2][:, :, :, :, start:start + width].reshape(512, width))

    def error_of(n):
        k, width, start = TEACHERS[n]
        cols = slice(start, start + width)
        total = hid[k][...].astype(f32) + keep[k][...]
        if n < 2:
            finish_all(sides[k])
            total = total + rside[k][0].astype(f32) + rside[k][1].astype(f32)
        target = total.astype(bf).astype(f32)
        err = ((r["predicted"][:, cols] - target) * (2.0 / width) * mask).astype(bf)
        rerr[0:128, cols] = err
        cp = pair_send(3 + n, rerr.at[pl.ds(0, 128), pl.ds(start, width)], rerr.at[pl.ds(128, 128), pl.ds(start, width)])
        back = dot_t(err, full[2][:, :, :, :, cols].reshape(512, width))
        if n == 0:
            r["fgrad"][...] = back
        elif n == 1:
            r["fgrad"][...] += back
        else:
            back = r["fgrad"][...] + back
        return cp, back

    def block_rows(joined, a):
        tiles = [joined[jnp.where(swap, b, a), jnp.where(swap, a, b)] for b in range(4)]
        return jnp.concatenate(tiles, axis=0)

    def products(n, a, store):
        if n < 3:
            heads = block_rows(r["lfeat"], a)
            _, width, start = TEACHERS[n]
            store(GROUP_COLUMNS[n][0], dot(heads, rerr[:, start:start + width]).reshape(4, 16, width))
        elif n == 3:
            outs = dot(block_rows(r["lact"], a), rfg[...]).reshape(4, 48, 512)
            for m in range(3):
                store(3072 + 512 * m, outs[:, 16 * m:16 * m + 16])
        else:
            store(4608, dot(block_rows(r["lin"], a), rpre[...]).reshape(4, 16, 1536))

    phase1, phase2 = {}, {}

    def start_group(n):
        start, width = GROUP_COLUMNS[n]
        cols = pl.ds(start, width)
        copies = []
        for d in (2, 1, 3):
            a = (first + d) % 4

            def put(at, v):
                r["send1"][d - 1, :, :, at:at + v.shape[2]] = v.astype(bf)
            products(n, a, put)
            copies.append(send(r["send1"].at[d - 1, :, :, cols], r["recv1"].at[d - 1, :, :, cols],
                               r["s1s"].at[n, d - 1], r["s1r"].at[n, d - 1], at_first(a)))

        def put_own(at, v):
            r["own1"][:, :, at:at + v.shape[2]] = v
        products(n, first, put_own)
        phase1[n] = copies

    def next_group(n):
        start, width = GROUP_COLUMNS[n]
        cols = slice(start, start + width)
        ref_cols = pl.ds(start, width)
        finish_all(phase1[n])

        def total1(b):
            v = r["own1"][b, :, cols]
            for i in range(3):
                v = v + r["recv1"][i, b, :, cols].astype(f32)
            return v
        copies = []
        for d in (2, 1, 3):
            b = (second + d) % 4
            r["send2"][d - 1, :, cols] = total1(b).astype(bf)
            copies.append(send(r["send2"].at[d - 1, :, ref_cols], r["recv2"].at[d - 1, :, ref_cols],
                               r["s2s"].at[n, d - 1], r["s2r"].at[n, d - 1], at_second(b)))
        r["own2"][:, cols] = total1(second)
        phase2[n] = copies

    cp, _ = error_of(0)
    shared["act"] = share_rows(2, r["active"][...], 48, r["tact"], r["lact"])
    finish_all([cp, shared["feat"]])
    start_group(0)
    beats_pair()
    cp, _ = error_of(1)
    finish_all([shared["in"], shared["act"]])
    next_group(0)
    cp.wait()
    start_group(1)
    finish_all(stage["b3"])
    beats_rest()
    cp, back = error_of(2)
    feat_grad = back.astype(bf)
    rfg[0:128] = feat_grad
    late = [pair_send(6, rfg.at[pl.ds(0, 128)], rfg.at[pl.ds(128, 128)])]
    cp.wait()
    start_group(2)
    act_grad = dot_t(feat_grad, full[1][...].reshape(1536, 512))
    rpre[0:128] = (act_grad * r["slope"][...]).astype(bf)
    cp = pair_send(7, rpre.at[pl.ds(0, 128)], rpre.at[pl.ds(128, 128)])
    finish_all(late)
    start_group(3)
    next_group(1)
    cp.wait()
    start_group(4)

    summed = {}

    def send_sums(q):
        start, width = GROUP_COLUMNS[q]
        cols, ref_cols = slice(start, start + width), pl.ds(start, width)
        total = r["own2"][:, cols]
        for i in range(3):
            total = total + r["recv2"][i, :, cols].astype(f32)
        sums[y, :, cols] = total.astype(bf)
        mine = sums.at[y, :, ref_cols]
        summed[q] = [send(mine, mine, r["s3s"].at[q, d - 1], r["s3r"].at[q, d - 1], at_y(y + d)) for d in (2, 1, 3)]

    finish_all(phase2[0])
    send_sums(0)
    finish_all(phase2[1])
    send_sums(1)
    next_group(2)
    next_group(3)
    finish_all(phase2[2])
    send_sums(2)
    next_group(4)
    finish_all(phase2[3])
    send_sums(3)
    finish_all(phase2[4])
    send_sums(4)
    for q in range(5):
        finish_all(summed[q])


def sum_kernel(sums, grad_in, grad_out, grad_head):
    def sum_of(start, width):
        cols = slice(start, start + width)
        total = sums[0, :, cols].astype(jnp.float32)
        for t in range(1, 4):
            total = total + sums[t, :, cols].astype(jnp.float32)
        return total

    grad_head[:, WH + WB:] = sum_of(0, 1024)
    grad_head[:, 0:WH + WB] = sum_of(1024, 2048)
    for m in range(3):
        grad_out[16 * m:16 * m + 16] = sum_of(3072 + 512 * m, 512)
    grad_in[...] = sum_of(4608, 1536)


def body(
    hid_whisper, hid_beats, hid_wavlm,
    up_whisper, down_whisper, up_beats, down_beats, up_wavlm, down_wavlm,
    clip_len, send_counts, student_in, w_in, w_out, w_head,
):
    vm = pl.BlockSpec(memory_space=pltpu.VMEM)
    hbm = pl.BlockSpec(memory_space=pl.ANY)
    plan = scratch_plan()
    f32 = jnp.float32
    sums = pl.pallas_call(
        functools.partial(step_kernel, tuple(plan)),
        out_shape=jax.ShapeDtypeStruct((4, 16, SPAN), jnp.bfloat16),
        in_specs=[hbm] * 14 + [pl.BlockSpec(memory_space=pltpu.SMEM)],
        out_specs=vm,
        scratch_shapes=list(plan.values()),
        compiler_params=pltpu.CompilerParams(
            collective_id=0, has_side_effects=True, vmem_limit_bytes=62 * 1024 * 1024),
    )(
        hid_whisper, hid_beats, hid_wavlm,
        up_whisper, down_whisper, up_beats, down_beats, up_wavlm, down_wavlm,
        w_in, w_out, w_head, student_in, send_counts[0], clip_len,
    )
    return tuple(pl.pallas_call(
        sum_kernel,
        out_shape=[jax.ShapeDtypeStruct((16, 1536), f32), jax.ShapeDtypeStruct((48, 512), f32),
                   jax.ShapeDtypeStruct((16, 3072), f32)],
        in_specs=[vm],
        out_specs=[vm] * 3,
    )(sums))


def solution(mesh):
    in_specs = (
        P(("teacher", "dp"), None),
        P(("teacher", "dp"), None),
        P(("teacher", "dp"), None),
        P(None, "teacher"),
        P("teacher", None),
        P(None, "teacher"),
        P("teacher", None),
        P(None, "teacher"),
        P("teacher", None),
        P(("teacher", "dp")),
        P("teacher", None, None),
        P(("teacher", "dp"), None),
        P("dp", None),
        P("dp", None),
        P("dp", None),
    )
    out_specs = (P("dp", None), P("dp", None), P("dp", None))
    return jax.shard_map(body, mesh=mesh, in_specs=in_specs, out_specs=out_specs, check_vma=False)
```

```python
import functools

import jax
import jax.numpy as jnp
from jax import lax
from jax.experimental import pallas as pl
from jax.experimental.pallas import tpu as pltpu
from jax.sharding import PartitionSpec as P

WH = 1280
WB = 768
WL = 1024
EPS = 1e-05


def layer_norm(values):
    wide = values.astype(jnp.float32)
    center = wide - jnp.mean(wide, axis=-1, keepdims=True)
    spread = jnp.mean(center * center, axis=-1, keepdims=True)
    return center * lax.rsqrt(spread + EPS)


MESH_ID = pl.DeviceIdType.MESH
TEACHERS = ((2, WL, WH + WB), (0, WH, 0), (1, WB, WH))
SPAN = 6144
GROUP_COLUMNS = ((0, 1024), (1024, 1280), (2304, 768), (3072, 1536), (4608, 1536))


def gelu(values):
    return 0.5 * values * (1.0 + lax.erf(values * 0.7071067811865476))


def dot(a, b):
    return jnp.dot(a, b, preferred_element_type=jnp.float32)


def dot_t(a, b):
    return lax.dot_general(a, b, (((1,), (1,)), ((), ())), preferred_element_type=jnp.float32)


def scratch_plan():
    bf, f32 = jnp.bfloat16, jnp.float32
    vm, dma = pltpu.VMEM, pltpu.SemaphoreType.DMA
    plan = {}
    for k, w in enumerate((WH, WB, WL)):
        plan[f"hid{k}"] = vm((128, w), bf)
        plan[f"vup{k}"] = vm((w, w), bf)
        plan[f"vdown{k}"] = vm((w, w), bf)
        plan[f"keep{k}"] = vm((128, w), f32)
        plan[f"normed{k}"] = vm((1 if k == 1 else 4, 128, w), bf)
    for k, w in ((0, WH), (2, WL)):
        plan[f"part{k}"] = vm((2, 128, w), f32)
        plan[f"sopp{k}"] = vm((2, 64, w), bf)
        plan[f"ropp{k}"] = vm((2, 64, w), bf)
        plan[f"sside{k}"] = vm((2, 128, w), bf)
        plan[f"rside{k}"] = vm((2, 128, w), bf)
    for m, (h, w) in enumerate(((16, 1536), (48, 512), (16, 3072))):
        plan[f"full{m}"] = vm((4, 4, 2, h, w), bf)
    plan.update(
        hidden=vm((256, WH), bf),
        outgoing=vm((32, 8, 512), HAND), incoming=vm((32, 8, 512), HAND),
        student=vm((128, 512), bf), active=vm((128, 1536), bf),
        slope=vm((128, 1536), f32), predicted=vm((128, 3072), f32), fgrad=vm((128, 512), f32),
        tin=vm((4, 4, 2, 16, 128), bf), tact=vm((4, 4, 2, 48, 128), bf), tfeat=vm((4, 4, 2, 16, 128), bf),
        lin=vm((4, 4, 16, 256), bf), lact=vm((4, 4, 48, 256), bf), lfeat=vm((4, 4, 16, 256), bf),
        rpre=vm((256, 1536), bf), rfg=vm((256, 512), bf), rerr=vm((256, 3072), bf),
        own1=vm((4, 16, SPAN), f32), send1=vm((3, 4, 16, SPAN), bf), recv1=vm((3, 4, 16, SPAN), bf),
        own2=vm((16, SPAN), f32), send2=vm((3, 16, SPAN), bf), recv2=vm((3, 16, SPAN), bf),
        rows_in=vm((128, 512), bf), counts=vm((32, 32), jnp.int32),
        wsem=dma((6,)), isem=dma((8,)),
        ags=dma((3, 2)), agr=dma((3, 2)), fws=dma((3, 2)), fwr=dma((3, 2)),
        ops=dma((3, 2)), opr=dma((3, 2)), sds=dma((3, 2)), sdr=dma((3, 2)),
        piece=vm((2, 48, WB), bf), others=vm((2, 4, 4, 3, 48, WB), bf),
        psem=dma((2,)), pys=dma((3,)), pyr=dma((3,)), gs=dma((96,)), gr=dma((96,)),
        hos=dma((32,)), hor=dma((32,)),
        xs=dma((8,)), xr=dma((8,)),
        s1s=dma((5, 3)), s1r=dma((5, 3)), s2s=dma((5, 3)), s2r=dma((5, 3)), s3s=dma((5, 3)), s3r=dma((5, 3)),
    )
    return plan


HAND = jnp.bfloat16


def step_kernel(names, *refs):
    ups, downs = refs[3:9:2], refs[4:9:2]
    shards = refs[9:12]
    clip_ref, sums = refs[14:16]
    r = dict(zip(names, refs[16:]))
    per = lambda name: [r.get(f"{name}{k}") for k in range(3)]
    hid = per("hid")
    vup, vdown, normed, keep, part = per("vup"), per("vdown"), per("normed"), per("keep"), per("part")
    sopp, ropp, sside, rside, full = per("sopp"), per("ropp"), per("sside"), per("rside"), per("full")
    hidden, rerr, rfg, rpre = r["hidden"], r["rerr"], r["rfg"], r["rpre"]
    bf, f32 = jnp.bfloat16, jnp.float32

    order = [k for k, _, _ in TEACHERS]
    y = lax.axis_index("teacher")
    dp = lax.axis_index("dp")
    c = dp % 2
    z = (dp // 2) % 4
    x = dp // 8
    swap = c == 1
    first = jnp.where(swap, z, x)
    second = jnp.where(swap, x, z)
    at_y = lambda t: {"teacher": t % 4}
    right, left = at_y(y + 1), at_y(y + 3)
    pair = {"dp": (x * 4 + z) * 2 + (1 - c)}

    def at_first(a):
        return {"dp": jnp.where(swap, (x * 4 + a) * 2 + 1, (a * 4 + z) * 2)}

    def at_second(b):
        return {"dp": jnp.where(swap, (b * 4 + z) * 2 + 1, (x * 4 + b) * 2)}

    def send(src, dst, ssem, rsem, dev):
        cp = pltpu.make_async_remote_copy(
            src_ref=src, dst_ref=dst, send_sem=ssem, recv_sem=rsem,
            device_id=dev, device_id_type=MESH_ID)
        cp.start()
        return cp

    def finish_all(copies):
        for cp in copies:
            cp.wait()

    ready = {}
    for i, (name, src, dst) in enumerate((
        (order[0], refs[order[0]], hid[order[0]]),
        ("counts", refs[13], r["counts"]),
        ("rows", refs[12], r["rows_in"]),
        ("in", shards[0], full[0].at[x, z, c]),
        ("out", shards[1], full[1].at[x, z, c]),
        ("head", shards[2], full[2].at[x, z, c]),
        (order[1], refs[order[1]], hid[order[1]]),
        (order[2], refs[order[2]], hid[order[2]]),
    )):
        ready[name] = pltpu.make_async_copy(src, dst, r["isem"].at[i])
        ready[name].start()
    piece_rows = pl.ds(pl.multiple_of((x * 4 + z) * 48, 48), 48)
    pieces = [pltpu.make_async_copy(src.at[piece_rows], r["piece"].at[i], r["psem"].at[i])
              for i, src in enumerate((ups[1], downs[1]))]
    for cp in pieces:
        cp.start()
    loads = {}
    for n, (k, _, _) in enumerate(TEACHERS):
        loads[k] = (pltpu.make_async_copy(ups[k], vup[k], r["wsem"].at[2 * n]),
                    pltpu.make_async_copy(downs[k], vdown[k], r["wsem"].at[2 * n + 1]))
        for cp in loads[k]:
            cp.start()

    barrier = pltpu.get_barrier_semaphore()
    for d in range(1, 4):
        pl.semaphore_signal(barrier, inc=1, device_id=at_y(y + d), device_id_type=MESH_ID)
    for d in range(1, 32):
        pl.semaphore_signal(barrier, inc=1, device_id={"dp": (dp + d) % 32}, device_id_type=MESH_ID)
    ready[order[0]].wait()
    normed[order[0]][0] = layer_norm(hid[order[0]][...]).astype(bf)

    ready["counts"].wait()
    counts = r["counts"][...].astype(f32)
    iota = lambda shape, axis: lax.broadcasted_iota(jnp.int32, shape, axis)
    src_at, own_at = iota((32, 32), 0), iota((32, 32), 1)
    one = lambda hit: jnp.where(hit, 1.0, 0.0)
    exact = lambda v: v.astype(bf)
    before_src = dot(exact(one(own_at < src_at)), exact(counts))
    before_own = dot(exact(counts), exact(one(src_at < own_at)))
    my_col, my_row = one(own_at == dp), one(src_at == dp)
    row_at, slot_at = iota((256, 32), 0), iota((256, 32), 1) * 8
    spread = exact(one((row_at >= slot_at) & (row_at < slot_at + 8)))
    wide_col = lambda v: dot(spread, exact(jnp.broadcast_to(jnp.sum(v * my_col, axis=1, keepdims=True), (32, 128))))
    slot = (iota((256, 128), 0) & 7).astype(f32)
    hit = (iota((256, 128), 1).astype(f32) == wide_col(before_src) + slot) & (slot < wide_col(counts))
    ready["rows"].wait()
    leaving = dot(exact(one(hit)), r["rows_in"][...])
    r["outgoing"][...] = leaving.reshape(32, 8, 512).astype(HAND)
    r["incoming"][dp] = r["outgoing"][dp]
    slot_at2, col_at = iota((32, 256), 0) * 8, iota((32, 256), 1)
    spread2 = exact(one((col_at >= slot_at2) & (col_at < slot_at2 + 8)))
    wide_row = lambda v: dot(exact(jnp.broadcast_to(jnp.sum(v * my_row, axis=0, keepdims=True), (128, 32))), spread2)
    slot2 = (iota((128, 256), 1) & 7).astype(f32)
    hit2 = (iota((128, 256), 0).astype(f32) == wide_row(before_own) + slot2) & (slot2 < wide_row(counts))
    place = exact(one(hit2))
    mask = one(iota((128, 1), 0) < clip_ref[0])

    finish_all([ready["in"], ready["out"], ready["head"]])
    pl.semaphore_wait(barrier, 34)

    def gather_out(k):
        return (send(normed[k].at[0], normed[k].at[1], r["ags"].at[k, 0], r["agr"].at[k, 0], right),
                send(normed[k].at[0], normed[k].at[2], r["ags"].at[k, 1], r["agr"].at[k, 1], left))

    def forward(k):
        lo, hi = pl.ds(0, 64), pl.ds(64, 64)
        return (send(normed[k].at[1, lo], normed[k].at[3, lo], r["fws"].at[k, 0], r["fwr"].at[k, 0], right),
                send(normed[k].at[2, hi], normed[k].at[3, hi], r["fws"].at[k, 1], r["fwr"].at[k, 1], left))

    def ffn(k, width, at, count, store):
        rows = count * 128
        values = normed[k][at:at + count].reshape(rows, width)
        for j in range(width // 256):
            cols = slice(256 * j, 256 * j + 256)
            hidden[0:rows, cols] = gelu(dot(values, vup[k][:, cols])).astype(bf)
        for j in range(width // 256):
            cols = slice(256 * j, 256 * j + 256)
            store(cols, dot(hidden[0:rows, 0:width], vdown[k][:, cols]))

    counter = iter(range(96))
    others = r["others"]

    def ring_send(ref, dev):
        i = next(counter)
        return send(ref, ref, r["gs"].at[i], r["gr"].at[i], dev)

    def slot_of(f, s):
        return jnp.where(swap, s, f), jnp.where(swap, f, s)

    def student_slot(f, s):
        i, j = slot_of(f, s)
        return [full[m].at[i, j, c] for m in range(3)]

    def beats_slot(f, s):
        i, j = slot_of(f, s)
        return others.at[c, i, j]

    up2, down2 = (second + 1) % 4, (second + 3) % 4
    up2_dev, down2_dev = at_second(up2), at_second(down2)
    row_devs = [at_first((first + d) % 4) for d in (2, 1, 3)]

    gathers = {order[0]: gather_out(order[0])}
    stage = {}
    stage["s1"] = [ring_send(ref, dev) for dev in row_devs for ref in student_slot(first, second)]
    finish_all(pieces)
    stage["py"] = [send(r["piece"].at[c], others.at[c, x, z, 3 - o], r["pys"].at[o - 1], r["pyr"].at[o - 1], at_y(y + o))
                   for o in (2, 1, 3)]
    ready[order[1]].wait()
    normed[order[1]][0] = layer_norm(hid[order[1]][...]).astype(bf)
    gathers[order[1]] = gather_out(order[1])
    hand = []
    for d in range(1, 32):
        to = (dp + d) % 32
        hand.append(send(r["outgoing"].at[to], r["incoming"].at[dp], r["hos"].at[d], r["hor"].at[d], {"dp": to}))
    ready[order[2]].wait()
    normed[order[2]][0] = layer_norm(hid[order[2]][...]).astype(bf)

    def spread_second(name, slots):
        stage[name + "a"], stage[name + "b"] = [], []
        for part, ups_first in ((name + "a", ((0, 2), (1, 3))), (name + "b", ((2, 0), (3, 1)))):
            for i, j in ups_first:
                stage[part] += [ring_send(ref, up2_dev) for ref in slots(i, second)]
                stage[part] += [ring_send(ref, down2_dev) for ref in slots(j, second)]

    def relay_second(name, slots):
        finish_all(stage[name + "a"])
        stage[name + "f"] = [ring_send(ref, up2_dev) for i in (0, 1) for ref in slots(i, down2)]
        stage[name + "f"] += [ring_send(ref, down2_dev) for i in (2, 3) for ref in slots(i, up2)]

    def student_second():
        finish_all(stage["s1"])
        spread_second("s2", student_slot)

    def student_pair():
        finish_all(stage["s2b"] + stage["s2f"])
        stage["s3"] = [ring_send(full[m].at[:, :, c], pair) for m in range(3)]

    def beats_slots(f, s):
        return [beats_slot(f, s)]

    def beats_first():
        finish_all(stage["py"])
        stage["b1"] = [ring_send(beats_slot(first, second), dev) for dev in row_devs]

    def beats_second():
        finish_all(stage["b1"])
        spread_second("b2", beats_slots)
        stage["b3"] = [ring_send(beats_slot(i, second), pair) for i in range(4)]

    def beats_share():
        finish_all(stage["b2b"])
        stage["b3"] += [ring_send(beats_slot(i, s), pair) for s in (down2, up2) for i in range(4)]

    def beats_pair():
        finish_all(stage["b2f"])
        stage["b3"] += [ring_send(beats_slot(i, (second + 2) % 4), pair) for i in range(4)]

    def beats_rest():
        values = normed[1][0]
        for d in range(3):
            for j in range(WB // 256):
                cols = slice(256 * j, 256 * j + 256)
                hidden[0:128, cols] = gelu(dot(values, others[0, :, :, d, :, cols].reshape(WB, 256))).astype(bf)
            for j in range(WB // 256):
                cols = slice(256 * j, 256 * j + 256)
                keep[1][:, cols] += dot(hidden[0:128, 0:WB], others[1, :, :, d, :, cols].reshape(WB, 256))

    opposite, sides = {}, {}

    def send_sides(k):
        finish_all(opposite[k])
        sside[k][0, 0:64] = part[k][0, 0:64].astype(bf)
        sside[k][0, 64:128] = (part[k][0, 64:128] + ropp[k][1].astype(f32)).astype(bf)
        sside[k][1, 0:64] = (part[k][1, 0:64] + ropp[k][0].astype(f32)).astype(bf)
        sside[k][1, 64:128] = part[k][1, 64:128].astype(bf)
        sides[k] = (send(sside[k].at[1], rside[k].at[0], r["sds"].at[k, 0], r["sdr"].at[k, 0], right),
                    send(sside[k].at[0], rside[k].at[1], r["sds"].at[k, 1], r["sdr"].at[k, 1], left))

    def pair_send(i, src, dst):
        return send(src, dst, r["xs"].at[i], r["xr"].at[i], pair)

    def share_rows(i, values, h, mine, joined):
        mine[...] = values.T.reshape(4, 4, 2, h, 128)
        joined[:, :, :, 0:128] = mine[:, :, c]
        return pair_send(i, mine.at[:, :, 1 - c], joined.at[:, :, :, pl.ds(128, 128)])

    shared, passed = {}, {}
    widths = [width for _, width, _ in TEACHERS]

    def own_rows(n):
        k = order[n]
        finish_all(loads[k])

        def put(cols, v):
            keep[k][:, cols] = v
        ffn(k, widths[n], 0, 1, put)

    def side_rows(n):
        k = order[n]

        def put(cols, v):
            part[k][:, :, cols] = v.reshape(2, 128, 256)
        ffn(k, widths[n], 1, 2, put)

    def pass_on(n):
        finish_all(gathers[order[n]])
        passed[n] = forward(order[n])

    def far_rows(n):
        k = order[n]
        finish_all(passed[n])

        def put(cols, v):
            sopp[k][:, :, cols] = v.astype(bf).reshape(2, 64, 256)
        ffn(k, widths[n], 3, 1, put)
        opposite[k] = (send(sopp[k].at[0], ropp[k].at[0], r["ops"].at[k, 0], r["opr"].at[k, 0], right),
                       send(sopp[k].at[1], ropp[k].at[1], r["ops"].at[k, 1], r["opr"].at[k, 1], left))

    own_rows(0)
    student_second()
    pass_on(0)
    own_rows(1)
    side_rows(0)
    own_rows(2)
    beats_first()
    pass_on(1)
    side_rows(1)
    relay_second("s2", student_slot)
    far_rows(0)
    beats_second()
    finish_all(hand)
    student = dot(place, r["incoming"][...].reshape(256, 512).astype(bf)).astype(bf)
    r["student"][...] = student
    shared["in"] = share_rows(0, student, 16, r["tin"], r["lin"])
    far_rows(1)
    student_pair()
    send_sides(order[0])
    stage["s3"][0].wait()
    student = r["student"][...]
    pre_act = dot(student, full[0][...].reshape(512, 1536))
    shifted = pre_act - 4.0
    decay = jnp.exp(-jnp.abs(shifted))
    soft = jnp.maximum(shifted, 0.0) + jnp.log1p(decay)
    activated = (soft - 0.08 * pre_act - 0.035).astype(bf)
    r["slope"][...] = jnp.where(shifted >= 0.0, 1.0, decay) / (1.0 + decay) - 0.08
    r["active"][...] = activated
    relay_second("b2", beats_slots)
    send_sides(order[1])
    stage["s3"][1].wait()
    features = (student.astype(f32) + dot(r["active"][...], full[1][...].reshape(1536, 512))).astype(bf)
    shared["feat"] = share_rows(1, features, 16, r["tfeat"], r["lfeat"])
    beats_share()
    stage["s3"][2].wait()
    for k, width, start in TEACHERS:
        r["predicted"][:, start:start + width] = dot(features, full[2][:, :, :, :, start:start + width].reshape(512, width))

    def error_of(n):
        k, width, start = TEACHERS[n]
        cols = slice(start, start + width)
        total = hid[k][...].astype(f32) + keep[k][...]
        if n < 2:
            finish_all(sides[k])
            total = total + rside[k][0].astype(f32) + rside[k][1].astype(f32)
        target = total.astype(bf).astype(f32)
        err = ((r["predicted"][:, cols] - target) * (2.0 / width) * mask).astype(bf)
        rerr[0:128, cols] = err
        cp = pair_send(3 + n, rerr.at[pl.ds(0, 128), pl.ds(start, width)], rerr.at[pl.ds(128, 128), pl.ds(start, width)])
        back = dot_t(err, full[2][:, :, :, :, cols].reshape(512, width))
        if n == 0:
            r["fgrad"][...] = back
        elif n == 1:
            r["fgrad"][...] += back
        else:
            back = r["fgrad"][...] + back
        return cp, back

    def block_rows(joined, a):
        tiles = [joined[jnp.where(swap, b, a), jnp.where(swap, a, b)] for b in range(4)]
        return jnp.concatenate(tiles, axis=0)

    def products(n, a, store):
        if n < 3:
            heads = block_rows(r["lfeat"], a)
            _, width, start = TEACHERS[n]
            store(GROUP_COLUMNS[n][0], dot(heads, rerr[:, start:start + width]).reshape(4, 16, width))
        elif n == 3:
            outs = dot(block_rows(r["lact"], a), rfg[...]).reshape(4, 48, 512)
            for m in range(3):
                store(3072 + 512 * m, outs[:, 16 * m:16 * m + 16])
        else:
            store(4608, dot(block_rows(r["lin"], a), rpre[...]).reshape(4, 16, 1536))

    phase1, phase2 = {}, {}

    def start_group(n):
        start, width = GROUP_COLUMNS[n]
        cols = pl.ds(start, width)
        copies = []
        for d in (2, 1, 3):
            a = (first + d) % 4

            def put(at, v):
                r["send1"][d - 1, :, :, at:at + v.shape[2]] = v.astype(bf)
            products(n, a, put)
            copies.append(send(r["send1"].at[d - 1, :, :, cols], r["recv1"].at[d - 1, :, :, cols],
                               r["s1s"].at[n, d - 1], r["s1r"].at[n, d - 1], at_first(a)))

        def put_own(at, v):
            r["own1"][:, :, at:at + v.shape[2]] = v
        products(n, first, put_own)
        phase1[n] = copies

    def next_group(n):
        start, width = GROUP_COLUMNS[n]
        cols = slice(start, start + width)
        ref_cols = pl.ds(start, width)
        finish_all(phase1[n])

        def total1(b):
            v = r["own1"][b, :, cols]
            for i in range(3):
                v = v + r["recv1"][i, b, :, cols].astype(f32)
            return v
        copies = []
        for d in (2, 1, 3):
            b = (second + d) % 4
            r["send2"][d - 1, :, cols] = total1(b).astype(bf)
            copies.append(send(r["send2"].at[d - 1, :, ref_cols], r["recv2"].at[d - 1, :, ref_cols],
                               r["s2s"].at[n, d - 1], r["s2r"].at[n, d - 1], at_second(b)))
        r["own2"][:, cols] = total1(second)
        phase2[n] = copies

    summed = {}

    def send_sums(q):
        start, width = GROUP_COLUMNS[q]
        cols, ref_cols = slice(start, start + width), pl.ds(start, width)
        total = r["own2"][:, cols]
        for i in range(3):
            total = total + r["recv2"][i, :, cols].astype(f32)
        sums[y, :, cols] = total.astype(bf)
        mine = sums.at[y, :, ref_cols]
        summed[q] = [send(mine, mine, r["s3s"].at[q, d - 1], r["s3r"].at[q, d - 1], at_y(y + d)) for d in (2, 1, 3)]

    cp, _ = error_of(0)
    shared["act"] = share_rows(2, r["active"][...], 48, r["tact"], r["lact"])
    finish_all([cp, shared["feat"]])
    start_group(0)
    beats_pair()
    cp, _ = error_of(1)
    finish_all([shared["in"], shared["act"]])
    next_group(0)
    cp.wait()
    start_group(1)
    finish_all(stage["b3"])
    beats_rest()
    cp, back = error_of(2)
    feat_grad = back.astype(bf)
    rfg[0:128] = feat_grad
    late = [pair_send(6, rfg.at[pl.ds(0, 128)], rfg.at[pl.ds(128, 128)])]
    cp.wait()
    start_group(2)
    act_grad = dot_t(feat_grad, full[1][...].reshape(1536, 512))
    rpre[0:128] = (act_grad * r["slope"][...]).astype(bf)
    cp = pair_send(7, rpre.at[pl.ds(0, 128)], rpre.at[pl.ds(128, 128)])
    finish_all(phase2[0])
    send_sums(0)
    finish_all(late)
    start_group(3)
    next_group(1)
    cp.wait()
    start_group(4)
    next_group(2)

    finish_all(phase2[1])
    send_sums(1)
    next_group(3)
    finish_all(phase2[2])
    send_sums(2)
    next_group(4)
    finish_all(phase2[3])
    send_sums(3)
    finish_all(phase2[4])
    send_sums(4)
    for q in range(5):
        finish_all(summed[q])


def sum_kernel(sums, grad_in, grad_out, grad_head):
    def sum_of(start, width):
        cols = slice(start, start + width)
        total = sums[0, :, cols].astype(jnp.float32)
        for t in range(1, 4):
            total = total + sums[t, :, cols].astype(jnp.float32)
        return total

    grad_head[:, WH + WB:] = sum_of(0, 1024)
    grad_head[:, 0:WH + WB] = sum_of(1024, 2048)
    for m in range(3):
        grad_out[16 * m:16 * m + 16] = sum_of(3072 + 512 * m, 512)
    grad_in[...] = sum_of(4608, 1536)


def body(
    hid_whisper, hid_beats, hid_wavlm,
    up_whisper, down_whisper, up_beats, down_beats, up_wavlm, down_wavlm,
    clip_len, send_counts, student_in, w_in, w_out, w_head,
):
    vm = pl.BlockSpec(memory_space=pltpu.VMEM)
    hbm = pl.BlockSpec(memory_space=pl.ANY)
    plan = scratch_plan()
    f32 = jnp.float32
    sums = pl.pallas_call(
        functools.partial(step_kernel, tuple(plan)),
        out_shape=jax.ShapeDtypeStruct((4, 16, SPAN), jnp.bfloat16),
        in_specs=[hbm] * 14 + [pl.BlockSpec(memory_space=pltpu.SMEM)],
        out_specs=vm,
        scratch_shapes=list(plan.values()),
        compiler_params=pltpu.CompilerParams(
            collective_id=0, has_side_effects=True, vmem_limit_bytes=62 * 1024 * 1024),
    )(
        hid_whisper, hid_beats, hid_wavlm,
        up_whisper, down_whisper, up_beats, down_beats, up_wavlm, down_wavlm,
        w_in, w_out, w_head, student_in, send_counts[0], clip_len,
    )
    return tuple(pl.pallas_call(
        sum_kernel,
        out_shape=[jax.ShapeDtypeStruct((16, 1536), f32), jax.ShapeDtypeStruct((48, 512), f32),
                   jax.ShapeDtypeStruct((16, 3072), f32)],
        in_specs=[vm],
        out_specs=[vm] * 3,
    )(sums))


def solution(mesh):
    in_specs = (
        P(("teacher", "dp"), None),
        P(("teacher", "dp"), None),
        P(("teacher", "dp"), None),
        P(None, "teacher"),
        P("teacher", None),
        P(None, "teacher"),
        P("teacher", None),
        P(None, "teacher"),
        P("teacher", None),
        P(("teacher", "dp")),
        P("teacher", None, None),
        P(("teacher", "dp"), None),
        P("dp", None),
        P("dp", None),
        P("dp", None),
    )
    out_specs = (P("dp", None), P("dp", None), P("dp", None))
    return jax.shard_map(body, mesh=mesh, in_specs=in_specs, out_specs=out_specs, check_vma=False)
```
